32 devices in a mesh: dp: 8 (over y, x, core), tensor: 4 (over z).
Axes of the slice: x: 2, y: 2, z: 4, core: 2. Of those that a mesh axis runs over, the one named last changes fastest.
Arguments:
- hidden_in: bfloat16 [32, 512, 768], P('dp'), may hold values from -6 to 6
- out_grad: bfloat16 [32, 512, 768], P('dp'), may hold values from -3 to 3
- segment_ids: int32 [32, 512], P('dp'), may hold values from 0 to 7, never falling along the last dimension, each value on 1 to 256 neighbouring positions
- step_count: int32 [1], replicated, may hold values from 1 to 199999
- qkv_state: float32 [3, 768, 3, 768], P(None, 'dp', None, 'tensor'), as said below
- qv_bias_state: float32 [3, 2, 12, 64], P(None, None, 'tensor', 'dp'), as said below
- out_state: float32 [3, 768, 768], P(None, 'tensor', 'dp'), as said below
- up_state: float32 [3, 768, 3072], P(None, 'dp', 'tensor'), as said below
- up_bias_state: float32 [3, 24, 128], P(None, 'tensor', 'dp'), as said below
- down_state: float32 [3, 3072, 768], P(None, 'tensor', 'dp'), as said below
- vector_state: float32 [3, 6, 768], P(None, None, 'dp'), as said below
Outputs:
- hidden_out: bfloat16 [32, 512, 768], P('dp')
- grad_in: bfloat16 [32, 512, 768], P('dp')
- grad_qkv: float32 [768, 3, 768], P('dp', None, 'tensor')
- grad_qv_bias: float32 [2, 12, 64], P(None, 'tensor', 'dp')
- grad_out: float32 [768, 768], P('tensor', 'dp')
- grad_up: float32 [768, 3072], P('dp', 'tensor')
- grad_up_bias: float32 [24, 128], P('tensor', 'dp')
- grad_down: float32 [3072, 768], P('tensor', 'dp')
- grad_vectors: float32 [6, 768], P(None, 'dp')
- new_qkv_state: float32 [2, 768, 3, 768], P(None, 'dp', None, 'tensor')
- new_qv_bias_state: float32 [2, 2, 12, 64], P(None, None, 'tensor', 'dp')
- new_out_state: float32 [2, 768, 768], P(None, 'tensor', 'dp')
- new_up_state: float32 [2, 768, 3072], P(None, 'dp', 'tensor')
- new_up_bias_state: float32 [2, 24, 128], P(None, 'tensor', 'dp')
- new_down_state: float32 [2, 3072, 768], P(None, 'tensor', 'dp')
- new_vector_state: float32 [2, 6, 768], P(None, None, 'dp')
- plan: float32 [3], replicated
The draws below stay inside these ranges and needn't reach their ends.
Inputs may be any that keep to these rules, and one draw needn't show every extreme that they name: `segment_ids`: within each packed row the fragment numbers never fall; a token attends exactly to the tokens of its own row with the same number. `qkv_state`: index 2 (second moments) is positive. `qv_bias_state`: index 2 (second moments) is positive. `out_state`: index 2 (second moments) is positive. `up_state`: index 2 (second moments) is positive. `up_bias_state`: index 2 (second moments) is positive. `down_state`: index 2 (second moments) is positive. `vector_state`: index 2 (second moments) is positive.
All inputs are finite; a program needn't handle non-finite values.
Results may differ from the reference program's by a relative error of at most 0.023.
The reference program's roundings to bfloat16 on the way count: a program that leaves them out, or rounds other values in their place, can miss the bound.
Values may be sent and summed in bfloat16 or wider, within the bound.
No kernel may reach another device: no remote copies, remote signals or barrier semaphores. Data moves between devices by JAX's collectives and lax.ppermute only.
A program may use at most 192 MiB of HBM per device.

```python
import math
import jax
import jax.numpy as jnp
import numpy as np
from jax import lax

D = 768
H = 12
HD = 64
FF = 3072
SEQ = 512
SEQS = 32
N_TENSOR = 4


def clipped_normal(key, shape):
    return jnp.clip(jax.random.normal(key, shape, jnp.float32), -4.0, 4.0)


def with_moments(key, weights):
    typical = 0.25 * math.sqrt(SEQS * SEQ)
    key_one, key_two = jax.random.split(jax.random.fold_in(key, 7))
    moment_one = 0.3 * typical * clipped_normal(key_one, weights.shape)
    moment_two = 0.001 * typical * typical * jnp.exp(jax.random.uniform(key_two, weights.shape, jnp.float32, math.log(0.5), math.log(2.0)))
    return jnp.stack([weights, moment_one, moment_two])


def draw_qkv_state(key, part):
    weights = 1.5 / math.sqrt(D) * clipped_normal(jax.random.fold_in(key, 1), (D, 3, H * HD))
    return with_moments(key, weights)


def draw_qv_bias_state(key, part):
    weights = 0.2 * clipped_normal(jax.random.fold_in(key, 1), (2, H, HD))
    return with_moments(key, weights)


def draw_out_state(key, part):
    weights = 4.0 / math.sqrt(H * HD) * clipped_normal(jax.random.fold_in(key, 1), (H * HD, D))
    return with_moments(key, weights)


def draw_up_state(key, part):
    weights = 1.0 / math.sqrt(D) * clipped_normal(jax.random.fold_in(key, 1), (D, FF))
    return with_moments(key, weights)


def draw_up_bias_state(key, part):
    weights = 0.2 * clipped_normal(jax.random.fold_in(key, 1), (FF // 128, 128))
    return with_moments(key, weights)


def draw_down_state(key, part):
    weights = 1.7 / math.sqrt(FF) * clipped_normal(jax.random.fold_in(key, 1), (FF, D))
    return with_moments(key, weights)


def draw_vector_state(key, part):
    centers = jnp.array([1.0, 0.0, 1.0, 0.0, 0.0, 0.0], jnp.float32)[:, None]
    spreads = jnp.array([0.15, 0.2, 0.15, 0.2, 0.2, 0.2], jnp.float32)[:, None]
    weights = centers + spreads * clipped_normal(jax.random.fold_in(key, 1), (6, D))
    return with_moments(key, weights)


def spiked(result, rng, source, target, blocks, factor):
    def block_of(axis_at):
        return (jnp.arange(result.shape[axis_at]) // (result.shape[axis_at] // blocks)).reshape((-1,) + (1,) * (result.ndim - 1 - axis_at))

    first = jax.random.permutation(rng, blocks)[block_of(target)]
    other_side = (block_of(target) + blocks // 2) % blocks
    return jnp.where((block_of(source) == first) | (block_of(source) == other_side), factor * result, result)


def levels(key, dims, pieces, least, high):
    level, own = 1.0, jax.random.fold_in(key, 6)
    for position, blocks in pieces:
        heights = jnp.exp(jax.random.uniform(jax.random.fold_in(own, position), (blocks,), jnp.float32, least / len(pieces), high / len(pieces)))
        level = level * jnp.repeat(heights, dims[position] // blocks).reshape([-1 if axis == position else 1 for axis in range(len(dims))])
    return level


def profile(amount, total, bound, skew):
    loads = [(1 << 20) // math.isqrt(standing ** skew) + 1 for standing in range(2, amount + 1)]
    surplus, counts = total - bound - (amount - 1), [1] * (amount - 1)
    while surplus > 0:
        candidates = [i for i in range(amount - 1) if counts[i] < bound]
        pool, budget = sum([loads[i] for i in candidates]), surplus
        for i in candidates:
            extra = min(bound - counts[i], max(1, budget * loads[i] // pool), surplus)
            counts[i] = counts[i] + extra
            surplus = surplus - extra
    return np.array([bound] + counts)


def uneven(own_key, count, total, limit, lean):
    if count == 2:
        one = jax.random.randint(own_key, (), max(1, total - limit), min(limit, total - 1) + 1)
        return jnp.stack([one, total - one])
    sizes = jnp.asarray(profile(count, total, limit, lean), jnp.int32)
    couples = (count - 1) // 2
    giver, taker = sizes[1:1 + 2 * couples:2], sizes[2:2 + 2 * couples:2]
    room = jnp.minimum(giver - 1, limit - taker)
    shifted = jax.random.randint(jax.random.fold_in(own_key, 1), (couples,), 0, 1 << 20) % (room + 1)
    sizes = sizes.at[1:1 + 2 * couples:2].set(giver - shifted).at[2:2 + 2 * couples:2].set(taker + shifted)
    return sizes[jax.random.permutation(jax.random.fold_in(own_key, 2), count)]


def noise(stream_key, dims, scale, reach, cuts=(), kind=jnp.bfloat16):
    result = jax.random.normal(stream_key, dims, jnp.float32) * scale
    if len(cuts) > 0:
        result = levels(stream_key, dims, cuts, -0.22, 0.18) * result
    return jnp.clip(result, min=-reach, max=reach).astype(kind)


def noise_with(own_key, shape, deviation, reach, pieces, heavy, kind=jnp.bfloat16):
    result = deviation * jax.random.normal(own_key, shape, jnp.float32)
    if pieces:
        result = result * levels(own_key, shape, pieces, -0.22, 0.18)
    return jnp.clip(spiked(result, jax.random.fold_in(own_key, 3), *heavy), -reach, reach).astype(kind)


def setup_inputs(seed: int = 0) -> dict:
    splits = jax.random.split(jax.random.key(seed), 12)
    return {
        "hidden_in": noise(splits[0], (SEQS, SEQ, D), 1.0, 6.0, ((0, 8),)),
        "out_grad": noise_with(splits[1], (SEQS, SEQ, D), 0.5, 3.0, ((0, 8),), (0, 2, 8, 2.0)),
        "segment_ids": jax.vmap(lambda own: jnp.searchsorted(jnp.cumsum(uneven(own, 8, SEQ, SEQ // 2, 2)), jnp.arange(SEQ), side="right"))(jax.random.split(splits[2], SEQS)).reshape((SEQS, SEQ)).astype(jnp.int32),
        "step_count": jax.random.randint(splits[3], (1,), 1, 200000).astype(jnp.int32),
        "qkv_state": draw_qkv_state(jax.random.fold_in(splits[11], 71), 0),
        "qv_bias_state": draw_qv_bias_state(jax.random.fold_in(splits[11], 71), 0),
        "out_state": draw_out_state(jax.random.fold_in(splits[11], 71), 0),
        "up_state": draw_up_state(jax.random.fold_in(splits[11], 71), 0),
        "up_bias_state": draw_up_bias_state(jax.random.fold_in(splits[11], 71), 0),
        "down_state": draw_down_state(jax.random.fold_in(splits[11], 71), 0),
        "vector_state": draw_vector_state(jax.random.fold_in(splits[11], 71), 0),
    }


@jax.custom_vjp
def low(v):
    return lax.optimization_barrier(v.astype(jnp.bfloat16)).astype(jnp.float32)

@jax.custom_vjp
def low_back(v):
    return v

def low_keep(v):
    return (low(v), None)

def low_pass(kept, grad):
    return (grad,)

def back_keep(v):
    return (v, None)

def back_low(kept, grad):
    return (low(grad),)
low.defvjp(low_keep, low_pass)
low_back.defvjp(back_keep, back_low)
precise = lax.Precision.HIGHEST
norm_eps = 1e-05
beta_first = 0.9
beta_second = 0.999
warm_steps = 10000.0
total_steps = 200000.0

def layer_norm(value, gain, shift):
    center = value - lax.optimization_barrier(jnp.mean(value, axis=-1, keepdims=True))
    spread = lax.optimization_barrier(jnp.mean(center * center, axis=-1, keepdims=True))
    return center * lax.rsqrt(spread + norm_eps) * gain + shift

def gelu_exact(value):
    return 0.5 * value * (1.0 + lax.erf(value * 0.7071067811865476))

def attend(query, key_rows, value_rows, segment):
    raw = jnp.einsum('qhd,khd->hqk', query, key_rows, precision=precise)
    scores = low_back(raw * HD ** (-0.5))
    same = segment[:, None] == segment[None, :]
    scores = jnp.where(same[None], scores, -1e+30)
    top = lax.optimization_barrier(jnp.max(scores, axis=-1, keepdims=True))
    weights = jnp.exp(scores - top)
    probs = weights / lax.optimization_barrier(jnp.sum(weights, axis=-1, keepdims=True))
    return jnp.einsum('hqk,khd->qhd', low(probs), value_rows, precision=precise)

def block_forward(params, rows, segments):
    w_qkv, b_qv, w_out, w_up, b_up, w_down, vectors = params
    count, length = segments.shape
    width = H * HD
    groups = N_TENSOR
    plain = rows.reshape(count * length, D)
    flat = low_back(plain)
    proj = jnp.einsum('td,dcf->tcf', flat, w_qkv, precision=precise)
    bias = jnp.stack([b_qv[0].reshape(width), jnp.zeros((width,), b_qv.dtype), b_qv[1].reshape(width)])
    proj = low_back(low(proj + bias[None]))
    heads = proj.reshape(count, length, 3, H, HD)
    context = jax.vmap(attend)(heads[:, :, 0], heads[:, :, 1], heads[:, :, 2], segments)
    context = low_back(low(context.reshape(count * length, width)))
    parts = jnp.einsum('tgf,gfd->gtd', context.reshape(count * length, groups, width // groups), w_out.reshape(groups, width // groups, D), precision=precise)
    attn = low_back(lax.optimization_barrier(jnp.sum(low(parts), axis=0)))
    first = layer_norm(plain + attn + vectors[4], vectors[0], vectors[1])
    first_in = low_back(low(first))
    up = low_back(jnp.dot(first_in, w_up, precision=precise) + b_up.reshape(FF))
    act = low(gelu_exact(up))
    parts_ffn = jnp.einsum('tgf,gfd->gtd', act.reshape(count * length, groups, FF // groups), w_down.reshape(groups, FF // groups, D), precision=precise)
    ffn = low_back(lax.optimization_barrier(jnp.sum(low(parts_ffn), axis=0)))
    out = layer_norm(first + ffn + vectors[5], vectors[2], vectors[3])
    return out.reshape(count, length, D)

def layer_forward(rows_all, segments_all, params):
    lowered = tuple((low(p) for p in params))
    total = segments_all.shape[0]
    per_block = math.gcd(total, max(1, 4096 // SEQ))
    blocks = total // per_block
    step_fn = jax.checkpoint(block_forward)

    def scan_body(carry, pair):
        return (carry, step_fn(lowered, pair[0], pair[1]))
    _, outs = lax.scan(scan_body, jnp.zeros((), jnp.float32), (rows_all.reshape(blocks, per_block, SEQ, D), segments_all.reshape(blocks, per_block, SEQ)))
    return outs.reshape(total, SEQ, D)

def moment_update(state, grad):
    moment_one = beta_first * state[1] + (1.0 - beta_first) * grad
    moment_two = beta_second * state[2] + (1.0 - beta_second) * grad * grad
    return jnp.stack([moment_one, moment_two])

def reference(hidden_in, out_grad, segment_ids, step_count, qkv_state, qv_bias_state, out_state, up_state, up_bias_state, down_state, vector_state):
    states = (qkv_state, qv_bias_state, out_state, up_state, up_bias_state, down_state, vector_state)
    params = tuple((s[0] for s in states))

    def wrapped(rows, *weights):
        return layer_forward(rows, segment_ids, weights)
    out, pull = jax.vjp(wrapped, hidden_in.astype(jnp.float32), *params)
    grads = pull(out_grad.astype(jnp.float32))
    steps_f = step_count[0].astype(jnp.float32)
    factor = jnp.minimum(steps_f / warm_steps, (total_steps - steps_f) / (total_steps - warm_steps))
    fix_first = 1.0 - jnp.exp(steps_f * math.log(beta_first))
    fix_second = 1.0 - jnp.exp(steps_f * math.log(beta_second))
    news = tuple((moment_update(s, g) for s, g in zip(states, grads[1:])))
    plan = jnp.stack([factor, fix_first, fix_second]).astype(jnp.float32)
    return (out.astype(jnp.bfloat16), grads[0].astype(jnp.bfloat16), grads[1], grads[2], grads[3], grads[4], grads[5], grads[6], grads[7], news[0], news[1], news[2], news[3], news[4], news[5], news[6], plan)
```

```python
import functools
import math

import jax
import jax.numpy as jnp
from jax import lax
from jax.experimental import pallas as pl
from jax.experimental.pallas import tpu as pltpu
from jax.sharding import PartitionSpec as P

HD = 64
LANES = 128
VMEM_LIMIT = 60 * 1024 * 1024

norm_eps = 1e-05
beta_first = 0.9
beta_second = 0.999
warm_steps = 10000.0
total_steps = 200000.0

bf = jnp.bfloat16
fl = jnp.float32

SLABS = 8
DEPTH = 96


def nt(left, right):
    return lax.dot_general(left, right, (((1,), (1,)), ((), ())), preferred_element_type=fl)


def nn(left, right):
    return lax.dot_general(left, right, (((1,), (0,)), ((), ())), preferred_element_type=fl)


def tn(left, right):
    return lax.dot_general(left, right, (((0,), (0,)), ((), ())), preferred_element_type=fl)


def low_lanes(shape):
    return lax.broadcasted_iota(jnp.int32, shape, 1) < HD


def assemble(where_ref, pieces, plan, weight_ref):
    for ref, (r, shifts) in zip(pieces, plan):
        slab = jnp.bitwise_xor(where_ref[0], r)
        for k, s in enumerate(shifts):
            group = jnp.bitwise_and(where_ref[1] + 4 - s, 3)
            weight_ref[group, slab] = ref[k]


def scatter_slabs(where_ref, group, value, out_ref):
    shift = jnp.bitwise_and(group + 4 - where_ref[1], 3)
    for j in range(SLABS):
        out_ref[jnp.bitwise_xor(where_ref[0], j), shift] = value[DEPTH * j : DEPTH * (j + 1)]


def matrix(ref, group):
    return ref[group].reshape(SLABS * DEPTH, ref.shape[-1])


def attn_fwd_kernel(plan, where_ref, x_ref, seg_row_ref, seg_col_ref, bias_ref, *refs):
    pieces, (proj_ref, ctx_ref, lse_ref, weight_ref) = refs[: len(plan)], refs[len(plan) :]
    assemble(where_ref, pieces, plan, weight_ref)
    scale = HD ** (-0.5)
    length = x_ref.shape[0]

    def group_step(g, carry):
        x = x_ref[...]
        proj = (nn(x, matrix(weight_ref, g)) + bias_ref[g]).astype(bf)
        proj_ref[g] = proj
        same = seg_col_ref[...] == seg_row_ref[...]
        low = low_lanes((length, LANES))
        none = jnp.zeros((length, LANES), bf)
        parts = [proj[:, LANES * k : LANES * (k + 1)] for k in range(6)]
        outs = []
        for head in range(3):
            query = parts[0] if head < 2 else parts[3]
            keys = parts[1] if head < 2 else parts[5]
            value = parts[2] if head < 2 else parts[3]
            query = jnp.where(low, none, query) if head == 1 else jnp.where(low, query, none)
            scores = jnp.where(same, nt(keys, query) * scale, -1e30)
            top = jnp.max(scores, axis=0, keepdims=True)
            expd = jnp.exp(scores - top)
            denom = jnp.sum(expd, axis=0, keepdims=True)
            lse_ref[g, head] = top + jnp.log(denom)
            probs = (expd / denom).astype(bf)
            outs.append(tn(probs, value).astype(bf))
        ctx_ref[g] = jnp.concatenate(
            [jnp.where(low, outs[0], outs[1]), jnp.where(low, none, outs[2])], axis=1
        )
        return carry

    lax.fori_loop(0, 4, group_step, 0)


def up_kernel(plan, where_ref, x_ref, ctx_ref, attn_weight_ref, vec_ref, b_up_ref, *refs):
    pieces, (xhat_ref, rstd_ref, first_ref, act_ref, slope_ref, weight_ref) = refs[: len(plan)], refs[len(plan) :]
    assemble(where_ref, pieces, plan, weight_ref)
    total = x_ref[...].astype(fl) + vec_ref[4:5]
    attn = None
    for g in range(4):
        w = attn_weight_ref[g][:, :, 512:768].reshape(SLABS * DEPTH, 256)
        part = nt(ctx_ref[g], w)
        attn = part if attn is None else attn + part
    total = total + attn
    center = total - jnp.mean(total, axis=-1, keepdims=True)
    rstd = lax.rsqrt(jnp.mean(center * center, axis=-1, keepdims=True) + norm_eps)
    xhat = center * rstd
    first = xhat * vec_ref[0:1] + vec_ref[1:2]
    xhat_ref[...] = xhat
    rstd_ref[...] = jnp.broadcast_to(rstd, rstd_ref.shape)
    first_ref[...] = first.astype(bf)

    def step(g, carry):
        up = nn(first_ref[...], matrix(weight_ref, g)) + b_up_ref[g]
        half = 0.5 * (1.0 + lax.erf(up * 0.7071067811865476))
        act_ref[g] = (up * half).astype(bf)
        slope_ref[g] = half + up * (jnp.exp(-0.5 * up * up) * 0.3989422804014327)
        return carry

    lax.fori_loop(0, 4, step, 0)


def down_kernel(plan, where_ref, xhat_ref, act_ref, slope_ref, dy_ref, vec_ref, *refs):
    pieces = refs[: len(plan)]
    out_ref, dr2_ref, dup_ref, grad_ref, small_ref, b_up_ref, weight_ref = refs[len(plan) :]
    assemble(where_ref, pieces, plan, weight_ref)
    ffn = None
    for g in range(4):
        part = nt(act_ref[g], matrix(weight_ref, g))
        ffn = part if ffn is None else ffn + part
    first = xhat_ref[...] * vec_ref[0:1] + vec_ref[1:2]
    total = first + ffn + vec_ref[5:6]
    center = total - jnp.mean(total, axis=-1, keepdims=True)
    rstd = lax.rsqrt(jnp.mean(center * center, axis=-1, keepdims=True) + norm_eps)
    xhat = center * rstd
    out_ref[...] = (xhat * vec_ref[2:3] + vec_ref[3:4]).astype(bf)
    dy = dy_ref[...].astype(fl)
    small_ref[0:1] = jnp.sum(dy * xhat, axis=0, keepdims=True)
    small_ref[1:2] = jnp.sum(dy, axis=0, keepdims=True)
    dxhat = dy * vec_ref[2:3]
    dr2 = rstd * (
        dxhat
        - jnp.mean(dxhat, axis=-1, keepdims=True)
        - xhat * jnp.mean(dxhat * xhat, axis=-1, keepdims=True)
    )
    dr2_ref[...] = dr2
    small_ref[2:3] = jnp.sum(dr2, axis=0, keepdims=True)

    def step(g, carry):
        dffn = dr2_ref[...].astype(bf)
        scatter_slabs(where_ref, g, tn(dffn, act_ref[g]).astype(bf), grad_ref)
        dup = (nn(dffn, matrix(weight_ref, g)) * slope_ref[g]).astype(bf)
        dup_ref[g] = dup
        b_up_ref[g] = jnp.sum(dup.astype(fl), axis=0, keepdims=True)
        return carry

    lax.fori_loop(0, 4, step, 0)


def up_bwd_kernel(where_ref, dr2_ref, dup_ref, xhat_ref, rstd_ref, first_ref, vec_ref, weight_ref, attn_weight_ref,
                  dr1_ref, dctx_ref, grad_ref, small_ref):
    feed = None
    for g in range(4):
        part = nt(dup_ref[g], matrix(weight_ref, g))
        feed = part if feed is None else feed + part
    dfirst = dr2_ref[...] + feed.astype(bf).astype(fl)
    xhat = xhat_ref[...]
    small_ref[0:1] = jnp.sum(dfirst * xhat, axis=0, keepdims=True)
    small_ref[1:2] = jnp.sum(dfirst, axis=0, keepdims=True)
    dxhat = dfirst * vec_ref[0:1]
    dr1 = rstd_ref[:, 0:1] * (
        dxhat
        - jnp.mean(dxhat, axis=-1, keepdims=True)
        - xhat * jnp.mean(dxhat * xhat, axis=-1, keepdims=True)
    )
    dr1_ref[...] = dr1
    small_ref[2:3] = jnp.sum(dr1, axis=0, keepdims=True)
    dattn = dr1.astype(bf)
    for g in range(4):
        w = attn_weight_ref[g][:, :, 512:768].reshape(SLABS * DEPTH, 256)
        dctx_ref[g] = nn(dattn, w).astype(bf)

    def step(g, carry):
        scatter_slabs(where_ref, g, tn(first_ref[...], dup_ref[g]).astype(bf), grad_ref)
        return carry

    lax.fori_loop(0, 4, step, 0)


def attn_bwd_kernel(where_ref, x_ref, seg_row_ref, seg_col_ref, proj_ref, ctx_ref, lse_ref, dr1_ref, dctx_ref, weight_ref,
                    grad_in_ref, grad_ref, bias_ref, dproj_ref, back_ref):
    scale = HD ** (-0.5)
    length = x_ref.shape[0]
    back_ref[...] = jnp.zeros_like(back_ref)

    def step(g, carry):
        same = seg_col_ref[...] == seg_row_ref[...]
        low = low_lanes((length, LANES))
        none = jnp.zeros((length, LANES), bf)
        parts = [proj_ref[g, :, LANES * k : LANES * (k + 1)] for k in range(6)]
        dctx = [dctx_ref[g, :, :LANES], dctx_ref[g, :, LANES:]]
        dq, dk, dv = [], [], []
        for head in range(3):
            query = parts[0] if head < 2 else parts[3]
            keys = parts[1] if head < 2 else parts[5]
            value = parts[2] if head < 2 else parts[3]
            dout = dctx[0] if head < 2 else dctx[1]
            query_in = jnp.where(low, none, query) if head == 1 else jnp.where(low, query, none)
            dout_in = jnp.where(low, dout, none) if head == 0 else jnp.where(low, none, dout)
            scores = jnp.where(same, nt(keys, query_in) * scale, -1e30)
            probs = jnp.exp(scores - lse_ref[g, head])
            dprobs = nt(value, dout_in)
            dv.append(nn(probs.astype(bf), dout))
            row_dot = jnp.sum(probs * dprobs, axis=0, keepdims=True)
            dscores = (probs * (dprobs - row_dot)).astype(bf)
            dq.append(tn(dscores, keys) * scale)
            dk.append(nn(dscores, query) * scale)
        dproj = jnp.concatenate(
            [
                jnp.where(low, dq[0], dq[1]).astype(bf),
                jnp.where(low, dk[0], dk[1]).astype(bf),
                jnp.where(low, dv[0], dv[1]).astype(bf),
                jnp.where(low, dq[2], dv[2]).astype(bf),
                none,
                jnp.where(low, dk[2].astype(bf), none),
            ],
            axis=1,
        )
        dproj_ref[g] = dproj
        bias_ref[g] = jnp.sum(dproj.astype(fl), axis=0, keepdims=True)
        back_ref[...] += nt(dproj, matrix(weight_ref, g))
        return carry

    lax.fori_loop(0, 4, step, 0)
    dr1 = dr1_ref[...]
    grad_in_ref[...] = (dr1 + back_ref[...].astype(bf).astype(fl)).astype(bf)

    def grads(g, carry):
        x = x_ref[...]
        main = tn(x, dproj_ref[g])
        side = tn(dr1_ref[...].astype(bf), ctx_ref[g])
        whole = jnp.concatenate([main[:, :512], main[:, 512:] + side], axis=1).astype(bf)
        scatter_slabs(where_ref, g, whole, grad_ref)
        return carry

    lax.fori_loop(0, 4, grads, 0)


def place_kernel(where_ref, *refs):
    out_ref = refs[-1]
    for s, ref in enumerate(refs[:-1]):
        out_ref[jnp.bitwise_and(where_ref[1] + 4 - s, 3)] = ref[...]


smem = pl.BlockSpec(memory_space=pltpu.SMEM)
vmem = pl.BlockSpec(memory_space=pltpu.VMEM)


def call(kernel, name, outs, where, *args, scratch=(), flops=0):
    size = sum(math.prod(a.shape) * a.dtype.itemsize for a in args)
    size += sum(math.prod(s) * jnp.dtype(d).itemsize for s, d in outs)
    return pl.pallas_call(
        kernel,
        name=name,
        out_shape=[jax.ShapeDtypeStruct(s, d) for s, d in outs],
        in_specs=[smem] + [vmem] * len(args),
        out_specs=[vmem] * len(outs),
        scratch_shapes=list(scratch),
        compiler_params=pltpu.CompilerParams(vmem_limit_bytes=VMEM_LIMIT),
        cost_estimate=pl.CostEstimate(flops=flops, bytes_accessed=size, transcendentals=0),
    )(where, *args)


def flip(value, bit):
    n = lax.axis_size("dp")
    return lax.ppermute(value, "dp", [(k, k ^ bit) for k in range(n)])


def shift(value, s):
    return lax.ppermute(value, "tensor", [(k, (k + s) % 4) for k in range(4)])


def gather_slabs(shard):
    own = jnp.stack([shard] + [shift(shard, s) for s in (1, 2, 3)])
    over_x = flip(own, 2)
    over_y = flip(own, 4)
    far_a = flip(over_x[:2], 4)
    far_b = flip(over_y[2:], 2)
    near = [(own, (0, (0, 1, 2, 3))), (over_x, (2, (0, 1, 2, 3))), (over_y, (4, (0, 1, 2, 3)))]
    near += [(far_a, (6, (0, 1))), (far_b, (6, (2, 3)))]
    return near + [(flip(a, 1), (r + 1, s)) for a, (r, s) in near]


def reduce_slabs(grad):
    pairs = grad.reshape(4, 2, 4, DEPTH, 768)
    half = (pairs[:, 0].astype(fl) + flip(pairs[:, 1], 1).astype(fl)).astype(bf)
    far_a = flip(half[3, :2], 2)
    far_b = flip(half[3, 2:], 4)
    to_y = jnp.concatenate([half[2, :2].astype(fl) + far_a.astype(fl), half[2, 2:].astype(fl)]).astype(bf)
    to_x = jnp.concatenate([half[1, :2].astype(fl), half[1, 2:].astype(fl) + far_b.astype(fl)]).astype(bf)
    plane = (half[0].astype(fl) + flip(to_x, 2).astype(fl) + flip(to_y, 4).astype(fl)).astype(bf)
    total = plane[0].astype(fl)
    for s in (1, 2, 3):
        total = total + shift(plane[s], s).astype(fl)
    return total


def gather_plain(shard):
    whole = lax.all_gather(lax.all_gather(shard, "dp", axis=0, tiled=True), "tensor", axis=0)
    whole = whole.reshape(4, SLABS, DEPTH, 768)
    order = [(4 - s) % 4 for s in range(4)]
    return [(jnp.stack([whole[t, r] for t in order]), (r, (0, 1, 2, 3))) for r in range(SLABS)]


def reduce_plain(grad):
    whole = grad.transpose(1, 0, 2, 3).reshape(4, SLABS * DEPTH, 768)
    part = lax.psum_scatter(whole.astype(fl), "tensor", scatter_dimension=0, tiled=True)
    return lax.psum_scatter(part[0], "dp", scatter_dimension=0, tiled=True)


def gather_row(row, where):
    rows = [row] + [shift(row, s) for s in (1, 2, 3)]
    return call(place_kernel, "place_rows", [((4,) + row.shape, row.dtype)], where, *rows)[0]


def moment_update(state, grad):
    moment_one = beta_first * state[1] + (1.0 - beta_first) * grad
    moment_two = beta_second * state[2] + (1.0 - beta_second) * grad * grad
    return jnp.stack([moment_one, moment_two])


def body(
    hidden_in,
    out_grad,
    segment_ids,
    step_count,
    qkv_state,
    qv_bias_state,
    out_state,
    up_state,
    up_bias_state,
    down_state,
    vector_state,
):
    n_dp = lax.axis_size("dp")
    place = lax.axis_index("tensor")
    fast = n_dp == SLABS
    spot = lax.axis_index("dp") if fast else 0
    where = jnp.stack([jnp.int32(spot), (place if fast else 0) * jnp.int32(1)])
    spin = jnp.stack([jnp.int32(0), place * jnp.int32(1)])
    gather = gather_slabs if fast else gather_plain
    reduce = reduce_slabs if fast else reduce_plain
    rows, width = qkv_state.shape[1], hidden_in.shape[2]

    q, k, v = (qkv_state[0, :, c].astype(bf) for c in range(3))
    o = out_state[0].T.astype(bf)
    cut = 2 * HD
    attn_shard = jnp.concatenate(
        [q[:, :cut], k[:, :cut], v[:, :cut], q[:, cut:], v[:, cut:], o[:, :cut], k[:, cut:], o[:, cut:]], axis=1
    )
    up_shard = up_state[0].astype(bf)
    down_shard = down_state[0].T.astype(bf)
    attn_pieces = gather(attn_shard)
    up_pieces = gather(up_shard)
    down_pieces = gather(down_shard)

    sizes = (qv_bias_state[0].size, up_bias_state[0].size, vector_state[0].size)
    small = jnp.concatenate([s[0].reshape(-1).astype(bf) for s in (qv_bias_state, up_bias_state, vector_state)])
    small = lax.all_gather(small, ("dp", "tensor")).reshape(n_dp, 4, -1).astype(fl)
    a, b = sizes[0], sizes[0] + sizes[1]
    qv = small[:, :, :a].reshape(n_dp, 4, 2, 3, -1).transpose(1, 2, 3, 0, 4).reshape(4, 2, 3 * HD)
    b_up = small[:, :, a:b].reshape(n_dp, 4, 6, -1).transpose(1, 2, 0, 3).reshape(4, 1, 768)
    vec = small[:, 0, b:].reshape(n_dp, 6, -1).transpose(1, 0, 2).reshape(6, width)
    gap = jnp.zeros((4, cut), fl)
    bias = jnp.concatenate(
        [qv[:, 0, :cut], gap, qv[:, 1, :cut], qv[:, 0, cut:], qv[:, 1, cut:], gap, gap], axis=1
    ).reshape(4, 1, 768)

    x = lax.dynamic_index_in_dim(hidden_in, place, 0, keepdims=False)
    dy = lax.dynamic_index_in_dim(out_grad, place, 0, keepdims=False)
    seg = lax.dynamic_index_in_dim(segment_ids, place, 0, keepdims=True)
    seg_col = seg.reshape(-1, 1)
    length = x.shape[0]
    wide = (4, length, 768)
    whole = ((4, SLABS, DEPTH, 768), bf)
    grad_shape = ((SLABS, 4, DEPTH, 768), bf)

    def split(pieces):
        return [p for p, _ in pieces], tuple(w for _, w in pieces)

    pieces, plan = split(attn_pieces)
    proj, ctx, lse, attn_w = call(
        functools.partial(attn_fwd_kernel, plan), "attn_fwd",
        [(wide, bf), ((4, length, 256), bf), ((4, 3, 1, length), fl), whole],
        where, x, seg, seg_col, bias, *pieces, flops=6 * 10**9,
    )
    pieces, plan = split(up_pieces)
    xhat, rstd, first, act, slope, up_w = call(
        functools.partial(up_kernel, plan), "up_fwd",
        [((length, width), fl), ((length, LANES), fl), ((length, width), bf), (wide, bf), (wide, fl), whole],
        where, x, ctx, attn_w, vec, b_up, *pieces, flops=4 * 10**9,
    )
    pieces, plan = split(down_pieces)
    out, dr2, dup, down_grad, small_two, b_up_grad = call(
        functools.partial(down_kernel, plan), "down_fwd_bwd",
        [((length, width), bf), ((length, width), fl), (wide, bf), grad_shape, ((3, width), fl), ((4, 1, 768), fl)],
        where, xhat, act, slope, dy, vec, *pieces, flops=8 * 10**9,
        scratch=[pltpu.VMEM(*whole)],
    )
    hidden_out = gather_row(out, spin)
    down_sum = reduce(down_grad)
    dr1, dctx, up_grad, small_one = call(
        up_bwd_kernel, "up_bwd",
        [((length, width), fl), ((4, length, 256), bf), grad_shape, ((3, width), fl)],
        where, dr2, dup, xhat, rstd, first, vec, up_w, attn_w, flops=6 * 10**9,
    )
    up_sum = reduce(up_grad)
    grad_row, attn_grad, bias_grad = call(
        attn_bwd_kernel, "attn_bwd",
        [((length, width), bf), grad_shape, ((4, 1, 768), fl)],
        where, x, seg, seg_col, proj, ctx, lse, dr1, dctx, attn_w, flops=10 * 10**9,
        scratch=[pltpu.VMEM(wide, bf), pltpu.VMEM((length, width), fl)],
    )
    grad_in = gather_row(grad_row, spin)
    attn_sum = reduce(attn_grad)

    bias_grad = bias_grad.reshape(4, 768)
    gq = jnp.concatenate([bias_grad[:, :cut], bias_grad[:, 384 : 384 + HD]], axis=1)
    gv = jnp.concatenate([bias_grad[:, 256 : 256 + cut], bias_grad[:, 384 + HD : 512]], axis=1)
    gqv = jnp.stack([gq, gv], axis=1).reshape(4, 2, 3, n_dp, -1).transpose(3, 0, 1, 2, 4).reshape(n_dp, 4, -1)
    gup = b_up_grad.reshape(4, 6, n_dp, -1).transpose(2, 0, 1, 3).reshape(n_dp, 4, -1)
    gvec = jnp.concatenate([small_one[:2], small_two[:2], small_one[2:], small_two[2:]])
    gvec = gvec.reshape(6, n_dp, -1).transpose(1, 0, 2).reshape(n_dp, 1, -1)
    gvec = jnp.broadcast_to(gvec, (n_dp, 4, gvec.shape[-1]))
    shares = jnp.concatenate([gqv, gup, gvec], axis=2).reshape(n_dp * 4, -1)
    shares = lax.all_to_all(shares, ("dp", "tensor"), 0, 0, tiled=True)
    sums = jnp.sum(shares, axis=0)

    gk = [attn_sum[:, 128 * n : 128 * (n + 1)] for n in range(6)]
    grad_qkv = jnp.stack(
        [
            jnp.concatenate([gk[0], gk[3][:, :HD]], axis=1),
            jnp.concatenate([gk[1], gk[5][:, :HD]], axis=1),
            jnp.concatenate([gk[2], gk[3][:, HD:]], axis=1),
        ],
        axis=1,
    )
    grad_out = jnp.concatenate([gk[4], gk[5][:, HD:]], axis=1).T
    summed = (
        grad_qkv,
        sums[:a].reshape(qv_bias_state.shape[1:]),
        grad_out,
        up_sum,
        sums[a:b].reshape(up_bias_state.shape[1:]),
        down_sum.T,
        sums[b:].reshape(vector_state.shape[1:]),
    )
    steps_f = step_count[0].astype(fl)
    factor = jnp.minimum(steps_f / warm_steps, (total_steps - steps_f) / (total_steps - warm_steps))
    fix_first = 1.0 - jnp.exp(steps_f * math.log(beta_first))
    fix_second = 1.0 - jnp.exp(steps_f * math.log(beta_second))
    states = (qkv_state, qv_bias_state, out_state, up_state, up_bias_state, down_state, vector_state)
    news = tuple((moment_update(s, g) for s, g in zip(states, summed)))
    plan_out = jnp.stack([factor, fix_first, fix_second])
    return (hidden_out, grad_in, *summed, *news, plan_out)


def solution(mesh):
    return jax.shard_map(
        body,
        mesh=mesh,
        in_specs=(
            P("dp", None, None),
            P("dp", None, None),
            P("dp", None),
            P(),
            P(None, "dp", None, "tensor"),
            P(None, None, "tensor", "dp"),
            P(None, "tensor", "dp"),
            P(None, "dp", "tensor"),
            P(None, "tensor", "dp"),
            P(None, "tensor", "dp"),
            P(None, None, "dp"),
        ),
        out_specs=(
            P("dp", None, None),
            P("dp", None, None),
            P("dp", None, "tensor"),
            P(None, "tensor", "dp"),
            P("tensor", "dp"),
            P("dp", "tensor"),
            P("tensor", "dp"),
            P("tensor", "dp"),
            P(None, "dp"),
            P(None, "dp", None, "tensor"),
            P(None, None, "tensor", "dp"),
            P(None, "tensor", "dp"),
            P(None, "dp", "tensor"),
            P(None, "tensor", "dp"),
            P(None, "tensor", "dp"),
            P(None, None, "dp"),
            P(),
        ),
        check_vma=False,
    )
```

```python
import functools
import math

import jax
import jax.numpy as jnp
from jax import lax
from jax.experimental import pallas as pl
from jax.experimental.pallas import tpu as pltpu
from jax.sharding import PartitionSpec as P

HD = 64
LANES = 128
VMEM_LIMIT = 60 * 1024 * 1024

norm_eps = 1e-05
beta_first = 0.9
beta_second = 0.999
warm_steps = 10000.0
total_steps = 200000.0

bf = jnp.bfloat16
fl = jnp.float32

SLABS = 8
DEPTH = 96
EXTRA = 16


def nt(left, right):
    return lax.dot_general(left, right, (((1,), (1,)), ((), ())), preferred_element_type=fl)


def nn(left, right):
    return lax.dot_general(left, right, (((1,), (0,)), ((), ())), preferred_element_type=fl)


def tn(left, right):
    return lax.dot_general(left, right, (((0,), (0,)), ((), ())), preferred_element_type=fl)


def low_lanes(shape):
    return lax.broadcasted_iota(jnp.int32, shape, 1) < HD


def assemble(where_ref, pieces, plan, *targets):
    for ref, (r, shifts) in zip(pieces, plan):
        slab = jnp.bitwise_xor(where_ref[0], r)
        for k, s in enumerate(shifts):
            group = jnp.bitwise_and(where_ref[1] + 4 - s, 3)
            first = 0
            for target in targets:
                last = first + target.shape[2]
                target[group, slab] = ref[k, first:last]
                first = last


def scatter_slabs(where_ref, group, value, near_ref, far_ref, extra=None):
    shift = jnp.bitwise_and(group + 4 - where_ref[1], 3)
    chip = jnp.right_shift(where_ref[0], 1)
    core = jnp.bitwise_and(where_ref[0], 1)

    def put(even_ref, odd_ref):
        for j in range(SLABS):
            out_ref = odd_ref if j % 2 else even_ref
            place = jnp.bitwise_xor(chip, j // 2)
            out_ref[place, shift, :DEPTH] = value[DEPTH * j : DEPTH * (j + 1)]
            if extra is not None:
                out_ref[place, shift, DEPTH:] = extra

    @pl.when(core == 0)
    def _():
        put(near_ref, far_ref)

    @pl.when(core == 1)
    def _():
        put(far_ref, near_ref)


def matrix(ref, group):
    return ref[group][:, :DEPTH].reshape(SLABS * DEPTH, ref.shape[-1])


def out_matrix(ref, group):
    return ref[group][:, :DEPTH, 512:768].reshape(SLABS * DEPTH, 256)


def attn_fwd_kernel(plan, where_ref, x_ref, seg_row_ref, seg_col_ref, *refs):
    pieces = refs[: len(plan)]
    proj_ref, ctx_ref, lse_ref, weight_ref, xhat_ref, rstd_ref, first_ref, vec_ref, b_up_ref = refs[-9:]
    assemble(where_ref, pieces, plan, weight_ref)
    scale = HD ** (-0.5)
    length = x_ref.shape[0]

    def group_step(g, carry):
        small = jnp.sum(weight_ref[g, :, DEPTH:].astype(fl), axis=0)
        vec_ref[...] = small[:8]
        b_up_ref[g] = small[7:8]
        x = x_ref[...]
        proj = (nn(x, matrix(weight_ref, g)) + small[6:7]).astype(bf)
        proj_ref[g] = proj
        same = seg_col_ref[...] == seg_row_ref[...]
        low = low_lanes((length, LANES))
        none = jnp.zeros((length, LANES), bf)
        parts = [proj[:, LANES * k : LANES * (k + 1)] for k in range(6)]
        outs = []
        for head in range(3):
            query = parts[0] if head < 2 else parts[3]
            keys = parts[1] if head < 2 else parts[5]
            value = parts[2] if head < 2 else parts[3]
            query = jnp.where(low, none, query) if head == 1 else jnp.where(low, query, none)
            scores = jnp.where(same, nt(keys, query) * scale, -1e30)
            top = jnp.max(scores, axis=0, keepdims=True)
            expd = jnp.exp(scores - top)
            denom = jnp.sum(expd, axis=0, keepdims=True)
            lse_ref[g, head] = top + jnp.log(denom)
            probs = (expd / denom).astype(bf)
            outs.append(tn(probs, value).astype(bf))
        ctx_ref[g] = jnp.concatenate(
            [jnp.where(low, outs[0], outs[1]), jnp.where(low, none, outs[2])], axis=1
        )
        return carry

    lax.fori_loop(0, 4, group_step, 0)
    total = x_ref[...].astype(fl) + vec_ref[4:5]
    attn = None
    for g in range(4):
        part = nt(ctx_ref[g], out_matrix(weight_ref, g))
        attn = part if attn is None else attn + part
    total = total + attn
    center = total - jnp.mean(total, axis=-1, keepdims=True)
    rstd = lax.rsqrt(jnp.mean(center * center, axis=-1, keepdims=True) + norm_eps)
    xhat = center * rstd
    xhat_ref[...] = xhat
    rstd_ref[...] = jnp.broadcast_to(rstd, rstd_ref.shape)
    first_ref[...] = (xhat * vec_ref[0:1] + vec_ref[1:2]).astype(bf)


def ffn_fwd_kernel(plan, where_ref, xhat_ref, first_ref, dy_ref, vec_ref, b_up_ref, *refs):
    pieces, refs = refs[: len(plan)], refs[len(plan) :]
    out_ref, dr2_ref, act_ref, slope_ref, small_ref, up_w_ref, down_w_ref = refs
    assemble(where_ref, pieces, plan, up_w_ref, down_w_ref)

    def step(g, carry):
        up = nn(first_ref[...], matrix(up_w_ref, g)) + b_up_ref[g]
        half = 0.5 * (1.0 + lax.erf(up * 0.7071067811865476))
        act_ref[g] = (up * half).astype(bf)
        slope_ref[g] = half + up * (jnp.exp(-0.5 * up * up) * 0.3989422804014327)
        return carry

    lax.fori_loop(0, 4, step, 0)
    ffn = None
    for g in range(4):
        part = nt(act_ref[g], matrix(down_w_ref, g))
        ffn = part if ffn is None else ffn + part
    first = xhat_ref[...] * vec_ref[0:1] + vec_ref[1:2]
    total = first + ffn + vec_ref[5:6]
    center = total - jnp.mean(total, axis=-1, keepdims=True)
    rstd = lax.rsqrt(jnp.mean(center * center, axis=-1, keepdims=True) + norm_eps)
    xhat = center * rstd
    out_ref[...] = (xhat * vec_ref[2:3] + vec_ref[3:4]).astype(bf)
    dy = dy_ref[...].astype(fl)
    small_ref[0:1] = jnp.sum(dy * xhat, axis=0, keepdims=True)
    small_ref[1:2] = jnp.sum(dy, axis=0, keepdims=True)
    dxhat = dy * vec_ref[2:3]
    dr2 = rstd * (
        dxhat
        - jnp.mean(dxhat, axis=-1, keepdims=True)
        - xhat * jnp.mean(dxhat * xhat, axis=-1, keepdims=True)
    )
    dr2_ref[...] = dr2
    small_ref[2:3] = jnp.sum(dr2, axis=0, keepdims=True)


def down_weights_kernel(where_ref, dr2_ref, act_ref, near_ref, far_ref):
    def step(g, carry):
        dffn = dr2_ref[...].astype(bf)
        scatter_slabs(where_ref, g, tn(dffn, act_ref[g]).astype(bf), near_ref, far_ref)
        return carry

    lax.fori_loop(0, 4, step, 0)


def down_bwd_kernel(where_ref, dr2_ref, slope_ref, weight_ref, dup_ref, b_up_ref):
    def step(g, carry):
        dffn = dr2_ref[...].astype(bf)
        dup = (nn(dffn, matrix(weight_ref, g)) * slope_ref[g]).astype(bf)
        dup_ref[g] = dup
        b_up_ref[g] = jnp.sum(dup.astype(fl), axis=0, keepdims=True)
        return carry

    lax.fori_loop(0, 4, step, 0)


def up_weights_kernel(where_ref, first_ref, dup_ref, *refs):
    near_ref, far_ref = refs[-2:]

    def step(g, carry):
        scatter_slabs(where_ref, g, tn(first_ref[...], dup_ref[g]).astype(bf), near_ref, far_ref)
        return carry

    lax.fori_loop(0, 4, step, 0)


def up_bwd_kernel(where_ref, dr2_ref, dup_ref, xhat_ref, rstd_ref, vec_ref, weight_ref, attn_weight_ref, *refs):
    dr1_ref, dctx_ref, small_ref = refs[-3:]
    feed = None
    for g in range(4):
        part = nt(dup_ref[g], matrix(weight_ref, g))
        feed = part if feed is None else feed + part
    dfirst = dr2_ref[...] + feed.astype(bf).astype(fl)
    xhat = xhat_ref[...]
    small_ref[0:1] = jnp.sum(dfirst * xhat, axis=0, keepdims=True)
    small_ref[1:2] = jnp.sum(dfirst, axis=0, keepdims=True)
    dxhat = dfirst * vec_ref[0:1]
    dr1 = rstd_ref[:, 0:1] * (
        dxhat
        - jnp.mean(dxhat, axis=-1, keepdims=True)
        - xhat * jnp.mean(dxhat * xhat, axis=-1, keepdims=True)
    )
    dr1_ref[...] = dr1
    small_ref[2:3] = jnp.sum(dr1, axis=0, keepdims=True)
    dattn = dr1.astype(bf)
    for g in range(4):
        dctx_ref[g] = nn(dattn, out_matrix(attn_weight_ref, g)).astype(bf)


def attn_bwd_kernel(where_ref, seg_row_ref, seg_col_ref, proj_ref, lse_ref, dr1_ref, dctx_ref, weight_ref, *refs):
    grad_in_ref, dproj_ref, bias_ref, back_ref = refs[-4:]
    scale = HD ** (-0.5)
    length = dr1_ref.shape[0]
    back_ref[...] = jnp.zeros_like(back_ref)

    def step(g, carry):
        same = seg_col_ref[...] == seg_row_ref[...]
        low = low_lanes((length, LANES))
        none = jnp.zeros((length, LANES), bf)
        parts = [proj_ref[g, :, LANES * k : LANES * (k + 1)] for k in range(6)]
        dctx = [dctx_ref[g, :, :LANES], dctx_ref[g, :, LANES:]]
        dq, dk, dv = [], [], []
        for head in range(3):
            query = parts[0] if head < 2 else parts[3]
            keys = parts[1] if head < 2 else parts[5]
            value = parts[2] if head < 2 else parts[3]
            dout = dctx[0] if head < 2 else dctx[1]
            query_in = jnp.where(low, none, query) if head == 1 else jnp.where(low, query, none)
            dout_in = jnp.where(low, dout, none) if head == 0 else jnp.where(low, none, dout)
            scores = jnp.where(same, nt(keys, query_in) * scale, -1e30)
            probs = jnp.exp(scores - lse_ref[g, head])
            dprobs = nt(value, dout_in)
            dv.append(nn(probs.astype(bf), dout))
            row_dot = jnp.sum(probs * dprobs, axis=0, keepdims=True)
            dscores = (probs * (dprobs - row_dot)).astype(bf)
            dq.append(tn(dscores, keys) * scale)
            dk.append(nn(dscores, query) * scale)
        dproj = jnp.concatenate(
            [
                jnp.where(low, dq[0], dq[1]).astype(bf),
                jnp.where(low, dk[0], dk[1]).astype(bf),
                jnp.where(low, dv[0], dv[1]).astype(bf),
                jnp.where(low, dq[2], dv[2]).astype(bf),
                none,
                jnp.where(low, dk[2].astype(bf), none),
            ],
            axis=1,
        )
        dproj_ref[g] = dproj
        bias_ref[g] = jnp.sum(dproj.astype(fl), axis=0, keepdims=True)
        back_ref[...] += nt(dproj, matrix(weight_ref, g))
        return carry

    lax.fori_loop(0, 4, step, 0)
    dr1 = dr1_ref[...]
    grad_in_ref[...] = (dr1 + back_ref[...].astype(bf).astype(fl)).astype(bf)


def attn_weights_kernel(where_ref, x_ref, dproj_ref, ctx_ref, dr1_ref, bias_ref, b_up_ref, one_ref, two_ref, *refs):
    near_ref, far_ref, small_ref = refs[-3:]
    small_ref[...] = jnp.zeros_like(small_ref)
    small_ref[0:2] = one_ref[0:2]
    small_ref[2:4] = two_ref[0:2]
    small_ref[4:5] = one_ref[2:3]
    small_ref[5:6] = two_ref[2:3]

    def grads(g, carry):
        small_ref[6:7] = bias_ref[g]
        small_ref[7:8] = b_up_ref[g]
        main = tn(x_ref[...], dproj_ref[g])
        side = tn(dr1_ref[...].astype(bf), ctx_ref[g])
        whole = jnp.concatenate([main[:, :512], main[:, 512:] + side], axis=1).astype(bf)
        scatter_slabs(where_ref, g, whole, near_ref, far_ref, small_ref[...].astype(bf))
        return carry

    lax.fori_loop(0, 4, grads, 0)


def place_kernel(where_ref, own_ref, *refs):
    out_ref = refs[-1]
    spot = where_ref[1]
    out_ref[spot] = own_ref[...]
    for d in (1, 2, 3):
        up_ref, down_ref = refs[2 * d - 2], refs[2 * d - 1]

        @pl.when(spot >= d)
        def _():
            out_ref[jnp.maximum(spot - d, 0)] = up_ref[...]

        @pl.when(spot + d < 4)
        def _():
            out_ref[jnp.minimum(spot + d, 3)] = down_ref[...]


smem = pl.BlockSpec(memory_space=pltpu.SMEM)
vmem = pl.BlockSpec(memory_space=pltpu.VMEM)


def call(kernel, name, outs, where, *args, scratch=(), after=()):
    return pl.pallas_call(
        kernel,
        name=name,
        out_shape=[jax.ShapeDtypeStruct(s, d) for s, d in outs],
        in_specs=[smem] + [vmem] * len(args) + [pl.BlockSpec(memory_space=pl.ANY)] * len(after),
        out_specs=[vmem] * len(outs),
        scratch_shapes=list(scratch),
        compiler_params=pltpu.CompilerParams(vmem_limit_bytes=VMEM_LIMIT),
        cost_estimate=pl.CostEstimate(flops=COST, bytes_accessed=COST, transcendentals=0),
    )(where, *args, *after)


COST = 1000


def flip(value, bits):
    n = lax.axis_size("dp")
    return lax.ppermute(value, "dp", [(k, k ^ bits) for k in range(n)])


def shift(value, s):
    return lax.ppermute(value, "tensor", [(k, (k + s) % 4) for k in range(4)])


def along(value, step, senders):
    return lax.ppermute(value, "tensor", [(k, k + step) for k in senders])


def with_core(near):
    return near + [(flip(a, 1), (r + 1, s)) for a, (r, s) in near]


ALL = (0, 1, 2, 3)


def tensor_stack(shard):
    return jnp.stack([shard] + [shift(shard, s) for s in (1, 2, 3)])


def gather_direct(own):
    return with_core([(own, (0, ALL))] + [(flip(own, r), (r, ALL)) for r in (2, 4, 6)])


def late(values, gate):
    return list(lax.optimization_barrier((*values, gate))[:-1])


def gather_staged(own, gate):
    over_x = flip(own, 2)
    over_y = flip(own, 4)
    half_x, half_y = late([over_x[:2], over_y[2:]], gate)
    far_a = flip(half_x, 4)
    far_b = flip(half_y, 2)
    near = [(own, (0, ALL)), (over_x, (2, ALL)), (over_y, (4, ALL))]
    return with_core(near + [(far_a, (6, (0, 1))), (far_b, (6, (2, 3)))])


def add(*values):
    total = values[0].astype(fl)
    for value in values[1:]:
        total = total + value.astype(fl)
    return total


def reduce_core(near, far, gate):
    (got,) = late([flip(far, 1)], gate)
    return [add(near[r], got[r]).astype(bf) for r in range(4)]


def reduce_plane(half, gate):
    got = late([flip(half[r], 2 * r) for r in (1, 2, 3)], gate)
    sums = [add(half[0][s], *[g[s] for g in got]) for s in range(4)]
    return [sums[0]] + [v.astype(bf) for v in sums[1:]]


def reduce_tensor(plane, gate):
    return [plane[0]] + late([shift(plane[s], s) for s in (1, 2, 3)], gate)


def gather_plain(shard, extra=None):
    whole = lax.all_gather(lax.all_gather(shard, "dp", axis=0, tiled=True), "tensor", axis=0)
    whole = whole.reshape(4, SLABS, -1, 768)
    if extra is not None:
        extra = lax.all_gather(lax.psum(extra, "dp"), "tensor", axis=0)[:, None].astype(bf)
        extra = jnp.concatenate([extra] + [jnp.zeros_like(extra)] * (SLABS - 1), axis=1)
        whole = jnp.concatenate([whole, extra], axis=2)
    order = [(4 - s) % 4 for s in range(4)]
    return [(jnp.stack([whole[t, r] for t in order]), (r, ALL)) for r in range(SLABS)]


def reduce_plain(near, far):
    grad = jnp.stack([near, far], axis=1).reshape(SLABS, 4, -1, 768).astype(fl)
    whole = grad[:, :, :DEPTH].transpose(1, 0, 2, 3).reshape(4, SLABS * DEPTH, 768)
    part = lax.psum_scatter(whole, "tensor", scatter_dimension=0, tiled=True)
    part = lax.psum_scatter(part[0], "dp", scatter_dimension=0, tiled=True)
    if near.shape[2] == DEPTH:
        return part
    extra = lax.psum_scatter(lax.psum(grad[0, :, DEPTH:], "dp"), "tensor", scatter_dimension=0, tiled=True)[0]
    return jnp.concatenate([part, extra])


def forward_rows(up, down, d, gate):
    return late([along(up, 1, range(d - 1, 3)), along(down, -1, range(1, 5 - d))], gate)


def place_rows(row, steps, where):
    pieces = [piece for step in steps for piece in step]
    return call(place_kernel, "place_rows", [((4,) + row.shape, row.dtype)], where, row, *pieces)[0]


def moment_update(state, grad):
    moment_one = beta_first * state[1] + (1.0 - beta_first) * grad
    moment_two = beta_second * state[2] + (1.0 - beta_second) * grad * grad
    return jnp.stack([moment_one, moment_two])


def body(
    hidden_in,
    out_grad,
    segment_ids,
    step_count,
    qkv_state,
    qv_bias_state,
    out_state,
    up_state,
    up_bias_state,
    down_state,
    vector_state,
):
    n_dp = lax.axis_size("dp")
    place = lax.axis_index("tensor")
    fast = n_dp == SLABS
    spot = lax.axis_index("dp") if fast else 0
    where = jnp.stack([jnp.int32(spot), (place if fast else 0) * jnp.int32(1)])
    spin = jnp.stack([jnp.int32(0), place * jnp.int32(1)])
    rows, width = qkv_state.shape[1], hidden_in.shape[2]
    cut = 2 * HD

    def spread(value, axis, whole):
        full = jnp.zeros(value.shape[:-1] + (whole,), bf)
        return lax.dynamic_update_slice_in_dim(full, value.astype(bf), axis * value.shape[-1], value.ndim - 1)

    dp = lax.axis_index("dp")
    q, k, v = (qkv_state[0, :, c].astype(bf) for c in range(3))
    o = out_state[0].T.astype(bf)
    attn_shard = jnp.concatenate(
        [q[:, :cut], k[:, :cut], v[:, :cut], q[:, cut:], v[:, cut:], o[:, :cut], k[:, cut:], o[:, cut:]], axis=1
    )
    bq, bv = spread(qv_bias_state[0], dp, HD).reshape(2, 3 * HD)
    gap = jnp.zeros((cut,), bf)
    bias = jnp.concatenate([bq[:cut], gap, bv[:cut], bq[cut:], bv[cut:], gap, gap])
    b_up = spread(up_bias_state[0], dp, LANES).reshape(1, 768)
    extra = jnp.concatenate(
        [spread(vector_state[0], dp, width), bias[None], b_up, jnp.zeros((EXTRA - 8, width), bf)]
    )
    up_shard = up_state[0].astype(bf)
    down_shard = down_state[0].T.astype(bf)

    x = lax.dynamic_index_in_dim(hidden_in, place, 0, keepdims=False)
    dy = lax.dynamic_index_in_dim(out_grad, place, 0, keepdims=False)
    seg = lax.dynamic_index_in_dim(segment_ids, place, 0, keepdims=True)
    seg_col = seg.reshape(-1, 1)
    length = x.shape[0]
    wide = (4, length, 768)
    row_f, row_b = ((length, width), fl), ((length, width), bf)
    whole = ((4, SLABS, DEPTH, 768), bf)
    attn_whole = ((4, SLABS, DEPTH + EXTRA, 768), bf)
    grad_shape = ((4, 4, DEPTH, 768), bf)
    attn_grad_shape = ((4, 4, DEPTH + EXTRA, 768), bf)
    thin = ((4, 1, 768), fl)

    if fast:
        own = tensor_stack(jnp.concatenate([attn_shard, extra]))
        attn_pieces = gather_direct(own)
        (ffn_shard,) = late([jnp.concatenate([up_shard, down_shard])], attn_pieces[4][0])
        ffn_own = tensor_stack(ffn_shard)
        wait = [ffn_own]
    else:
        attn_pieces = gather_plain(attn_shard, extra)
        ups, downs = gather_plain(up_shard), gather_plain(down_shard)
        ffn_pieces = [(jnp.concatenate([u, d], axis=1), w) for (u, w), (d, _) in zip(ups, downs)]
        wait = []

    def split(pieces):
        return [p for p, _ in pieces], tuple(w for _, w in pieces)

    pieces, plan = split(attn_pieces)
    proj, ctx, lse, attn_w, xhat, rstd, first, vec, b_up = call(
        functools.partial(attn_fwd_kernel, plan), "attn_fwd",
        [(wide, bf), ((4, length, 256), bf), ((4, 3, 1, length), fl), attn_whole, row_f, ((length, LANES), fl), row_b,
         ((8, width), fl), thin],
        where, x, seg, seg_col, *pieces, after=wait,
    )
    if fast:
        ffn_pieces = gather_staged(ffn_own, vec)
    pieces, plan = split(ffn_pieces)
    out, dr2, act, slope, small_two, up_w, down_w = call(
        functools.partial(ffn_fwd_kernel, plan), "ffn_fwd",
        [row_b, row_f, (wide, bf), (wide, fl), ((3, width), fl), whole, whole],
        where, xhat, first, dy, vec, b_up, *pieces,
    )
    down_near, down_far = call(
        down_weights_kernel, "down_weights", [grad_shape, grad_shape], where, dr2, act,
    )
    dup, b_up_grad = call(down_bwd_kernel, "down_bwd", [(wide, bf), thin], where, dr2, slope, down_w)
    down_half = reduce_core(down_near, down_far, b_up_grad) if fast else []
    out_one = forward_rows(out, out, 1, b_up_grad)
    up_near, up_far = call(
        up_weights_kernel, "up_weights", [grad_shape, grad_shape], where, first, dup, after=out_one,
    )
    dr1, dctx, small_one = call(
        up_bwd_kernel, "up_bwd", [row_f, ((4, length, 256), bf), ((3, width), fl)],
        where, dr2, dup, xhat, rstd, vec, up_w, attn_w, after=down_half,
    )
    out_two = forward_rows(*out_one, 2, small_one)
    down_plane = reduce_plane(down_half, small_one) if fast else []
    up_half = reduce_core(up_near, up_far, small_one) if fast else []
    grad_row, dproj, bias_grad = call(
        attn_bwd_kernel, "attn_bwd", [row_b, (wide, bf), thin],
        where, seg, seg_col, proj, lse, dr1, dctx, attn_w, after=out_two + down_plane + up_half,
        scratch=[pltpu.VMEM((length, width), fl)],
    )
    out_three = forward_rows(*out_two, 3, bias_grad)
    down_parts = reduce_tensor(down_plane, bias_grad) if fast else []
    up_plane = reduce_plane(up_half, bias_grad) if fast else []
    attn_near, attn_far = call(
        attn_weights_kernel, "attn_weights", [attn_grad_shape, attn_grad_shape],
        where, x, dproj, ctx, dr1, bias_grad, b_up_grad, small_one, small_two,
        scratch=[pltpu.VMEM((EXTRA, width), fl)], after=out_three + down_parts + up_plane,
    )
    in_one = forward_rows(grad_row, grad_row, 1, attn_near)
    in_two = forward_rows(*in_one, 2, attn_near)
    in_three = forward_rows(*in_two, 3, attn_near)
    hidden_out = place_rows(out, (out_one, out_two, out_three), spin)
    grad_in = place_rows(grad_row, (in_one, in_two, in_three), spin)
    if fast:
        down_sum = add(*down_parts)
        up_sum = add(*reduce_tensor(up_plane, attn_near))
        attn_half = reduce_core(attn_near, attn_far, attn_near)
        attn_sum = add(*reduce_tensor(reduce_plane(attn_half, attn_near), attn_near))
    else:
        down_sum = reduce_plain(down_near, down_far)
        up_sum = reduce_plain(up_near, up_far)
        attn_sum = reduce_plain(attn_near, attn_far)

    def own_part(value):
        size = value.shape[-1] // n_dp
        return lax.dynamic_slice_in_dim(value, dp * size, size, value.ndim - 1)

    small = attn_sum[rows:]
    gq = jnp.concatenate([small[6, :cut], small[6, 384 : 384 + HD]])
    gv = jnp.concatenate([small[6, 256 : 256 + cut], small[6, 384 + HD : 512]])
    grad_qv = own_part(jnp.stack([gq, gv]).reshape(2, 3, HD))
    grad_b_up = own_part(small[7].reshape(6, LANES))
    grad_vectors = own_part(small[:6])

    gk = [attn_sum[:rows, 128 * n : 128 * (n + 1)] for n in range(6)]
    grad_qkv = jnp.stack(
        [
            jnp.concatenate([gk[0], gk[3][:, :HD]], axis=1),
            jnp.concatenate([gk[1], gk[5][:, :HD]], axis=1),
            jnp.concatenate([gk[2], gk[3][:, HD:]], axis=1),
        ],
        axis=1,
    )
    grad_out = jnp.concatenate([gk[4], gk[5][:, HD:]], axis=1).T
    summed = (grad_qkv, grad_qv, grad_out, up_sum, grad_b_up, down_sum.T, grad_vectors)
    steps_f = step_count[0].astype(fl)
    factor = jnp.minimum(steps_f / warm_steps, (total_steps - steps_f) / (total_steps - warm_steps))
    fix_first = 1.0 - jnp.exp(steps_f * math.log(beta_first))
    fix_second = 1.0 - jnp.exp(steps_f * math.log(beta_second))
    states = (qkv_state, qv_bias_state, out_state, up_state, up_bias_state, down_state, vector_state)
    news = tuple((moment_update(s, g) for s, g in zip(states, summed)))
    plan_out = jnp.stack([factor, fix_first, fix_second])
    return (hidden_out, grad_in, *summed, *news, plan_out)


def solution(mesh):
    return jax.shard_map(
        body,
        mesh=mesh,
        in_specs=(
            P("dp", None, None),
            P("dp", None, None),
            P("dp", None),
            P(),
            P(None, "dp", None, "tensor"),
            P(None, None, "tensor", "dp"),
            P(None, "tensor", "dp"),
            P(None, "dp", "tensor"),
            P(None, "tensor", "dp"),
            P(None, "tensor", "dp"),
            P(None, None, "dp"),
        ),
        out_specs=(
            P("dp", None, None),
            P("dp", None, None),
            P("dp", None, "tensor"),
            P(None, "tensor", "dp"),
            P("tensor", "dp"),
            P("dp", "tensor"),
            P("tensor", "dp"),
            P("tensor", "dp"),
            P(None, "dp"),
            P(None, "dp", None, "tensor"),
            P(None, None, "tensor", "dp"),
            P(None, "tensor", "dp"),
            P(None, "dp", "tensor"),
            P(None, "tensor", "dp"),
            P(None, "tensor", "dp"),
            P(None, None, "dp"),
            P(),
        ),
        check_vma=False,
    )
```

```python
import functools
import math

import jax
import jax.numpy as jnp
from jax import lax
from jax.experimental import pallas as pl
from jax.experimental.pallas import tpu as pltpu
from jax.sharding import PartitionSpec as P

HD = 64
LANES = 128
VMEM_LIMIT = 60 * 1024 * 1024

norm_eps = 1e-05
beta_first = 0.9
beta_second = 0.999
warm_steps = 10000.0
total_steps = 200000.0

bf = jnp.bfloat16
fl = jnp.float32

SLABS = 8
DEPTH = 96
EXTRA = 16


def nt(left, right):
    return lax.dot_general(left, right, (((1,), (1,)), ((), ())), preferred_element_type=fl)


def nn(left, right):
    return lax.dot_general(left, right, (((1,), (0,)), ((), ())), preferred_element_type=fl)


def tn(left, right):
    return lax.dot_general(left, right, (((0,), (0,)), ((), ())), preferred_element_type=fl)


def low_lanes(shape):
    return lax.broadcasted_iota(jnp.int32, shape, 1) < HD


def assemble(where_ref, pieces, plan, *targets):
    for ref, (r, hops) in zip(pieces, plan):
        slab = jnp.bitwise_xor(where_ref[0], r)
        for k, hop in enumerate(hops):
            group = jnp.bitwise_xor(where_ref[1], hop)
            first = 0
            for target in targets:
                last = first + target.shape[2]
                target[group, slab] = ref[k, first:last]
                first = last


def scatter_slabs(where_ref, group, value, near_ref, far_refs, extra=None, x_last=False):
    hop = jnp.bitwise_xor(group, where_ref[1])
    hop = 2 * jnp.bitwise_and(hop, 1) + jnp.right_shift(hop, 1)
    chip = jnp.right_shift(where_ref[0], 1)
    core = jnp.bitwise_and(where_ref[0], 1)

    def put(near, far):
        for j in range(SLABS // 2):
            place = jnp.bitwise_xor(chip, j)
            if x_last:
                place = 2 * jnp.bitwise_and(place, 1) + jnp.right_shift(place, 1)
            half, low = jnp.right_shift(place, 1), jnp.bitwise_and(place, 1)

            def store(ref, index, slab):
                ref[index, hop, :DEPTH] = value[DEPTH * slab : DEPTH * (slab + 1)]
                if extra is not None:
                    ref[index, hop, DEPTH:] = extra

            store(near_ref, place, 2 * j + near)
            for k in (0, 1):
                pl.when(half == k)(functools.partial(store, far_refs[k], low, 2 * j + far))

    pl.when(core == 0)(functools.partial(put, 0, 1))
    pl.when(core == 1)(functools.partial(put, 1, 0))


def matrix(ref, group):
    return ref[group][:, :DEPTH].reshape(SLABS * DEPTH, ref.shape[-1])


def out_matrix(ref, group):
    return ref[group][:, :DEPTH, 512:768].reshape(SLABS * DEPTH, 256)


def attn_fwd_kernel(plan, where_ref, x_ref, seg_row_ref, seg_col_ref, *refs):
    pieces = refs[: len(plan)]
    proj_ref, ctx_ref, lse_ref, weight_ref, xhat_ref, rstd_ref, first_ref, vec_ref, b_up_ref = refs[-9:]
    assemble(where_ref, pieces, plan, weight_ref)
    scale = HD ** (-0.5)
    length = x_ref.shape[0]

    def group_step(g, carry):
        small = jnp.sum(weight_ref[g, :, DEPTH:].astype(fl), axis=0)
        vec_ref[...] = small[:8]
        b_up_ref[g] = small[7:8]
        x = x_ref[...]
        proj = (nn(x, matrix(weight_ref, g)) + small[6:7]).astype(bf)
        proj_ref[g] = proj
        same = seg_col_ref[...] == seg_row_ref[...]
        low = low_lanes((length, LANES))
        none = jnp.zeros((length, LANES), bf)
        parts = [proj[:, LANES * k : LANES * (k + 1)] for k in range(6)]
        outs = []
        for head in range(3):
            query = parts[0] if head < 2 else parts[3]
            keys = parts[1] if head < 2 else parts[5]
            value = parts[2] if head < 2 else parts[3]
            query = jnp.where(low, none, query) if head == 1 else jnp.where(low, query, none)
            scores = jnp.where(same, nt(keys, query) * scale, -1e30)
            top = jnp.max(scores, axis=0, keepdims=True)
            expd = jnp.exp(scores - top)
            denom = jnp.sum(expd, axis=0, keepdims=True)
            lse_ref[g, head] = top + jnp.log(denom)
            probs = (expd / denom).astype(bf)
            outs.append(tn(probs, value).astype(bf))
        ctx_ref[g] = jnp.concatenate(
            [jnp.where(low, outs[0], outs[1]), jnp.where(low, none, outs[2])], axis=1
        )
        return carry

    lax.fori_loop(0, 4, group_step, 0)
    total = x_ref[...].astype(fl) + vec_ref[4:5]
    attn = None
    for g in range(4):
        part = nt(ctx_ref[g], out_matrix(weight_ref, g))
        attn = part if attn is None else attn + part
    total = total + attn
    center = total - jnp.mean(total, axis=-1, keepdims=True)
    rstd = lax.rsqrt(jnp.mean(center * center, axis=-1, keepdims=True) + norm_eps)
    xhat = center * rstd
    xhat_ref[...] = xhat
    rstd_ref[...] = jnp.broadcast_to(rstd, rstd_ref.shape)
    first_ref[...] = (xhat * vec_ref[0:1] + vec_ref[1:2]).astype(bf)


def ffn_fwd_kernel(plan, where_ref, xhat_ref, first_ref, dy_ref, vec_ref, b_up_ref, *refs):
    pieces, refs = refs[: len(plan)], refs[len(plan) :]
    out_ref, dr2_ref, act_ref, slope_ref, small_ref, up_w_ref, down_w_ref = refs
    assemble(where_ref, pieces, plan, up_w_ref, down_w_ref)

    def step(g, carry):
        up = nn(first_ref[...], matrix(up_w_ref, g)) + b_up_ref[g]
        half = 0.5 * (1.0 + lax.erf(up * 0.7071067811865476))
        act_ref[g] = (up * half).astype(bf)
        slope_ref[g] = half + up * (jnp.exp(-0.5 * up * up) * 0.3989422804014327)
        return carry

    lax.fori_loop(0, 4, step, 0)
    ffn = None
    for g in range(4):
        part = nt(act_ref[g], matrix(down_w_ref, g))
        ffn = part if ffn is None else ffn + part
    first = xhat_ref[...] * vec_ref[0:1] + vec_ref[1:2]
    total = first + ffn + vec_ref[5:6]
    center = total - jnp.mean(total, axis=-1, keepdims=True)
    rstd = lax.rsqrt(jnp.mean(center * center, axis=-1, keepdims=True) + norm_eps)
    xhat = center * rstd
    out_ref[...] = (xhat * vec_ref[2:3] + vec_ref[3:4]).astype(bf)
    dy = dy_ref[...].astype(fl)
    small_ref[0:1] = jnp.sum(dy * xhat, axis=0, keepdims=True)
    small_ref[1:2] = jnp.sum(dy, axis=0, keepdims=True)
    dxhat = dy * vec_ref[2:3]
    dr2 = rstd * (
        dxhat
        - jnp.mean(dxhat, axis=-1, keepdims=True)
        - xhat * jnp.mean(dxhat * xhat, axis=-1, keepdims=True)
    )
    dr2_ref[...] = dr2
    small_ref[2:3] = jnp.sum(dr2, axis=0, keepdims=True)


def down_weights_kernel(where_ref, dr2_ref, act_ref, near_ref, *far_refs):
    def step(g, carry):
        dffn = dr2_ref[...].astype(bf)
        scatter_slabs(where_ref, g, tn(dffn, act_ref[g]).astype(bf), near_ref, far_refs, x_last=True)
        return carry

    lax.fori_loop(0, 4, step, 0)


def down_bwd_kernel(where_ref, dr2_ref, slope_ref, weight_ref, dup_ref, b_up_ref):
    def step(g, carry):
        dffn = dr2_ref[...].astype(bf)
        dup = (nn(dffn, matrix(weight_ref, g)) * slope_ref[g]).astype(bf)
        dup_ref[g] = dup
        b_up_ref[g] = jnp.sum(dup.astype(fl), axis=0, keepdims=True)
        return carry

    lax.fori_loop(0, 4, step, 0)


def up_weights_kernel(where_ref, first_ref, dup_ref, *refs):
    near_ref, *far_refs = refs

    def step(g, carry):
        scatter_slabs(where_ref, g, tn(first_ref[...], dup_ref[g]).astype(bf), near_ref, far_refs)
        return carry

    lax.fori_loop(0, 4, step, 0)


def up_bwd_kernel(where_ref, dr2_ref, dup_ref, xhat_ref, rstd_ref, vec_ref, weight_ref, attn_weight_ref, *refs):
    dr1_ref, dctx_ref, small_ref = refs[-3:]
    feed = None
    for g in range(4):
        part = nt(dup_ref[g], matrix(weight_ref, g))
        feed = part if feed is None else feed + part
    dfirst = dr2_ref[...] + feed.astype(bf).astype(fl)
    xhat = xhat_ref[...]
    small_ref[0:1] = jnp.sum(dfirst * xhat, axis=0, keepdims=True)
    small_ref[1:2] = jnp.sum(dfirst, axis=0, keepdims=True)
    dxhat = dfirst * vec_ref[0:1]
    dr1 = rstd_ref[:, 0:1] * (
        dxhat
        - jnp.mean(dxhat, axis=-1, keepdims=True)
        - xhat * jnp.mean(dxhat * xhat, axis=-1, keepdims=True)
    )
    dr1_ref[...] = dr1
    small_ref[2:3] = jnp.sum(dr1, axis=0, keepdims=True)
    dattn = dr1.astype(bf)
    for g in range(4):
        dctx_ref[g] = nn(dattn, out_matrix(attn_weight_ref, g)).astype(bf)


def attn_bwd_kernel(where_ref, seg_row_ref, seg_col_ref, proj_ref, lse_ref, dr1_ref, dctx_ref, weight_ref, *refs):
    grad_in_ref, dproj_ref, bias_ref, back_ref = refs[-4:]
    scale = HD ** (-0.5)
    length = dr1_ref.shape[0]
    back_ref[...] = jnp.zeros_like(back_ref)

    def step(g, carry):
        same = seg_col_ref[...] == seg_row_ref[...]
        low = low_lanes((length, LANES))
        none = jnp.zeros((length, LANES), bf)
        parts = [proj_ref[g, :, LANES * k : LANES * (k + 1)] for k in range(6)]
        dctx = [dctx_ref[g, :, :LANES], dctx_ref[g, :, LANES:]]
        dq, dk, dv = [], [], []
        for head in range(3):
            query = parts[0] if head < 2 else parts[3]
            keys = parts[1] if head < 2 else parts[5]
            value = parts[2] if head < 2 else parts[3]
            dout = dctx[0] if head < 2 else dctx[1]
            query_in = jnp.where(low, none, query) if head == 1 else jnp.where(low, query, none)
            dout_in = jnp.where(low, dout, none) if head == 0 else jnp.where(low, none, dout)
            scores = jnp.where(same, nt(keys, query_in) * scale, -1e30)
            probs = jnp.exp(scores - lse_ref[g, head])
            dprobs = nt(value, dout_in)
            dv.append(nn(probs.astype(bf), dout))
            row_dot = jnp.sum(probs * dprobs, axis=0, keepdims=True)
            dscores = (probs * (dprobs - row_dot)).astype(bf)
            dq.append(tn(dscores, keys) * scale)
            dk.append(nn(dscores, query) * scale)
        dproj = jnp.concatenate(
            [
                jnp.where(low, dq[0], dq[1]).astype(bf),
                jnp.where(low, dk[0], dk[1]).astype(bf),
                jnp.where(low, dv[0], dv[1]).astype(bf),
                jnp.where(low, dq[2], dv[2]).astype(bf),
                none,
                jnp.where(low, dk[2].astype(bf), none),
            ],
            axis=1,
        )
        dproj_ref[g] = dproj
        bias_ref[g] = jnp.sum(dproj.astype(fl), axis=0, keepdims=True)
        back_ref[...] += nt(dproj, matrix(weight_ref, g))
        return carry

    lax.fori_loop(0, 4, step, 0)
    dr1 = dr1_ref[...]
    grad_in_ref[...] = (dr1 + back_ref[...].astype(bf).astype(fl)).astype(bf)


def attn_weights_kernel(where_ref, x_ref, dproj_ref, ctx_ref, dr1_ref, bias_ref, b_up_ref, one_ref, two_ref, *refs):
    near_ref, *far_refs, small_ref = refs
    small_ref[...] = jnp.zeros_like(small_ref)
    small_ref[0:2] = one_ref[0:2]
    small_ref[2:4] = two_ref[0:2]
    small_ref[4:5] = one_ref[2:3]
    small_ref[5:6] = two_ref[2:3]

    def grads(g, carry):
        small_ref[6:7] = bias_ref[g]
        small_ref[7:8] = b_up_ref[g]
        main = tn(x_ref[...], dproj_ref[g])
        side = tn(dr1_ref[...].astype(bf), ctx_ref[g])
        whole = jnp.concatenate([main[:, :512], main[:, 512:] + side], axis=1).astype(bf)
        scatter_slabs(where_ref, g, whole, near_ref, far_refs, small_ref[...].astype(bf))
        return carry

    lax.fori_loop(0, 4, grads, 0)


def place_kernel(where_ref, *refs):
    out_ref = refs[-1]
    for d, ref in enumerate(refs[:-1]):
        out_ref[jnp.bitwise_and(where_ref[1] + 4 - d, 3)] = ref[...]


smem = pl.BlockSpec(memory_space=pltpu.SMEM)
vmem = pl.BlockSpec(memory_space=pltpu.VMEM)


def call(kernel, name, outs, where, *args, scratch=(), after=()):
    if after:
        (where,) = late([where], *after)
    return pl.pallas_call(
        kernel,
        name=name,
        out_shape=[jax.ShapeDtypeStruct(s, d) for s, d in outs],
        in_specs=[smem] + [vmem] * len(args),
        out_specs=[vmem] * len(outs),
        scratch_shapes=list(scratch),
        compiler_params=pltpu.CompilerParams(vmem_limit_bytes=VMEM_LIMIT),
        cost_estimate=pl.CostEstimate(flops=COST, bytes_accessed=COST, transcendentals=0),
    )(where, *args)


COST = 1000


def flip(value, bits):
    n = lax.axis_size("dp")
    return lax.ppermute(value, "dp", [(k, k ^ bits) for k in range(n)])


def cross(value, bits):
    return lax.ppermute(value, "tensor", [(k, k ^ bits) for k in range(4)])


def rotate(value):
    return lax.ppermute(value, "tensor", [(k, (k + 1) % 4) for k in range(4)])


def late(values, *gates):
    return list(lax.optimization_barrier((*values, *gates))[: len(values)])


def with_core(near):
    return near + [(flip(a, 1), (r + 1, s)) for a, (r, s) in near]


ALL = (0, 1, 2, 3)


def tensor_stack(shard):
    return jnp.stack([shard] + [cross(shard, hop) for hop in (1, 2, 3)])


def tensor_stack_doubling(shard):
    pair = jnp.stack([shard, cross(shard, 1)])
    return jnp.concatenate([pair, cross(pair, 2)])


def gather_direct(own):
    return with_core([(own, (0, ALL))] + [(flip(own, r), (r, ALL)) for r in (2, 4, 6)])


def gather_staged(own, gate):
    over_x = flip(own, 2)
    over_y = flip(own, 4)
    half_x, half_y = late([over_x[:2], over_y[2:]], gate)
    far_a = flip(half_x, 4)
    far_b = flip(half_y, 2)
    near = [(own, (0, ALL)), (over_x, (2, ALL)), (over_y, (4, ALL))]
    return with_core(near + [(far_a, (6, (0, 1))), (far_b, (6, (2, 3)))])


def add(*values):
    total = values[0].astype(fl)
    for value in values[1:]:
        total = total + value.astype(fl)
    return total


def reduce_core(near, far, gate, cuts=(0, 2)):
    got = late([flip(half, 1) for half in far], gate)
    return [
        add(near[2 * k + a : 2 * k + b], got[k][a:b]).astype(bf) for k in (0, 1) for a, b in zip(cuts, cuts[1:])
    ]


def reduce_pair(half, axis, gate):
    (got,) = late([flip(half[1], 2 * axis)], gate)
    return [add(half[0][k], got[k]).astype(bf) for k in (0, 1)]


def reduce_chip(pair, axis, gate):
    (got,) = late([flip(pair[1], 2 * axis)], gate)
    return [add(pair[0][:2], got[:2]).astype(bf), add(pair[0][2:], got[2:]).astype(bf)]


def reduce_plane(half, gate):
    half = [h[0] for h in half]
    got = late([flip(half[r], 2 * r) for r in (1, 2, 3)], gate)
    return [add(half[0][k : k + 2], *[g[k : k + 2] for g in got]).astype(bf) for k in (0, 2)]


def reduce_tensor(plane, gate):
    (got,) = late([cross(plane[1], 1)], gate)
    near, far = add(plane[0][0], got[0]), add(plane[0][1], got[1]).astype(bf)
    return add(near, cross(far, 2))


def gather_plain(shard, extra=None):
    whole = lax.all_gather(lax.all_gather(shard, "dp", axis=0, tiled=True), "tensor", axis=0)
    whole = whole.reshape(4, SLABS, -1, 768)
    if extra is not None:
        extra = lax.all_gather(lax.psum(extra, "dp"), "tensor", axis=0)[:, None].astype(bf)
        extra = jnp.concatenate([extra] + [jnp.zeros_like(extra)] * (SLABS - 1), axis=1)
        whole = jnp.concatenate([whole, extra], axis=2)
    return [(whole[:, r], (r, ALL)) for r in range(SLABS)]


def reduce_plain(near, far, x_last=False):
    order = jnp.array([0, 2, 1, 3])
    grad = jnp.stack([near, jnp.concatenate(far)], axis=1)[:, :, order]
    grad = (grad[order] if x_last else grad).reshape(SLABS, 4, -1, 768).astype(fl)
    whole = grad[:, :, :DEPTH].transpose(1, 0, 2, 3).reshape(4, SLABS * DEPTH, 768)
    part = lax.psum_scatter(whole, "tensor", scatter_dimension=0, tiled=True)
    part = lax.psum_scatter(part[0], "dp", scatter_dimension=0, tiled=True)
    if near.shape[2] == DEPTH:
        return part
    extra = lax.psum_scatter(lax.psum(grad[0, :, DEPTH:], "dp"), "tensor", scatter_dimension=0, tiled=True)[0]
    return jnp.concatenate([part, extra])


def next_row(row, gate):
    (row,) = late([rotate(row)], gate)
    return row


def place_rows(rows, where):
    return call(place_kernel, "place_rows", [((4,) + rows[0].shape, rows[0].dtype)], where, *rows)[0]


def moment_update(state, grad):
    moment_one = beta_first * state[1] + (1.0 - beta_first) * grad
    moment_two = beta_second * state[2] + (1.0 - beta_second) * grad * grad
    return jnp.stack([moment_one, moment_two])


def body(
    hidden_in,
    out_grad,
    segment_ids,
    step_count,
    qkv_state,
    qv_bias_state,
    out_state,
    up_state,
    up_bias_state,
    down_state,
    vector_state,
):
    n_dp = lax.axis_size("dp")
    place = lax.axis_index("tensor")
    fast = n_dp == SLABS
    spot = lax.axis_index("dp") if fast else 0
    where = jnp.stack([jnp.int32(spot), (place if fast else 0) * jnp.int32(1)])
    spin = jnp.stack([jnp.int32(0), place * jnp.int32(1)])
    rows, width = qkv_state.shape[1], hidden_in.shape[2]
    cut = 2 * HD

    def spread(value, axis, whole):
        full = jnp.zeros(value.shape[:-1] + (whole,), bf)
        return lax.dynamic_update_slice_in_dim(full, value.astype(bf), axis * value.shape[-1], value.ndim - 1)

    dp = lax.axis_index("dp")
    q, k, v = (qkv_state[0, :, c].astype(bf) for c in range(3))
    o = out_state[0].T.astype(bf)
    attn_shard = jnp.concatenate(
        [q[:, :cut], k[:, :cut], v[:, :cut], q[:, cut:], v[:, cut:], o[:, :cut], k[:, cut:], o[:, cut:]], axis=1
    )
    bq, bv = spread(qv_bias_state[0], dp, HD).reshape(2, 3 * HD)
    gap = jnp.zeros((cut,), bf)
    bias = jnp.concatenate([bq[:cut], gap, bv[:cut], bq[cut:], bv[cut:], gap, gap])
    b_up = spread(up_bias_state[0], dp, LANES).reshape(1, 768)
    extra = jnp.concatenate(
        [spread(vector_state[0], dp, width), bias[None], b_up, jnp.zeros((EXTRA - 8, width), bf)]
    )
    up_shard = up_state[0].astype(bf)
    down_shard = down_state[0].T.astype(bf)

    x = lax.dynamic_index_in_dim(hidden_in, place, 0, keepdims=False)
    dy = lax.dynamic_index_in_dim(out_grad, place, 0, keepdims=False)
    seg = lax.dynamic_index_in_dim(segment_ids, place, 0, keepdims=True)
    seg_col = seg.reshape(-1, 1)
    length = x.shape[0]
    wide = (4, length, 768)
    row_f, row_b = ((length, width), fl), ((length, width), bf)
    whole = ((4, SLABS, DEPTH, 768), bf)
    attn_whole = ((4, SLABS, DEPTH + EXTRA, 768), bf)
    grad_shapes = [((n, 4, DEPTH, 768), bf) for n in (4, 2, 2)]
    attn_grad_shapes = [((n, 4, DEPTH + EXTRA, 768), bf) for n in (4, 2, 2)]
    thin = ((4, 1, 768), fl)

    if fast:
        own = tensor_stack(jnp.concatenate([attn_shard, extra]))
        attn_pieces = gather_direct(own)
        (ffn_shard,) = late([jnp.concatenate([up_shard, down_shard])], own)
        ffn_own = tensor_stack_doubling(ffn_shard)
        wait = [ffn_own]
    else:
        attn_pieces = gather_plain(attn_shard, extra)
        ups, downs = gather_plain(up_shard), gather_plain(down_shard)
        ffn_pieces = [(jnp.concatenate([u, d], axis=1), w) for (u, w), (d, _) in zip(ups, downs)]
        wait = []

    def split(pieces):
        return [p for p, _ in pieces], tuple(w for _, w in pieces)

    pieces, plan = split(attn_pieces)
    proj, ctx, lse, attn_w, xhat, rstd, first, vec, b_up = call(
        functools.partial(attn_fwd_kernel, plan), "attn_fwd",
        [(wide, bf), ((4, length, 256), bf), ((4, 3, 1, length), fl), attn_whole, row_f, ((length, LANES), fl), row_b,
         ((8, width), fl), thin],
        where, x, seg, seg_col, *pieces, after=wait,
    )
    if fast:
        ffn_pieces = gather_staged(ffn_own, vec)
    pieces, plan = split(ffn_pieces)
    out, dr2, act, slope, small_two, up_w, down_w = call(
        functools.partial(ffn_fwd_kernel, plan), "ffn_fwd",
        [row_b, row_f, (wide, bf), (wide, fl), ((3, width), fl), whole, whole],
        where, xhat, first, dy, vec, b_up, *pieces,
    )
    down_near, *down_far = call(
        down_weights_kernel, "down_weights", grad_shapes, where, dr2, act,
    )
    dup, b_up_grad = call(down_bwd_kernel, "down_bwd", [(wide, bf), thin], where, dr2, slope, down_w)
    out_one = next_row(out, b_up_grad)
    wait = [out_one]
    if fast:
        down_half = reduce_core(down_near, down_far, b_up_grad)
        wait += down_half
    dr1, dctx, small_one = call(
        up_bwd_kernel, "up_bwd", [row_f, ((4, length, 256), bf), ((3, width), fl)],
        where, dr2, dup, xhat, rstd, vec, up_w, attn_w, after=wait,
    )
    out_two = next_row(out_one, small_one)
    up_near, *up_far = call(
        up_weights_kernel, "up_weights", grad_shapes, where, first, dup, after=[small_one, out_two],
    )
    wait = [up_near]
    if fast:
        down_pair = reduce_pair(down_half, 1, up_near)
        up_half = reduce_core(up_near, up_far, up_near)
        wait += down_pair + up_half
    grad_row, dproj, bias_grad = call(
        attn_bwd_kernel, "attn_bwd", [row_b, (wide, bf), thin],
        where, seg, seg_col, proj, lse, dr1, dctx, attn_w, after=wait,
        scratch=[pltpu.VMEM((length, width), fl)],
    )
    out_three = next_row(out_two, bias_grad)
    wait = [out_three]
    if fast:
        down_plane = reduce_chip(down_pair, 2, bias_grad)
        wait += down_plane
    attn_near, *attn_far = call(
        attn_weights_kernel, "attn_weights", attn_grad_shapes,
        where, x, dproj, ctx, dr1, bias_grad, b_up_grad, small_one, small_two,
        scratch=[pltpu.VMEM((EXTRA, width), fl)], after=wait,
    )
    in_one = next_row(grad_row, attn_near)
    in_two = rotate(in_one)
    hidden_out = place_rows([out, out_one, out_two, out_three], spin)
    grad_in = place_rows([grad_row, in_one, in_two, rotate(in_two)], spin)
    if fast:
        down_sum = reduce_tensor(down_plane, attn_near)
        up_plane = reduce_chip(reduce_pair(up_half, 2, attn_near), 1, attn_near)
        up_sum = reduce_tensor(up_plane, attn_near)
        attn_plane = reduce_plane(reduce_core(attn_near, attn_far, attn_near, (0, 1, 2)), attn_near)
        attn_sum = reduce_tensor([attn_plane[0]] + late(attn_plane[1:], in_two), attn_near)
    else:
        down_sum = reduce_plain(down_near, down_far, x_last=True)
        up_sum = reduce_plain(up_near, up_far)
        attn_sum = reduce_plain(attn_near, attn_far)

    def own_part(value):
        size = value.shape[-1] // n_dp
        return lax.dynamic_slice_in_dim(value, dp * size, size, value.ndim - 1)

    small = attn_sum[rows:]
    gq = jnp.concatenate([small[6, :cut], small[6, 384 : 384 + HD]])
    gv = jnp.concatenate([small[6, 256 : 256 + cut], small[6, 384 + HD : 512]])
    grad_qv = own_part(jnp.stack([gq, gv]).reshape(2, 3, HD))
    grad_b_up = own_part(small[7].reshape(6, LANES))
    grad_vectors = own_part(small[:6])

    gk = [attn_sum[:rows, 128 * n : 128 * (n + 1)] for n in range(6)]
    grad_qkv = jnp.stack(
        [
            jnp.concatenate([gk[0], gk[3][:, :HD]], axis=1),
            jnp.concatenate([gk[1], gk[5][:, :HD]], axis=1),
            jnp.concatenate([gk[2], gk[3][:, HD:]], axis=1),
        ],
        axis=1,
    )
    grad_out = jnp.concatenate([gk[4], gk[5][:, HD:]], axis=1).T
    summed = (grad_qkv, grad_qv, grad_out, up_sum, grad_b_up, down_sum.T, grad_vectors)
    steps_f = step_count[0].astype(fl)
    factor = jnp.minimum(steps_f / warm_steps, (total_steps - steps_f) / (total_steps - warm_steps))
    fix_first = 1.0 - jnp.exp(steps_f * math.log(beta_first))
    fix_second = 1.0 - jnp.exp(steps_f * math.log(beta_second))
    states = (qkv_state, qv_bias_state, out_state, up_state, up_bias_state, down_state, vector_state)
    news = tuple((moment_update(s, g) for s, g in zip(states, summed)))
    plan_out = jnp.stack([factor, fix_first, fix_second])
    return (hidden_out, grad_in, *summed, *news, plan_out)


def solution(mesh):
    return jax.shard_map(
        body,
        mesh=mesh,
        in_specs=(
            P("dp", None, None),
            P("dp", None, None),
            P("dp", None),
            P(),
            P(None, "dp", None, "tensor"),
            P(None, None, "tensor", "dp"),
            P(None, "tensor", "dp"),
            P(None, "dp", "tensor"),
            P(None, "tensor", "dp"),
            P(None, "tensor", "dp"),
            P(None, None, "dp"),
        ),
        out_specs=(
            P("dp", None, None),
            P("dp", None, None),
            P("dp", None, "tensor"),
            P(None, "tensor", "dp"),
            P("tensor", "dp"),
            P("dp", "tensor"),
            P("tensor", "dp"),
            P("tensor", "dp"),
            P(None, "dp"),
            P(None, "dp", None, "tensor"),
            P(None, None, "tensor", "dp"),
            P(None, "tensor", "dp"),
            P(None, "dp", "tensor"),
            P(None, "tensor", "dp"),
            P(None, "tensor", "dp"),
            P(None, None, "dp"),
            P(),
        ),
        check_vma=False,
    )
```

```python
import functools
import math

import jax
import jax.numpy as jnp
from jax import lax
from jax.experimental import pallas as pl
from jax.experimental.pallas import tpu as pltpu
from jax.sharding import PartitionSpec as P

HD = 64
LANES = 128
VMEM_LIMIT = 60 * 1024 * 1024

norm_eps = 1e-05
beta_first = 0.9
beta_second = 0.999
warm_steps = 10000.0
total_steps = 200000.0

bf = jnp.bfloat16
fl = jnp.float32

SLABS = 8
DEPTH = 96
EXTRA = 16


def nt(left, right):
    return lax.dot_general(left, right, (((1,), (1,)), ((), ())), preferred_element_type=fl)


def nn(left, right):
    return lax.dot_general(left, right, (((1,), (0,)), ((), ())), preferred_element_type=fl)


def tn(left, right):
    return lax.dot_general(left, right, (((0,), (0,)), ((), ())), preferred_element_type=fl)


def low_lanes(shape):
    return lax.broadcasted_iota(jnp.int32, shape, 1) < HD


def assemble(where_ref, pieces, plan, *targets):
    for ref, (r, hops) in zip(pieces, plan):
        slab = jnp.bitwise_xor(where_ref[0], r)
        for k, hop in enumerate(hops):
            group = jnp.bitwise_xor(where_ref[1], hop)
            first = 0
            for target in targets:
                last = first + target.shape[2]
                target[group, slab] = ref[k, first:last]
                first = last


def scatter_slabs(where_ref, group, value, near_ref, far_refs, extra=None, x_last=False):
    hop = jnp.bitwise_xor(group, where_ref[1])
    hop = 2 * jnp.bitwise_and(hop, 1) + jnp.right_shift(hop, 1)
    chip = jnp.right_shift(where_ref[0], 1)
    core = jnp.bitwise_and(where_ref[0], 1)

    def put(near, far):
        for j in range(SLABS // 2):
            place = jnp.bitwise_xor(chip, j)
            if x_last:
                place = 2 * jnp.bitwise_and(place, 1) + jnp.right_shift(place, 1)

            def store(ref, index, slab):
                ref[index, hop, :DEPTH] = value[DEPTH * slab : DEPTH * (slab + 1)]
                if extra is not None:
                    ref[index, hop, DEPTH:] = extra

            store(near_ref, place, 2 * j + near)
            size = 4 // len(far_refs)
            for k, ref in enumerate(far_refs):
                inside = jnp.logical_and(place >= size * k, place < size * (k + 1))
                index = jnp.clip(place - size * k, 0, size - 1)
                pl.when(inside)(functools.partial(store, ref, index, 2 * j + far))

    pl.when(core == 0)(functools.partial(put, 0, 1))
    pl.when(core == 1)(functools.partial(put, 1, 0))


def matrix(ref, group):
    return ref[group][:, :DEPTH].reshape(SLABS * DEPTH, ref.shape[-1])


def out_matrix(ref, group):
    return ref[group][:, :DEPTH, 512:768].reshape(SLABS * DEPTH, 256)


def attn_fwd_kernel(plan, where_ref, x_ref, seg_row_ref, seg_col_ref, *refs):
    pieces = refs[: len(plan)]
    proj_ref, ctx_ref, lse_ref, weight_ref, xhat_ref, rstd_ref, first_ref, vec_ref, b_up_ref = refs[-9:]
    assemble(where_ref, pieces, plan, weight_ref)
    scale = HD ** (-0.5)
    length = x_ref.shape[0]

    def group_step(g, carry):
        small = jnp.sum(weight_ref[g, :, DEPTH:].astype(fl), axis=0)
        vec_ref[...] = small[:8]
        b_up_ref[g] = small[7:8]
        x = x_ref[...]
        proj = (nn(x, matrix(weight_ref, g)) + small[6:7]).astype(bf)
        proj_ref[g] = proj
        same = seg_col_ref[...] == seg_row_ref[...]
        low = low_lanes((length, LANES))
        none = jnp.zeros((length, LANES), bf)
        parts = [proj[:, LANES * k : LANES * (k + 1)] for k in range(6)]
        outs = []
        for head in range(3):
            query = parts[0] if head < 2 else parts[3]
            keys = parts[1] if head < 2 else parts[5]
            value = parts[2] if head < 2 else parts[3]
            query = jnp.where(low, none, query) if head == 1 else jnp.where(low, query, none)
            scores = jnp.where(same, nt(keys, query) * scale, -1e30)
            top = jnp.max(scores, axis=0, keepdims=True)
            expd = jnp.exp(scores - top)
            denom = jnp.sum(expd, axis=0, keepdims=True)
            lse_ref[g, head] = top + jnp.log(denom)
            probs = (expd / denom).astype(bf)
            outs.append(tn(probs, value).astype(bf))
        ctx_ref[g] = jnp.concatenate(
            [jnp.where(low, outs[0], outs[1]), jnp.where(low, none, outs[2])], axis=1
        )
        return carry

    lax.fori_loop(0, 4, group_step, 0)
    total = x_ref[...].astype(fl) + vec_ref[4:5]
    attn = None
    for g in range(4):
        part = nt(ctx_ref[g], out_matrix(weight_ref, g))
        attn = part if attn is None else attn + part
    total = total + attn
    center = total - jnp.mean(total, axis=-1, keepdims=True)
    rstd = lax.rsqrt(jnp.mean(center * center, axis=-1, keepdims=True) + norm_eps)
    xhat = center * rstd
    xhat_ref[...] = xhat
    rstd_ref[...] = jnp.broadcast_to(rstd, rstd_ref.shape)
    first_ref[...] = (xhat * vec_ref[0:1] + vec_ref[1:2]).astype(bf)


def ffn_fwd_kernel(plan, where_ref, xhat_ref, first_ref, dy_ref, vec_ref, b_up_ref, *refs):
    pieces, refs = refs[: len(plan)], refs[len(plan) :]
    out_ref, dr2_ref, act_ref, slope_ref, small_ref, up_w_ref, down_w_ref = refs
    assemble(where_ref, pieces, plan, up_w_ref, down_w_ref)

    def step(g, carry):
        up = nn(first_ref[...], matrix(up_w_ref, g)) + b_up_ref[g]
        half = 0.5 * (1.0 + lax.erf(up * 0.7071067811865476))
        act_ref[g] = (up * half).astype(bf)
        slope_ref[g] = half + up * (jnp.exp(-0.5 * up * up) * 0.3989422804014327)
        return carry

    lax.fori_loop(0, 4, step, 0)
    ffn = None
    for g in range(4):
        part = nt(act_ref[g], matrix(down_w_ref, g))
        ffn = part if ffn is None else ffn + part
    first = xhat_ref[...] * vec_ref[0:1] + vec_ref[1:2]
    total = first + ffn + vec_ref[5:6]
    center = total - jnp.mean(total, axis=-1, keepdims=True)
    rstd = lax.rsqrt(jnp.mean(center * center, axis=-1, keepdims=True) + norm_eps)
    xhat = center * rstd
    out_ref[...] = (xhat * vec_ref[2:3] + vec_ref[3:4]).astype(bf)
    dy = dy_ref[...].astype(fl)
    small_ref[0:1] = jnp.sum(dy * xhat, axis=0, keepdims=True)
    small_ref[1:2] = jnp.sum(dy, axis=0, keepdims=True)
    dxhat = dy * vec_ref[2:3]
    dr2 = rstd * (
        dxhat
        - jnp.mean(dxhat, axis=-1, keepdims=True)
        - xhat * jnp.mean(dxhat * xhat, axis=-1, keepdims=True)
    )
    dr2_ref[...] = dr2
    small_ref[2:3] = jnp.sum(dr2, axis=0, keepdims=True)


def down_weights_kernel(where_ref, dr2_ref, act_ref, near_ref, *far_refs):
    def step(g, carry):
        dffn = dr2_ref[...].astype(bf)
        scatter_slabs(where_ref, g, tn(dffn, act_ref[g]).astype(bf), near_ref, far_refs, x_last=True)
        return carry

    lax.fori_loop(0, 4, step, 0)


def down_bwd_kernel(where_ref, dr2_ref, slope_ref, weight_ref, dup_ref, b_up_ref):
    def step(g, carry):
        dffn = dr2_ref[...].astype(bf)
        dup = (nn(dffn, matrix(weight_ref, g)) * slope_ref[g]).astype(bf)
        dup_ref[g] = dup
        b_up_ref[g] = jnp.sum(dup.astype(fl), axis=0, keepdims=True)
        return carry

    lax.fori_loop(0, 4, step, 0)


def up_weights_kernel(where_ref, first_ref, dup_ref, *refs):
    near_ref, *far_refs = refs

    def step(g, carry):
        scatter_slabs(where_ref, g, tn(first_ref[...], dup_ref[g]).astype(bf), near_ref, far_refs, x_last=True)
        return carry

    lax.fori_loop(0, 4, step, 0)


def up_bwd_kernel(where_ref, dr2_ref, dup_ref, xhat_ref, rstd_ref, vec_ref, weight_ref, attn_weight_ref, *refs):
    dr1_ref, dctx_ref, small_ref = refs[-3:]
    feed = None
    for g in range(4):
        part = nt(dup_ref[g], matrix(weight_ref, g))
        feed = part if feed is None else feed + part
    dfirst = dr2_ref[...] + feed.astype(bf).astype(fl)
    xhat = xhat_ref[...]
    small_ref[0:1] = jnp.sum(dfirst * xhat, axis=0, keepdims=True)
    small_ref[1:2] = jnp.sum(dfirst, axis=0, keepdims=True)
    dxhat = dfirst * vec_ref[0:1]
    dr1 = rstd_ref[:, 0:1] * (
        dxhat
        - jnp.mean(dxhat, axis=-1, keepdims=True)
        - xhat * jnp.mean(dxhat * xhat, axis=-1, keepdims=True)
    )
    dr1_ref[...] = dr1
    small_ref[2:3] = jnp.sum(dr1, axis=0, keepdims=True)
    dattn = dr1.astype(bf)
    for g in range(4):
        dctx_ref[g] = nn(dattn, out_matrix(attn_weight_ref, g)).astype(bf)


def attn_bwd_kernel(where_ref, seg_row_ref, seg_col_ref, proj_ref, lse_ref, dr1_ref, dctx_ref, weight_ref, *refs):
    grad_in_ref, dproj_ref, bias_ref, back_ref = refs[-4:]
    scale = HD ** (-0.5)
    length = dr1_ref.shape[0]
    back_ref[...] = jnp.zeros_like(back_ref)

    def step(g, carry):
        same = seg_col_ref[...] == seg_row_ref[...]
        low = low_lanes((length, LANES))
        none = jnp.zeros((length, LANES), bf)
        parts = [proj_ref[g, :, LANES * k : LANES * (k + 1)] for k in range(6)]
        dctx = [dctx_ref[g, :, :LANES], dctx_ref[g, :, LANES:]]
        dq, dk, dv = [], [], []
        for head in range(3):
            query = parts[0] if head < 2 else parts[3]
            keys = parts[1] if head < 2 else parts[5]
            value = parts[2] if head < 2 else parts[3]
            dout = dctx[0] if head < 2 else dctx[1]
            query_in = jnp.where(low, none, query) if head == 1 else jnp.where(low, query, none)
            dout_in = jnp.where(low, dout, none) if head == 0 else jnp.where(low, none, dout)
            scores = jnp.where(same, nt(keys, query_in) * scale, -1e30)
            probs = jnp.exp(scores - lse_ref[g, head])
            dprobs = nt(value, dout_in)
            dv.append(nn(probs.astype(bf), dout))
            row_dot = jnp.sum(probs * dprobs, axis=0, keepdims=True)
            dscores = (probs * (dprobs - row_dot)).astype(bf)
            dq.append(tn(dscores, keys) * scale)
            dk.append(nn(dscores, query) * scale)
        dproj = jnp.concatenate(
            [
                jnp.where(low, dq[0], dq[1]).astype(bf),
                jnp.where(low, dk[0], dk[1]).astype(bf),
                jnp.where(low, dv[0], dv[1]).astype(bf),
                jnp.where(low, dq[2], dv[2]).astype(bf),
                none,
                jnp.where(low, dk[2].astype(bf), none),
            ],
            axis=1,
        )
        dproj_ref[g] = dproj
        bias_ref[g] = jnp.sum(dproj.astype(fl), axis=0, keepdims=True)
        back_ref[...] += nt(dproj, matrix(weight_ref, g))
        return carry

    lax.fori_loop(0, 4, step, 0)
    dr1 = dr1_ref[...]
    grad_in_ref[...] = (dr1 + back_ref[...].astype(bf).astype(fl)).astype(bf)


def attn_weights_kernel(where_ref, x_ref, dproj_ref, ctx_ref, dr1_ref, bias_ref, b_up_ref, one_ref, two_ref, *refs):
    near_ref, *far_refs, small_ref = refs
    small_ref[...] = jnp.zeros_like(small_ref)
    small_ref[0:2] = one_ref[0:2]
    small_ref[2:4] = two_ref[0:2]
    small_ref[4:5] = one_ref[2:3]
    small_ref[5:6] = two_ref[2:3]

    def grads(g, carry):
        small_ref[6:7] = bias_ref[g]
        small_ref[7:8] = b_up_ref[g]
        main = tn(x_ref[...], dproj_ref[g])
        side = tn(dr1_ref[...].astype(bf), ctx_ref[g])
        whole = jnp.concatenate([main[:, :512], main[:, 512:] + side], axis=1).astype(bf)
        scatter_slabs(where_ref, g, whole, near_ref, far_refs, small_ref[...].astype(bf))
        return carry

    lax.fori_loop(0, 4, grads, 0)


def place_kernel(where_ref, *refs):
    out_ref = refs[-1]
    for d, ref in enumerate(refs[:-1]):
        out_ref[jnp.bitwise_and(where_ref[1] + 4 - d, 3)] = ref[...]


smem = pl.BlockSpec(memory_space=pltpu.SMEM)
vmem = pl.BlockSpec(memory_space=pltpu.VMEM)


def call(kernel, name, outs, where, *args, scratch=(), after=()):
    if after:
        (where,) = late([where], *after)
    return pl.pallas_call(
        kernel,
        name=name,
        out_shape=[jax.ShapeDtypeStruct(s, d) for s, d in outs],
        in_specs=[smem] + [vmem] * len(args),
        out_specs=[vmem] * len(outs),
        scratch_shapes=list(scratch),
        compiler_params=pltpu.CompilerParams(vmem_limit_bytes=VMEM_LIMIT),
        cost_estimate=pl.CostEstimate(flops=COST, bytes_accessed=COST, transcendentals=0),
    )(where, *args)


COST = 1000


def flip(value, bits):
    n = lax.axis_size("dp")
    return lax.ppermute(value, "dp", [(k, k ^ bits) for k in range(n)])


def cross(value, bits):
    return lax.ppermute(value, "tensor", [(k, k ^ bits) for k in range(4)])


def rotate(value):
    return lax.ppermute(value, "tensor", [(k, (k + 1) % 4) for k in range(4)])


def late(values, *gates):
    return list(lax.optimization_barrier((*values, *gates))[: len(values)])


def with_core(near):
    return near + [(flip(a, 1), (r + 1, s)) for a, (r, s) in near]


ALL = (0, 1, 2, 3)


def tensor_stack(shard):
    return jnp.stack([shard] + [cross(shard, hop) for hop in (1, 2, 3)])


def gather_staged(own, gates=()):
    over_x = flip(own, 2)
    over_y = flip(own, 4)
    half_x, half_y = late([over_x[:2], over_y[2:]], *gates)
    far_a = flip(half_x, 4)
    far_b = flip(half_y, 2)
    near = [(own, (0, ALL)), (over_x, (2, ALL)), (over_y, (4, ALL))]
    return with_core(near + [(far_a, (6, (0, 1))), (far_b, (6, (2, 3)))])


def add(*values):
    total = values[0].astype(fl)
    for value in values[1:]:
        total = total + value.astype(fl)
    return total


def reduce_core(near, far, gates=(), parts=1):
    got = late([flip(part, 1) for part in far], *gates) if gates else [flip(part, 1) for part in far]
    size, each = 4 // len(far), len(far) * parts
    return [
        add(near[a : a + 4 // each], got[a // size][a % size : a % size + 4 // each]).astype(bf)
        for a in range(0, 4, 4 // each)
    ]


def halves(parts):
    return [jnp.concatenate(parts[:2]), jnp.concatenate(parts[2:])]


def reduce_pair(half, axis, gates=()):
    got = flip(half[1], 2 * axis)
    if gates:
        (got,) = late([got], *gates)
    return [add(half[0][k], got[k]).astype(bf) for k in (0, 1)]


def reduce_chip(pair, axis, gates=()):
    got = flip(pair[1], 2 * axis)
    if gates:
        (got,) = late([got], *gates)
    return [add(pair[0][k : k + 2], got[k : k + 2]).astype(bf) for k in (0, 2)]


def reduce_tensor(plane):
    got = cross(plane[1], 1)
    near, far = add(plane[0][0], got[0]), add(plane[0][1], got[1]).astype(bf)
    return add(near, cross(far, 2))


def gather_plain(shard, extra=None):
    whole = lax.all_gather(lax.all_gather(shard, "dp", axis=0, tiled=True), "tensor", axis=0)
    whole = whole.reshape(4, SLABS, -1, 768)
    if extra is not None:
        extra = lax.all_gather(lax.psum(extra, "dp"), "tensor", axis=0)[:, None].astype(bf)
        extra = jnp.concatenate([extra] + [jnp.zeros_like(extra)] * (SLABS - 1), axis=1)
        whole = jnp.concatenate([whole, extra], axis=2)
    return [(whole[:, r], (r, ALL)) for r in range(SLABS)]


def reduce_plain(near, far, x_last=False):
    order = jnp.array([0, 2, 1, 3])
    grad = jnp.stack([near, jnp.concatenate(far)], axis=1)[:, :, order]
    grad = (grad[order] if x_last else grad).reshape(SLABS, 4, -1, 768).astype(fl)
    whole = grad[:, :, :DEPTH].transpose(1, 0, 2, 3).reshape(4, SLABS * DEPTH, 768)
    part = lax.psum_scatter(whole, "tensor", scatter_dimension=0, tiled=True)
    part = lax.psum_scatter(part[0], "dp", scatter_dimension=0, tiled=True)
    if near.shape[2] == DEPTH:
        return part
    extra = lax.psum_scatter(lax.psum(grad[0, :, DEPTH:], "dp"), "tensor", scatter_dimension=0, tiled=True)[0]
    return jnp.concatenate([part, extra])


def next_row(row, gate):
    (row,) = late([rotate(row)], gate)
    return row


def place_rows(rows, where):
    return call(place_kernel, "place_rows", [((4,) + rows[0].shape, rows[0].dtype)], where, *rows)[0]


def moment_update(state, grad):
    moment_one = beta_first * state[1] + (1.0 - beta_first) * grad
    moment_two = beta_second * state[2] + (1.0 - beta_second) * grad * grad
    return jnp.stack([moment_one, moment_two])


def body(
    hidden_in,
    out_grad,
    segment_ids,
    step_count,
    qkv_state,
    qv_bias_state,
    out_state,
    up_state,
    up_bias_state,
    down_state,
    vector_state,
):
    n_dp = lax.axis_size("dp")
    place = lax.axis_index("tensor")
    fast = n_dp == SLABS
    spot = lax.axis_index("dp") if fast else 0
    where = jnp.stack([jnp.int32(spot), (place if fast else 0) * jnp.int32(1)])
    spin = jnp.stack([jnp.int32(0), place * jnp.int32(1)])
    rows, width = qkv_state.shape[1], hidden_in.shape[2]
    cut = 2 * HD

    def spread(value, axis, whole):
        full = jnp.zeros(value.shape[:-1] + (whole,), bf)
        return lax.dynamic_update_slice_in_dim(full, value.astype(bf), axis * value.shape[-1], value.ndim - 1)

    dp = lax.axis_index("dp")
    q, k, v = (qkv_state[0, :, c].astype(bf) for c in range(3))
    o = out_state[0].T.astype(bf)
    attn_shard = jnp.concatenate(
        [q[:, :cut], k[:, :cut], v[:, :cut], q[:, cut:], v[:, cut:], o[:, :cut], k[:, cut:], o[:, cut:]], axis=1
    )
    bq, bv = spread(qv_bias_state[0], dp, HD).reshape(2, 3 * HD)
    gap = jnp.zeros((cut,), bf)
    bias = jnp.concatenate([bq[:cut], gap, bv[:cut], bq[cut:], bv[cut:], gap, gap])
    b_up = spread(up_bias_state[0], dp, LANES).reshape(1, 768)
    extra = jnp.concatenate(
        [spread(vector_state[0], dp, width), bias[None], b_up, jnp.zeros((EXTRA - 8, width), bf)]
    )
    up_shard = up_state[0].astype(bf)
    down_shard = down_state[0].T.astype(bf)

    x = lax.dynamic_index_in_dim(hidden_in, place, 0, keepdims=False)
    dy = lax.dynamic_index_in_dim(out_grad, place, 0, keepdims=False)
    seg = lax.dynamic_index_in_dim(segment_ids, place, 0, keepdims=True)
    seg_col = seg.reshape(-1, 1)
    length = x.shape[0]
    wide = (4, length, 768)
    row_f, row_b = ((length, width), fl), ((length, width), bf)
    whole = ((4, SLABS, DEPTH, 768), bf)
    attn_whole = ((4, SLABS, DEPTH + EXTRA, 768), bf)
    down_shapes = [((n, 4, DEPTH, 768), bf) for n in (4, 1, 1, 1, 1)]
    up_shapes = [((n, 4, DEPTH, 768), bf) for n in (4, 4)]
    attn_shapes = [((n, 4, DEPTH + EXTRA, 768), bf) for n in (4, 1, 1, 1, 1)]
    thin = ((4, 1, 768), fl)

    if fast:
        own = tensor_stack(jnp.concatenate([attn_shard, extra]))
        attn_pieces = gather_staged(own)
        (ffn_shard,) = late([jnp.concatenate([up_shard, down_shard])], own)
        ffn_own = tensor_stack(ffn_shard)
        wait = [ffn_own]
    else:
        attn_pieces = gather_plain(attn_shard, extra)
        ups, downs = gather_plain(up_shard), gather_plain(down_shard)
        ffn_pieces = [(jnp.concatenate([u, d], axis=1), w) for (u, w), (d, _) in zip(ups, downs)]
        wait = []

    def split(pieces):
        return [p for p, _ in pieces], tuple(w for _, w in pieces)

    pieces, plan = split(attn_pieces)
    proj, ctx, lse, attn_w, xhat, rstd, first, vec, b_up = call(
        functools.partial(attn_fwd_kernel, plan), "attn_fwd",
        [(wide, bf), ((4, length, 256), bf), ((4, 3, 1, length), fl), attn_whole, row_f, ((length, LANES), fl), row_b,
         ((8, width), fl), thin],
        where, x, seg, seg_col, *pieces, after=wait,
    )
    if fast:
        ffn_pieces = gather_staged(ffn_own, [vec])
    pieces, plan = split(ffn_pieces)
    out, dr2, act, slope, small_two, up_w, down_w = call(
        functools.partial(ffn_fwd_kernel, plan), "ffn_fwd",
        [row_b, row_f, (wide, bf), (wide, fl), ((3, width), fl), whole, whole],
        where, xhat, first, dy, vec, b_up, *pieces,
    )
    down_near, *down_far = call(
        down_weights_kernel, "down_weights", down_shapes, where, dr2, act,
    )
    dup, b_up_grad = call(down_bwd_kernel, "down_bwd", [(wide, bf), thin], where, dr2, slope, down_w)
    out_one = next_row(out, b_up_grad)
    wait = [out_one]
    if fast:
        down_half = halves(reduce_core(down_near, down_far, [b_up_grad, out_one]))
        wait += down_half
    dr1, dctx, small_one = call(
        up_bwd_kernel, "up_bwd", [row_f, ((4, length, 256), bf), ((3, width), fl)],
        where, dr2, dup, xhat, rstd, vec, up_w, attn_w, after=wait,
    )
    out_two = next_row(out_one, small_one)
    grad_row, dproj, bias_grad = call(
        attn_bwd_kernel, "attn_bwd", [row_b, (wide, bf), thin],
        where, seg, seg_col, proj, lse, dr1, dctx, attn_w, after=[out_two],
        scratch=[pltpu.VMEM((length, width), fl)],
    )
    out_three = next_row(out_two, bias_grad)
    wait = [out_three]
    if fast:
        down_pair = reduce_pair(down_half, 1, [bias_grad])
        wait += down_pair
    attn_near, *attn_far = call(
        attn_weights_kernel, "attn_weights", attn_shapes,
        where, x, dproj, ctx, dr1, bias_grad, b_up_grad, small_one, small_two,
        scratch=[pltpu.VMEM((EXTRA, width), fl)], after=wait,
    )
    up_near, *up_far = call(
        up_weights_kernel, "up_weights", up_shapes, where, first, dup, after=[bias_grad, attn_near],
    )
    in_one = rotate(grad_row)
    in_two = rotate(in_one)
    in_three = rotate(in_two)
    hidden_out = place_rows([out, out_one, out_two, out_three], spin)
    grad_in = place_rows([grad_row, in_one, in_two, in_three], spin)
    if fast:
        attn_half = halves(reduce_core(attn_near, attn_far, [up_near, in_one]))
        up_far = late(up_far, in_one, *attn_half)
        down_sum = reduce_tensor(reduce_chip([down_pair[0]] + late(down_pair[1:], in_one), 2))
        up_pair = reduce_pair(reduce_core(up_near, up_far, parts=2), 1, [in_two])
        up_plane = reduce_chip(up_pair, 2)
        attn_plane = reduce_chip(reduce_pair(attn_half, 2), 1, [in_three])
        attn_sum = reduce_tensor([attn_plane[0]] + late(attn_plane[1:], *up_plane))
        up_sum = reduce_tensor(up_plane)
    else:
        down_sum = reduce_plain(down_near, down_far, x_last=True)
        up_sum = reduce_plain(up_near, up_far, x_last=True)
        attn_sum = reduce_plain(attn_near, attn_far)

    def own_part(value):
        size = value.shape[-1] // n_dp
        return lax.dynamic_slice_in_dim(value, dp * size, size, value.ndim - 1)

    small = attn_sum[rows:]
    gq = jnp.concatenate([small[6, :cut], small[6, 384 : 384 + HD]])
    gv = jnp.concatenate([small[6, 256 : 256 + cut], small[6, 384 + HD : 512]])
    grad_qv = own_part(jnp.stack([gq, gv]).reshape(2, 3, HD))
    grad_b_up = own_part(small[7].reshape(6, LANES))
    grad_vectors = own_part(small[:6])

    gk = [attn_sum[:rows, 128 * n : 128 * (n + 1)] for n in range(6)]
    grad_qkv = jnp.stack(
        [
            jnp.concatenate([gk[0], gk[3][:, :HD]], axis=1),
            jnp.concatenate([gk[1], gk[5][:, :HD]], axis=1),
            jnp.concatenate([gk[2], gk[3][:, HD:]], axis=1),
        ],
        axis=1,
    )
    grad_out = jnp.concatenate([gk[4], gk[5][:, HD:]], axis=1).T
    summed = (grad_qkv, grad_qv, grad_out, up_sum, grad_b_up, down_sum.T, grad_vectors)
    steps_f = step_count[0].astype(fl)
    factor = jnp.minimum(steps_f / warm_steps, (total_steps - steps_f) / (total_steps - warm_steps))
    fix_first = 1.0 - jnp.exp(steps_f * math.log(beta_first))
    fix_second = 1.0 - jnp.exp(steps_f * math.log(beta_second))
    states = (qkv_state, qv_bias_state, out_state, up_state, up_bias_state, down_state, vector_state)
    news = tuple((moment_update(s, g) for s, g in zip(states, summed)))
    plan_out = jnp.stack([factor, fix_first, fix_second])
    return (hidden_out, grad_in, *summed, *news, plan_out)


def solution(mesh):
    return jax.shard_map(
        body,
        mesh=mesh,
        in_specs=(
            P("dp", None, None),
            P("dp", None, None),
            P("dp", None),
            P(),
            P(None, "dp", None, "tensor"),
            P(None, None, "tensor", "dp"),
            P(None, "tensor", "dp"),
            P(None, "dp", "tensor"),
            P(None, "tensor", "dp"),
            P(None, "tensor", "dp"),
            P(None, None, "dp"),
        ),
        out_specs=(
            P("dp", None, None),
            P("dp", None, None),
            P("dp", None, "tensor"),
            P(None, "tensor", "dp"),
            P("tensor", "dp"),
            P("dp", "tensor"),
            P("tensor", "dp"),
            P("tensor", "dp"),
            P(None, "dp"),
            P(None, "dp", None, "tensor"),
            P(None, None, "tensor", "dp"),
            P(None, "tensor", "dp"),
            P(None, "dp", "tensor"),
            P(None, "tensor", "dp"),
            P(None, "tensor", "dp"),
            P(None, None, "dp"),
            P(),
        ),
        check_vma=False,
    )
```

```python
import functools
import math

import jax
import jax.numpy as jnp
from jax import lax
from jax.experimental import pallas as pl
from jax.experimental.pallas import tpu as pltpu
from jax.sharding import PartitionSpec as P

HD = 64
LANES = 128
VMEM_LIMIT = 60 * 1024 * 1024

norm_eps = 1e-05
beta_first = 0.9
beta_second = 0.999
warm_steps = 10000.0
total_steps = 200000.0

bf = jnp.bfloat16
fl = jnp.float32

SLABS = 8
DEPTH = 96
EXTRA = 16


def nt(left, right):
    return lax.dot_general(left, right, (((1,), (1,)), ((), ())), preferred_element_type=fl)


def nn(left, right):
    return lax.dot_general(left, right, (((1,), (0,)), ((), ())), preferred_element_type=fl)


def tn(left, right):
    return lax.dot_general(left, right, (((0,), (0,)), ((), ())), preferred_element_type=fl)


def low_lanes(shape):
    return lax.broadcasted_iota(jnp.int32, shape, 1) < HD


def assemble(where_ref, pieces, plan, *targets):
    for ref, (r, hops) in zip(pieces, plan):
        slab = jnp.bitwise_xor(where_ref[0], r)
        for k, hop in enumerate(hops):
            group = jnp.bitwise_xor(where_ref[1], hop)
            first = 0
            for target in targets:
                last = first + target.shape[2]
                target[group, slab] = ref[k, first:last]
                first = last


def scatter_slabs(where_ref, group, value, near_ref, far_refs, extra=None, x_last=False):
    hop = jnp.bitwise_xor(group, where_ref[1])
    hop = 2 * jnp.bitwise_and(hop, 1) + jnp.right_shift(hop, 1)
    chip = jnp.right_shift(where_ref[0], 1)
    core = jnp.bitwise_and(where_ref[0], 1)

    def put(near, far):
        for j in range(SLABS // 2):
            place = jnp.bitwise_xor(chip, j)
            if x_last:
                place = 2 * jnp.bitwise_and(place, 1) + jnp.right_shift(place, 1)

            def store(ref, index, slab):
                ref[index, hop, :DEPTH] = value[DEPTH * slab : DEPTH * (slab + 1)]
                if extra is not None:
                    ref[index, hop, DEPTH:] = extra

            store(near_ref, place, 2 * j + near)
            size = 4 // len(far_refs)
            for k, ref in enumerate(far_refs):
                inside = jnp.logical_and(place >= size * k, place < size * (k + 1))
                index = jnp.clip(place - size * k, 0, size - 1)
                pl.when(inside)(functools.partial(store, ref, index, 2 * j + far))

    pl.when(core == 0)(functools.partial(put, 0, 1))
    pl.when(core == 1)(functools.partial(put, 1, 0))


def matrix(ref, group):
    return ref[group][:, :DEPTH].reshape(SLABS * DEPTH, ref.shape[-1])


def out_matrix(ref, group):
    return ref[group][:, :DEPTH, 512:768].reshape(SLABS * DEPTH, 256)


def attn_fwd_kernel(plan, where_ref, x_ref, seg_row_ref, seg_col_ref, *refs):
    pieces = refs[: len(plan)]
    proj_ref, ctx_ref, lse_ref, weight_ref, xhat_ref, rstd_ref, first_ref, vec_ref, b_up_ref = refs[-9:]
    assemble(where_ref, pieces, plan, weight_ref)
    scale = HD ** (-0.5)
    length = x_ref.shape[0]

    def group_step(g, carry):
        small = jnp.sum(weight_ref[g, :, DEPTH:].astype(fl), axis=0)
        vec_ref[...] = small[:8]
        b_up_ref[g] = small[7:8]
        x = x_ref[...]
        proj = (nn(x, matrix(weight_ref, g)) + small[6:7]).astype(bf)
        proj_ref[g] = proj
        same = seg_col_ref[...] == seg_row_ref[...]
        low = low_lanes((length, LANES))
        none = jnp.zeros((length, LANES), bf)
        parts = [proj[:, LANES * k : LANES * (k + 1)] for k in range(6)]
        outs = []
        for head in range(3):
            query = parts[0] if head < 2 else parts[3]
            keys = parts[1] if head < 2 else parts[5]
            value = parts[2] if head < 2 else parts[3]
            query = jnp.where(low, none, query) if head == 1 else jnp.where(low, query, none)
            scores = jnp.where(same, nt(keys, query) * scale, -1e30)
            top = jnp.max(scores, axis=0, keepdims=True)
            expd = jnp.exp(scores - top)
            denom = jnp.sum(expd, axis=0, keepdims=True)
            lse_ref[g, head] = top + jnp.log(denom)
            probs = (expd / denom).astype(bf)
            outs.append(tn(probs, value).astype(bf))
        ctx_ref[g] = jnp.concatenate(
            [jnp.where(low, outs[0], outs[1]), jnp.where(low, none, outs[2])], axis=1
        )
        return carry

    lax.fori_loop(0, 4, group_step, 0)
    total = x_ref[...].astype(fl) + vec_ref[4:5]
    attn = None
    for g in range(4):
        part = nt(ctx_ref[g], out_matrix(weight_ref, g))
        attn = part if attn is None else attn + part
    total = total + attn
    center = total - jnp.mean(total, axis=-1, keepdims=True)
    rstd = lax.rsqrt(jnp.mean(center * center, axis=-1, keepdims=True) + norm_eps)
    xhat = center * rstd
    xhat_ref[...] = xhat
    rstd_ref[...] = jnp.broadcast_to(rstd, rstd_ref.shape)
    first_ref[...] = (xhat * vec_ref[0:1] + vec_ref[1:2]).astype(bf)


def ffn_fwd_kernel(plan, where_ref, xhat_ref, first_ref, dy_ref, vec_ref, b_up_ref, *refs):
    pieces, refs = refs[: len(plan)], refs[len(plan) :]
    out_ref, dr2_ref, act_ref, slope_ref, small_ref, up_w_ref, down_w_ref = refs
    assemble(where_ref, pieces, plan, up_w_ref, down_w_ref)

    def step(g, carry):
        up = nn(first_ref[...], matrix(up_w_ref, g)) + b_up_ref[g]
        half = 0.5 * (1.0 + lax.erf(up * 0.7071067811865476))
        act_ref[g] = (up * half).astype(bf)
        slope_ref[g] = half + up * (jnp.exp(-0.5 * up * up) * 0.3989422804014327)
        return carry

    lax.fori_loop(0, 4, step, 0)
    ffn = None
    for g in range(4):
        part = nt(act_ref[g], matrix(down_w_ref, g))
        ffn = part if ffn is None else ffn + part
    first = xhat_ref[...] * vec_ref[0:1] + vec_ref[1:2]
    total = first + ffn + vec_ref[5:6]
    center = total - jnp.mean(total, axis=-1, keepdims=True)
    rstd = lax.rsqrt(jnp.mean(center * center, axis=-1, keepdims=True) + norm_eps)
    xhat = center * rstd
    out_ref[...] = (xhat * vec_ref[2:3] + vec_ref[3:4]).astype(bf)
    dy = dy_ref[...].astype(fl)
    small_ref[0:1] = jnp.sum(dy * xhat, axis=0, keepdims=True)
    small_ref[1:2] = jnp.sum(dy, axis=0, keepdims=True)
    dxhat = dy * vec_ref[2:3]
    dr2 = rstd * (
        dxhat
        - jnp.mean(dxhat, axis=-1, keepdims=True)
        - xhat * jnp.mean(dxhat * xhat, axis=-1, keepdims=True)
    )
    dr2_ref[...] = dr2
    small_ref[2:3] = jnp.sum(dr2, axis=0, keepdims=True)


def down_weights_kernel(where_ref, dr2_ref, act_ref, near_ref, *far_refs):
    def step(g, carry):
        dffn = dr2_ref[...].astype(bf)
        scatter_slabs(where_ref, g, tn(dffn, act_ref[g]).astype(bf), near_ref, far_refs, x_last=True)
        return carry

    lax.fori_loop(0, 4, step, 0)


def down_bwd_kernel(where_ref, dr2_ref, slope_ref, weight_ref, dup_ref, b_up_ref):
    def step(g, carry):
        dffn = dr2_ref[...].astype(bf)
        dup = (nn(dffn, matrix(weight_ref, g)) * slope_ref[g]).astype(bf)
        dup_ref[g] = dup
        b_up_ref[g] = jnp.sum(dup.astype(fl), axis=0, keepdims=True)
        return carry

    lax.fori_loop(0, 4, step, 0)


def up_weights_kernel(where_ref, first_ref, dup_ref, *refs):
    near_ref, *far_refs = refs

    def step(g, carry):
        scatter_slabs(where_ref, g, tn(first_ref[...], dup_ref[g]).astype(bf), near_ref, far_refs, x_last=True)
        return carry

    lax.fori_loop(0, 4, step, 0)


def up_bwd_kernel(where_ref, dr2_ref, dup_ref, xhat_ref, rstd_ref, vec_ref, weight_ref, attn_weight_ref, *refs):
    dr1_ref, dctx_ref, small_ref = refs[-3:]
    feed = None
    for g in range(4):
        part = nt(dup_ref[g], matrix(weight_ref, g))
        feed = part if feed is None else feed + part
    dfirst = dr2_ref[...] + feed.astype(bf).astype(fl)
    xhat = xhat_ref[...]
    small_ref[0:1] = jnp.sum(dfirst * xhat, axis=0, keepdims=True)
    small_ref[1:2] = jnp.sum(dfirst, axis=0, keepdims=True)
    dxhat = dfirst * vec_ref[0:1]
    dr1 = rstd_ref[:, 0:1] * (
        dxhat
        - jnp.mean(dxhat, axis=-1, keepdims=True)
        - xhat * jnp.mean(dxhat * xhat, axis=-1, keepdims=True)
    )
    dr1_ref[...] = dr1
    small_ref[2:3] = jnp.sum(dr1, axis=0, keepdims=True)
    dattn = dr1.astype(bf)
    for g in range(4):
        dctx_ref[g] = nn(dattn, out_matrix(attn_weight_ref, g)).astype(bf)


def attn_bwd_kernel(where_ref, seg_row_ref, seg_col_ref, proj_ref, lse_ref, dr1_ref, dctx_ref, weight_ref, *refs):
    grad_in_ref, dproj_ref, bias_ref, back_ref = refs[-4:]
    scale = HD ** (-0.5)
    length = dr1_ref.shape[0]
    back_ref[...] = jnp.zeros_like(back_ref)

    def step(g, carry):
        same = seg_col_ref[...] == seg_row_ref[...]
        low = low_lanes((length, LANES))
        none = jnp.zeros((length, LANES), bf)
        parts = [proj_ref[g, :, LANES * k : LANES * (k + 1)] for k in range(6)]
        dctx = [dctx_ref[g, :, :LANES], dctx_ref[g, :, LANES:]]
        dq, dk, dv = [], [], []
        for head in range(3):
            query = parts[0] if head < 2 else parts[3]
            keys = parts[1] if head < 2 else parts[5]
            value = parts[2] if head < 2 else parts[3]
            dout = dctx[0] if head < 2 else dctx[1]
            query_in = jnp.where(low, none, query) if head == 1 else jnp.where(low, query, none)
            dout_in = jnp.where(low, dout, none) if head == 0 else jnp.where(low, none, dout)
            scores = jnp.where(same, nt(keys, query_in) * scale, -1e30)
            probs = jnp.exp(scores - lse_ref[g, head])
            dprobs = nt(value, dout_in)
            dv.append(nn(probs.astype(bf), dout))
            row_dot = jnp.sum(probs * dprobs, axis=0, keepdims=True)
            dscores = (probs * (dprobs - row_dot)).astype(bf)
            dq.append(tn(dscores, keys) * scale)
            dk.append(nn(dscores, query) * scale)
        dproj = jnp.concatenate(
            [
                jnp.where(low, dq[0], dq[1]).astype(bf),
                jnp.where(low, dk[0], dk[1]).astype(bf),
                jnp.where(low, dv[0], dv[1]).astype(bf),
                jnp.where(low, dq[2], dv[2]).astype(bf),
                none,
                jnp.where(low, dk[2].astype(bf), none),
            ],
            axis=1,
        )
        dproj_ref[g] = dproj
        bias_ref[g] = jnp.sum(dproj.astype(fl), axis=0, keepdims=True)
        back_ref[...] += nt(dproj, matrix(weight_ref, g))
        return carry

    lax.fori_loop(0, 4, step, 0)
    dr1 = dr1_ref[...]
    grad_in_ref[...] = (dr1 + back_ref[...].astype(bf).astype(fl)).astype(bf)


def attn_weights_kernel(where_ref, x_ref, dproj_ref, ctx_ref, dr1_ref, bias_ref, b_up_ref, one_ref, two_ref, *refs):
    near_ref, *far_refs, small_ref = refs
    small_ref[...] = jnp.zeros_like(small_ref)
    small_ref[0:2] = one_ref[0:2]
    small_ref[2:4] = two_ref[0:2]
    small_ref[4:5] = one_ref[2:3]
    small_ref[5:6] = two_ref[2:3]

    def grads(g, carry):
        small_ref[6:7] = bias_ref[g]
        small_ref[7:8] = b_up_ref[g]
        main = tn(x_ref[...], dproj_ref[g])
        side = tn(dr1_ref[...].astype(bf), ctx_ref[g])
        whole = jnp.concatenate([main[:, :512], main[:, 512:] + side], axis=1).astype(bf)
        scatter_slabs(where_ref, g, whole, near_ref, far_refs, small_ref[...].astype(bf))
        return carry

    lax.fori_loop(0, 4, grads, 0)


def place_kernel(where_ref, *refs):
    out_ref = refs[-1]
    for d, ref in enumerate(refs[:-1]):
        out_ref[jnp.bitwise_and(where_ref[1] + 4 - d, 3)] = ref[...]


smem = pl.BlockSpec(memory_space=pltpu.SMEM)
vmem = pl.BlockSpec(memory_space=pltpu.VMEM)


def call(kernel, name, outs, where, *args, scratch=(), after=()):
    if after:
        (where,) = late([where], *after)
    return pl.pallas_call(
        kernel,
        name=name,
        out_shape=[jax.ShapeDtypeStruct(s, d) for s, d in outs],
        in_specs=[smem] + [vmem] * len(args),
        out_specs=[vmem] * len(outs),
        scratch_shapes=list(scratch),
        compiler_params=pltpu.CompilerParams(vmem_limit_bytes=VMEM_LIMIT),
        cost_estimate=pl.CostEstimate(flops=COST, bytes_accessed=COST, transcendentals=0),
    )(where, *args)


COST = 1000


def flip(value, bits):
    n = lax.axis_size("dp")
    return lax.ppermute(value, "dp", [(k, k ^ bits) for k in range(n)])


def cross(value, bits):
    return lax.ppermute(value, "tensor", [(k, k ^ bits) for k in range(4)])


def rotate(value):
    return lax.ppermute(value, "tensor", [(k, (k + 1) % 4) for k in range(4)])


def late(values, *gates):
    return list(lax.optimization_barrier((*values, *gates))[: len(values)])


def with_core(near):
    return near + [(flip(a, 1), (r + 1, s)) for a, (r, s) in near]


ALL = (0, 1, 2, 3)


def over_tensor(shard):
    return [shard] + [cross(shard, hop) for hop in (1, 2, 3)]


def gather_staged(own, gates=()):
    over_x = flip(own, 2)
    over_y = flip(own, 4)
    half_x, half_y = late([over_x[:2], over_y[2:]], *gates)
    far_a = flip(half_x, 4)
    far_b = flip(half_y, 2)
    near = [(own, (0, ALL)), (over_x, (2, ALL)), (over_y, (4, ALL))]
    return with_core(near + [(far_a, (6, (0, 1))), (far_b, (6, (2, 3)))])


def add(*values):
    total = values[0].astype(fl)
    for value in values[1:]:
        total = total + value.astype(fl)
    return total


def reduce_core(near, far, gates=(), parts=1):
    got = late([flip(part, 1) for part in far], *gates) if gates else [flip(part, 1) for part in far]
    size, each = 4 // len(far), len(far) * parts
    return [
        add(near[a : a + 4 // each], got[a // size][a % size : a % size + 4 // each]).astype(bf)
        for a in range(0, 4, 4 // each)
    ]


def halves(parts):
    return [jnp.concatenate(parts[:2]), jnp.concatenate(parts[2:])]


def reduce_pair(half, axis, gates=()):
    got = flip(half[1], 2 * axis)
    if gates:
        (got,) = late([got], *gates)
    return [add(half[0][k], got[k]).astype(bf) for k in (0, 1)]


def reduce_chip(pair, axis, gates=()):
    got = flip(pair[1], 2 * axis)
    if gates:
        (got,) = late([got], *gates)
    return [add(pair[0][k : k + 2], got[k : k + 2]).astype(bf) for k in (0, 2)]


def reduce_tensor(plane):
    got = cross(plane[1], 1)
    near, far = add(plane[0][0], got[0]), add(plane[0][1], got[1]).astype(bf)
    return add(near, cross(far, 2))


def gather_plain(shard, extra=None):
    whole = lax.all_gather(lax.all_gather(shard, "dp", axis=0, tiled=True), "tensor", axis=0)
    whole = whole.reshape(4, SLABS, -1, 768)
    if extra is not None:
        extra = lax.all_gather(lax.psum(extra, "dp"), "tensor", axis=0)[:, None].astype(bf)
        extra = jnp.concatenate([extra] + [jnp.zeros_like(extra)] * (SLABS - 1), axis=1)
        whole = jnp.concatenate([whole, extra], axis=2)
    return [(whole[:, r], (r, ALL)) for r in range(SLABS)]


def reduce_plain(near, far, x_last=False):
    order = jnp.array([0, 2, 1, 3])
    grad = jnp.stack([near, jnp.concatenate(far)], axis=1)[:, :, order]
    grad = (grad[order] if x_last else grad).reshape(SLABS, 4, -1, 768).astype(fl)
    whole = grad[:, :, :DEPTH].transpose(1, 0, 2, 3).reshape(4, SLABS * DEPTH, 768)
    part = lax.psum_scatter(whole, "tensor", scatter_dimension=0, tiled=True)
    part = lax.psum_scatter(part[0], "dp", scatter_dimension=0, tiled=True)
    if near.shape[2] == DEPTH:
        return part
    extra = lax.psum_scatter(lax.psum(grad[0, :, DEPTH:], "dp"), "tensor", scatter_dimension=0, tiled=True)[0]
    return jnp.concatenate([part, extra])


def next_row(row, gate):
    (row,) = late([rotate(row)], gate)
    return row


def place_rows(rows, where):
    return call(place_kernel, "place_rows", [((4,) + rows[0].shape, rows[0].dtype)], where, *rows)[0]


def moment_update(state, grad):
    moment_one = beta_first * state[1] + (1.0 - beta_first) * grad
    moment_two = beta_second * state[2] + (1.0 - beta_second) * grad * grad
    return jnp.stack([moment_one, moment_two])


def body(
    hidden_in,
    out_grad,
    segment_ids,
    step_count,
    qkv_state,
    qv_bias_state,
    out_state,
    up_state,
    up_bias_state,
    down_state,
    vector_state,
):
    n_dp = lax.axis_size("dp")
    place = lax.axis_index("tensor")
    fast = n_dp == SLABS
    spot = lax.axis_index("dp") if fast else 0
    where = jnp.stack([jnp.int32(spot), (place if fast else 0) * jnp.int32(1)])
    spin = jnp.stack([jnp.int32(0), place * jnp.int32(1)])
    rows, width = qkv_state.shape[1], hidden_in.shape[2]
    cut = 2 * HD

    def spread(value, axis, whole):
        full = jnp.zeros(value.shape[:-1] + (whole,), bf)
        return lax.dynamic_update_slice_in_dim(full, value.astype(bf), axis * value.shape[-1], value.ndim - 1)

    dp = lax.axis_index("dp")
    q, k, v = (qkv_state[0, :, c].astype(bf) for c in range(3))
    o = out_state[0].T.astype(bf)
    attn_shard = jnp.concatenate(
        [q[:, :cut], k[:, :cut], v[:, :cut], q[:, cut:], v[:, cut:], o[:, :cut], k[:, cut:], o[:, cut:]], axis=1
    )
    bq, bv = spread(qv_bias_state[0], dp, HD).reshape(2, 3 * HD)
    gap = jnp.zeros((cut,), bf)
    bias = jnp.concatenate([bq[:cut], gap, bv[:cut], bq[cut:], bv[cut:], gap, gap])
    b_up = spread(up_bias_state[0], dp, LANES).reshape(1, 768)
    extra = jnp.concatenate(
        [spread(vector_state[0], dp, width), bias[None], b_up, jnp.zeros((EXTRA - 8, width), bf)]
    )
    up_shard = up_state[0].astype(bf)
    down_shard = down_state[0].T.astype(bf)

    x = lax.dynamic_index_in_dim(hidden_in, place, 0, keepdims=False)
    dy = lax.dynamic_index_in_dim(out_grad, place, 0, keepdims=False)
    seg = lax.dynamic_index_in_dim(segment_ids, place, 0, keepdims=True)
    seg_col = seg.reshape(-1, 1)
    length = x.shape[0]
    wide = (4, length, 768)
    row_f, row_b = ((length, width), fl), ((length, width), bf)
    whole = ((4, SLABS, DEPTH, 768), bf)
    attn_whole = ((4, SLABS, DEPTH + EXTRA, 768), bf)
    down_shapes = [((n, 4, DEPTH, 768), bf) for n in (4, 1, 1, 1, 1)]
    up_shapes = [((n, 4, DEPTH, 768), bf) for n in (4, 4)]
    attn_shapes = [((n, 4, DEPTH + EXTRA, 768), bf) for n in (4, 1, 1, 1, 1)]
    thin = ((4, 1, 768), fl)

    if fast:
        own = jnp.stack(over_tensor(jnp.concatenate([attn_shard, extra])))
        ffn_slabs = over_tensor(late([jnp.concatenate([up_shard, down_shard])], own)[0])
        attn_pieces = gather_staged(own, ffn_slabs[1:3])
        ffn_own = jnp.stack(late(ffn_slabs, attn_pieces[3][0], attn_pieces[4][0]))
        wait = [ffn_own]
    else:
        attn_pieces = gather_plain(attn_shard, extra)
        ups, downs = gather_plain(up_shard), gather_plain(down_shard)
        ffn_pieces = [(jnp.concatenate([u, d], axis=1), w) for (u, w), (d, _) in zip(ups, downs)]
        wait = []

    def split(pieces):
        return [p for p, _ in pieces], tuple(w for _, w in pieces)

    pieces, plan = split(attn_pieces)
    proj, ctx, lse, attn_w, xhat, rstd, first, vec, b_up = call(
        functools.partial(attn_fwd_kernel, plan), "attn_fwd",
        [(wide, bf), ((4, length, 256), bf), ((4, 3, 1, length), fl), attn_whole, row_f, ((length, LANES), fl), row_b,
         ((8, width), fl), thin],
        where, x, seg, seg_col, *pieces, after=wait,
    )
    if fast:
        ffn_pieces = gather_staged(ffn_own, [vec])
    pieces, plan = split(ffn_pieces)
    out, dr2, act, slope, small_two, up_w, down_w = call(
        functools.partial(ffn_fwd_kernel, plan), "ffn_fwd",
        [row_b, row_f, (wide, bf), (wide, fl), ((3, width), fl), whole, whole],
        where, xhat, first, dy, vec, b_up, *pieces,
    )
    down_near, *down_far = call(
        down_weights_kernel, "down_weights", down_shapes, where, dr2, act,
    )
    dup, b_up_grad = call(down_bwd_kernel, "down_bwd", [(wide, bf), thin], where, dr2, slope, down_w)
    out_one = next_row(out, b_up_grad)
    wait = [out_one]
    if fast:
        down_half = halves(reduce_core(down_near, down_far, [b_up_grad, out_one]))
        wait += down_half
    dr1, dctx, small_one = call(
        up_bwd_kernel, "up_bwd", [row_f, ((4, length, 256), bf), ((3, width), fl)],
        where, dr2, dup, xhat, rstd, vec, up_w, attn_w, after=wait,
    )
    out_two = next_row(out_one, small_one)
    grad_row, dproj, bias_grad = call(
        attn_bwd_kernel, "attn_bwd", [row_b, (wide, bf), thin],
        where, seg, seg_col, proj, lse, dr1, dctx, attn_w, after=[out_two],
        scratch=[pltpu.VMEM((length, width), fl)],
    )
    out_three = next_row(out_two, bias_grad)
    wait = [out_three]
    if fast:
        down_pair = reduce_pair(down_half, 1, [bias_grad])
        wait += down_pair
    attn_near, *attn_far = call(
        attn_weights_kernel, "attn_weights", attn_shapes,
        where, x, dproj, ctx, dr1, bias_grad, b_up_grad, small_one, small_two,
        scratch=[pltpu.VMEM((EXTRA, width), fl)], after=wait,
    )
    up_near, *up_far = call(
        up_weights_kernel, "up_weights", up_shapes, where, first, dup, after=[bias_grad, attn_near],
    )
    in_one = rotate(grad_row)
    in_two = rotate(in_one)
    in_three = rotate(in_two)
    hidden_out = place_rows([out, out_one, out_two, out_three], spin)
    grad_in = place_rows([grad_row, in_one, in_two, in_three], spin)
    if fast:
        down_plane = reduce_chip(down_pair, 2)
        attn_far = late(attn_far, *down_plane)
        attn_half = halves(reduce_core(attn_near, attn_far, [up_near, in_one]))
        up_far = late(up_far, in_one, *attn_half)
        down_sum = reduce_tensor(down_plane)
        up_pair = reduce_pair(reduce_core(up_near, up_far, parts=2), 1, [in_two])
        up_plane = reduce_chip(up_pair, 2)
        attn_plane = reduce_chip(reduce_pair(attn_half, 2), 1, [in_three])
        attn_sum = reduce_tensor([attn_plane[0]] + late(attn_plane[1:], *up_plane))
        up_sum = reduce_tensor(up_plane)
    else:
        down_sum = reduce_plain(down_near, down_far, x_last=True)
        up_sum = reduce_plain(up_near, up_far, x_last=True)
        attn_sum = reduce_plain(attn_near, attn_far)

    def own_part(value):
        size = value.shape[-1] // n_dp
        return lax.dynamic_slice_in_dim(value, dp * size, size, value.ndim - 1)

    small = attn_sum[rows:]
    gq = jnp.concatenate([small[6, :cut], small[6, 384 : 384 + HD]])
    gv = jnp.concatenate([small[6, 256 : 256 + cut], small[6, 384 + HD : 512]])
    grad_qv = own_part(jnp.stack([gq, gv]).reshape(2, 3, HD))
    grad_b_up = own_part(small[7].reshape(6, LANES))
    grad_vectors = own_part(small[:6])

    gk = [attn_sum[:rows, 128 * n : 128 * (n + 1)] for n in range(6)]
    grad_qkv = jnp.stack(
        [
            jnp.concatenate([gk[0], gk[3][:, :HD]], axis=1),
            jnp.concatenate([gk[1], gk[5][:, :HD]], axis=1),
            jnp.concatenate([gk[2], gk[3][:, HD:]], axis=1),
        ],
        axis=1,
    )
    grad_out = jnp.concatenate([gk[4], gk[5][:, HD:]], axis=1).T
    summed = (grad_qkv, grad_qv, grad_out, up_sum, grad_b_up, down_sum.T, grad_vectors)
    steps_f = step_count[0].astype(fl)
    factor = jnp.minimum(steps_f / warm_steps, (total_steps - steps_f) / (total_steps - warm_steps))
    fix_first = 1.0 - jnp.exp(steps_f * math.log(beta_first))
    fix_second = 1.0 - jnp.exp(steps_f * math.log(beta_second))
    states = (qkv_state, qv_bias_state, out_state, up_state, up_bias_state, down_state, vector_state)
    news = tuple((moment_update(s, g) for s, g in zip(states, summed)))
    plan_out = jnp.stack([factor, fix_first, fix_second])
    return (hidden_out, grad_in, *summed, *news, plan_out)


def solution(mesh):
    return jax.shard_map(
        body,
        mesh=mesh,
        in_specs=(
            P("dp", None, None),
            P("dp", None, None),
            P("dp", None),
            P(),
            P(None, "dp", None, "tensor"),
            P(None, None, "tensor", "dp"),
            P(None, "tensor", "dp"),
            P(None, "dp", "tensor"),
            P(None, "tensor", "dp"),
            P(None, "tensor", "dp"),
            P(None, None, "dp"),
        ),
        out_specs=(
            P("dp", None, None),
            P("dp", None, None),
            P("dp", None, "tensor"),
            P(None, "tensor", "dp"),
            P("tensor", "dp"),
            P("dp", "tensor"),
            P("tensor", "dp"),
            P("tensor", "dp"),
            P(None, "dp"),
            P(None, "dp", None, "tensor"),
            P(None, None, "tensor", "dp"),
            P(None, "tensor", "dp"),
            P(None, "dp", "tensor"),
            P(None, "tensor", "dp"),
            P(None, "tensor", "dp"),
            P(None, None, "dp"),
            P(),
        ),
        check_vma=False,
    )
```

```python
import functools
import math

import jax
import jax.numpy as jnp
from jax import lax
from jax.experimental import pallas as pl
from jax.experimental.pallas import tpu as pltpu
from jax.sharding import PartitionSpec as P

HD = 64
LANES = 128
VMEM_LIMIT = 60 * 1024 * 1024

norm_eps = 1e-05
beta_first = 0.9
beta_second = 0.999
warm_steps = 10000.0
total_steps = 200000.0

bf = jnp.bfloat16
fl = jnp.float32

SLABS = 8
DEPTH = 96
EXTRA = 16


def nt(left, right):
    return lax.dot_general(left, right, (((1,), (1,)), ((), ())), preferred_element_type=fl)


def nn(left, right):
    return lax.dot_general(left, right, (((1,), (0,)), ((), ())), preferred_element_type=fl)


def tn(left, right):
    return lax.dot_general(left, right, (((0,), (0,)), ((), ())), preferred_element_type=fl)


def low_lanes(shape):
    return lax.broadcasted_iota(jnp.int32, shape, 1) < HD


def assemble(where_ref, pieces, plan, *targets):
    for ref, (r, hops) in zip(pieces, plan):
        slab = jnp.bitwise_xor(where_ref[0], r)
        for k, hop in enumerate(hops):
            group = jnp.bitwise_xor(where_ref[1], hop)
            first = 0
            for target in targets:
                last = first + target.shape[2]
                target[group, slab] = ref[k, first:last]
                first = last


def scatter_slabs(where_ref, value, near_ref, far_refs, extra=None, x_last=False):
    chip = jnp.right_shift(where_ref[0], 1)
    core = jnp.bitwise_and(where_ref[0], 1)

    def put(near, far):
        for j in range(SLABS // 2):
            place = jnp.bitwise_xor(chip, j)
            if x_last:
                place = 2 * jnp.bitwise_and(place, 1) + jnp.right_shift(place, 1)

            def store(ref, index, slab):
                ref[index, 0, :DEPTH] = value[DEPTH * slab : DEPTH * (slab + 1)]
                if extra is not None:
                    ref[index, 0, DEPTH:] = extra

            store(near_ref, place, 2 * j + near)
            size = 4 // len(far_refs)
            for k, ref in enumerate(far_refs):
                inside = jnp.logical_and(place >= size * k, place < size * (k + 1))
                index = jnp.clip(place - size * k, 0, size - 1)
                pl.when(inside)(functools.partial(store, ref, index, 2 * j + far))

    pl.when(core == 0)(functools.partial(put, 0, 1))
    pl.when(core == 1)(functools.partial(put, 1, 0))


def matrix(ref, group):
    return ref[group][:, :DEPTH].reshape(SLABS * DEPTH, ref.shape[-1])


def out_matrix(ref, group):
    return ref[group][:, :DEPTH, 512:768].reshape(SLABS * DEPTH, 256)


def attn_fwd_kernel(plan, where_ref, x_ref, seg_row_ref, seg_col_ref, *refs):
    pieces = refs[: len(plan)]
    proj_ref, ctx_ref, lse_ref, weight_ref, xhat_ref, rstd_ref, first_ref, vec_ref, b_up_ref = refs[-9:]
    assemble(where_ref, pieces, plan, weight_ref)
    scale = HD ** (-0.5)
    length = x_ref.shape[0]

    def group_step(g, carry):
        small = jnp.sum(weight_ref[g, :, DEPTH:].astype(fl), axis=0)
        vec_ref[...] = small[:8]
        b_up_ref[g] = small[7:8]
        x = x_ref[...]
        proj = (nn(x, matrix(weight_ref, g)) + small[6:7]).astype(bf)
        proj_ref[g] = proj
        same = seg_col_ref[...] == seg_row_ref[...]
        low = low_lanes((length, LANES))
        none = jnp.zeros((length, LANES), bf)
        parts = [proj[:, LANES * k : LANES * (k + 1)] for k in range(6)]
        outs = []
        for head in range(3):
            query = parts[0] if head < 2 else parts[3]
            keys = parts[1] if head < 2 else parts[5]
            value = parts[2] if head < 2 else parts[3]
            query = jnp.where(low, none, query) if head == 1 else jnp.where(low, query, none)
            scores = jnp.where(same, nt(keys, query) * scale, -1e30)
            top = jnp.max(scores, axis=0, keepdims=True)
            expd = jnp.exp(scores - top)
            denom = jnp.sum(expd, axis=0, keepdims=True)
            lse_ref[g, head] = top + jnp.log(denom)
            probs = (expd / denom).astype(bf)
            outs.append(tn(probs, value).astype(bf))
        ctx_ref[g] = jnp.concatenate(
            [jnp.where(low, outs[0], outs[1]), jnp.where(low, none, outs[2])], axis=1
        )
        return carry

    lax.fori_loop(0, 4, group_step, 0)
    total = x_ref[...].astype(fl) + vec_ref[4:5]
    attn = None
    for g in range(4):
        part = nt(ctx_ref[g], out_matrix(weight_ref, g))
        attn = part if attn is None else attn + part
    total = total + attn
    center = total - jnp.mean(total, axis=-1, keepdims=True)
    rstd = lax.rsqrt(jnp.mean(center * center, axis=-1, keepdims=True) + norm_eps)
    xhat = center * rstd
    xhat_ref[...] = xhat
    rstd_ref[...] = jnp.broadcast_to(rstd, rstd_ref.shape)
    first_ref[...] = (xhat * vec_ref[0:1] + vec_ref[1:2]).astype(bf)


def ffn_fwd_kernel(plan, where_ref, xhat_ref, first_ref, dy_ref, vec_ref, b_up_ref, *refs):
    pieces, refs = refs[: len(plan)], refs[len(plan) :]
    out_ref, dr2_ref, act_ref, slope_ref, small_ref, up_w_ref, down_w_ref = refs
    assemble(where_ref, pieces, plan, up_w_ref, down_w_ref)

    def step(g, carry):
        up = nn(first_ref[...], matrix(up_w_ref, g)) + b_up_ref[g]
        half = 0.5 * (1.0 + lax.erf(up * 0.7071067811865476))
        act_ref[g] = (up * half).astype(bf)
        slope_ref[g] = half + up * (jnp.exp(-0.5 * up * up) * 0.3989422804014327)
        return carry

    lax.fori_loop(0, 4, step, 0)
    ffn = None
    for g in range(4):
        part = nt(act_ref[g], matrix(down_w_ref, g))
        ffn = part if ffn is None else ffn + part
    first = xhat_ref[...] * vec_ref[0:1] + vec_ref[1:2]
    total = first + ffn + vec_ref[5:6]
    center = total - jnp.mean(total, axis=-1, keepdims=True)
    rstd = lax.rsqrt(jnp.mean(center * center, axis=-1, keepdims=True) + norm_eps)
    xhat = center * rstd
    out_ref[...] = (xhat * vec_ref[2:3] + vec_ref[3:4]).astype(bf)
    dy = dy_ref[...].astype(fl)
    small_ref[0:1] = jnp.sum(dy * xhat, axis=0, keepdims=True)
    small_ref[1:2] = jnp.sum(dy, axis=0, keepdims=True)
    dxhat = dy * vec_ref[2:3]
    dr2 = rstd * (
        dxhat
        - jnp.mean(dxhat, axis=-1, keepdims=True)
        - xhat * jnp.mean(dxhat * xhat, axis=-1, keepdims=True)
    )
    dr2_ref[...] = dr2
    small_ref[2:3] = jnp.sum(dr2, axis=0, keepdims=True)


def down_weights_kernel(where_ref, dr2_ref, act_ref, near_ref, *refs):
    *far_refs, turned_ref = refs

    @pl.when(pl.program_id(0) == 0)
    def _():
        turned_ref[...] = dr2_ref[...].astype(bf).T

    scatter_slabs(where_ref, nn(turned_ref[...], act_ref[0]).astype(bf), near_ref, far_refs, x_last=True)


def down_bwd_kernel(where_ref, dr2_ref, slope_ref, weight_ref, dup_ref, b_up_ref):
    dup = (nn(dr2_ref[...].astype(bf), matrix(weight_ref, 0)) * slope_ref[0]).astype(bf)
    dup_ref[0] = dup
    b_up_ref[0] = jnp.sum(dup.astype(fl), axis=0, keepdims=True)


def up_weights_kernel(where_ref, first_ref, dup_ref, near_ref, *refs):
    *far_refs, turned_ref = refs

    @pl.when(pl.program_id(0) == 0)
    def _():
        turned_ref[...] = first_ref[...].T

    scatter_slabs(where_ref, nn(turned_ref[...], dup_ref[0]).astype(bf), near_ref, far_refs, x_last=True)


def up_bwd_kernel(where_ref, dr2_ref, dup_ref, xhat_ref, rstd_ref, vec_ref, weight_ref, attn_weight_ref, *refs):
    dr1_ref, dctx_ref, small_ref = refs[-3:]
    feed = None
    for g in range(4):
        part = nt(dup_ref[g], matrix(weight_ref, g))
        feed = part if feed is None else feed + part
    dfirst = dr2_ref[...] + feed.astype(bf).astype(fl)
    xhat = xhat_ref[...]
    small_ref[0:1] = jnp.sum(dfirst * xhat, axis=0, keepdims=True)
    small_ref[1:2] = jnp.sum(dfirst, axis=0, keepdims=True)
    dxhat = dfirst * vec_ref[0:1]
    dr1 = rstd_ref[:, 0:1] * (
        dxhat
        - jnp.mean(dxhat, axis=-1, keepdims=True)
        - xhat * jnp.mean(dxhat * xhat, axis=-1, keepdims=True)
    )
    dr1_ref[...] = dr1
    small_ref[2:3] = jnp.sum(dr1, axis=0, keepdims=True)
    dattn = dr1.astype(bf)
    for g in range(4):
        dctx_ref[g] = nn(dattn, out_matrix(attn_weight_ref, g)).astype(bf)


def attn_bwd_kernel(where_ref, seg_row_ref, seg_col_ref, proj_ref, lse_ref, dr1_ref, dctx_ref, weight_ref, *refs):
    grad_in_ref, dproj_ref, bias_ref, back_ref = refs[-4:]
    scale = HD ** (-0.5)
    length = dr1_ref.shape[0]
    back_ref[...] = jnp.zeros_like(back_ref)

    def step(g, carry):
        same = seg_col_ref[...] == seg_row_ref[...]
        low = low_lanes((length, LANES))
        none = jnp.zeros((length, LANES), bf)
        parts = [proj_ref[g, :, LANES * k : LANES * (k + 1)] for k in range(6)]
        dctx = [dctx_ref[g, :, :LANES], dctx_ref[g, :, LANES:]]
        dq, dk, dv = [], [], []
        for head in range(3):
            query = parts[0] if head < 2 else parts[3]
            keys = parts[1] if head < 2 else parts[5]
            value = parts[2] if head < 2 else parts[3]
            dout = dctx[0] if head < 2 else dctx[1]
            query_in = jnp.where(low, none, query) if head == 1 else jnp.where(low, query, none)
            dout_in = jnp.where(low, dout, none) if head == 0 else jnp.where(low, none, dout)
            scores = jnp.where(same, nt(keys, query_in) * scale, -1e30)
            probs = jnp.exp(scores - lse_ref[g, head])
            dprobs = nt(value, dout_in)
            dv.append(nn(probs.astype(bf), dout))
            row_dot = jnp.sum(probs * dprobs, axis=0, keepdims=True)
            dscores = (probs * (dprobs - row_dot)).astype(bf)
            dq.append(tn(dscores, keys) * scale)
            dk.append(nn(dscores, query) * scale)
        dproj = jnp.concatenate(
            [
                jnp.where(low, dq[0], dq[1]).astype(bf),
                jnp.where(low, dk[0], dk[1]).astype(bf),
                jnp.where(low, dv[0], dv[1]).astype(bf),
                jnp.where(low, dq[2], dv[2]).astype(bf),
                none,
                jnp.where(low, dk[2].astype(bf), none),
            ],
            axis=1,
        )
        dproj_ref[g] = dproj
        bias_ref[g] = jnp.sum(dproj.astype(fl), axis=0, keepdims=True)
        back_ref[...] += nt(dproj, matrix(weight_ref, g))
        return carry

    lax.fori_loop(0, 4, step, 0)
    dr1 = dr1_ref[...]
    grad_in_ref[...] = (dr1 + back_ref[...].astype(bf).astype(fl)).astype(bf)


def attn_weights_kernel(where_ref, x_ref, dproj_ref, ctx_ref, dr1_ref, bias_ref, b_up_ref, one_ref, two_ref,
                        near_ref, *refs):
    *far_refs, small_ref, x_turned_ref, dr1_turned_ref = refs

    @pl.when(pl.program_id(0) == 0)
    def _():
        small_ref[...] = jnp.zeros_like(small_ref)
        small_ref[0:2] = one_ref[0:2]
        small_ref[2:4] = two_ref[0:2]
        small_ref[4:5] = one_ref[2:3]
        small_ref[5:6] = two_ref[2:3]
        x_turned_ref[...] = x_ref[...].T
        dr1_turned_ref[...] = dr1_ref[...].astype(bf).T

    small_ref[6:7] = bias_ref[0]
    small_ref[7:8] = b_up_ref[0]
    main = nn(x_turned_ref[...], dproj_ref[0])
    side = nn(dr1_turned_ref[...], ctx_ref[0])
    whole = jnp.concatenate([main[:, :512], main[:, 512:] + side], axis=1).astype(bf)
    scatter_slabs(where_ref, whole, near_ref, far_refs, small_ref[...].astype(bf))


def place_kernel(where_ref, *refs):
    out_ref = refs[-1]
    for d, ref in enumerate(refs[:-1]):
        out_ref[jnp.bitwise_and(where_ref[1] + 4 - d, 3)] = ref[...]


smem = pl.BlockSpec(memory_space=pltpu.SMEM)
vmem = pl.BlockSpec(memory_space=pltpu.VMEM)


def call(kernel, name, outs, where, *args, scratch=(), after=()):
    if after:
        (where,) = late([where], *after)
    return pl.pallas_call(
        kernel,
        name=name,
        out_shape=[jax.ShapeDtypeStruct(s, d) for s, d in outs],
        in_specs=[smem] + [vmem] * len(args),
        out_specs=[vmem] * len(outs),
        scratch_shapes=list(scratch),
        compiler_params=pltpu.CompilerParams(vmem_limit_bytes=VMEM_LIMIT),
        cost_estimate=pl.CostEstimate(flops=COST, bytes_accessed=COST, transcendentals=0),
    )(where, *args)


COST = 1000


def whole_block(shape):
    return pl.BlockSpec(shape, lambda g, where: (0,) * len(shape))


def group_block(shape):
    return pl.BlockSpec((1, *shape[1:]), lambda g, where: (g,) + (0,) * (len(shape) - 1))


def slab_block(shape):
    def index(g, where):
        hop = jnp.bitwise_xor(g, where[1])
        return (0, 2 * jnp.bitwise_and(hop, 1) + jnp.right_shift(hop, 1), 0, 0)

    return pl.BlockSpec((shape[0], 1, *shape[2:]), index)


def call_groups(kernel, name, outs, where, *args, scratch=(), after=()):
    if after:
        (where,) = late([where], *after)
    return pl.pallas_call(
        kernel,
        name=name,
        out_shape=[jax.ShapeDtypeStruct(s, d) for (s, d), _ in outs],
        grid_spec=pltpu.PrefetchScalarGridSpec(
            num_scalar_prefetch=1,
            grid=(4,),
            in_specs=[block(a.shape) for a, block in args],
            out_specs=[block(s) for (s, _), block in outs],
            scratch_shapes=list(scratch),
        ),
        compiler_params=pltpu.CompilerParams(
            vmem_limit_bytes=VMEM_LIMIT, dimension_semantics=("arbitrary",)
        ),
        cost_estimate=pl.CostEstimate(flops=COST, bytes_accessed=COST, transcendentals=0),
    )(where, *[a for a, _ in args])


def flip(value, bits):
    n = lax.axis_size("dp")
    return lax.ppermute(value, "dp", [(k, k ^ bits) for k in range(n)])


def cross(value, bits):
    return lax.ppermute(value, "tensor", [(k, k ^ bits) for k in range(4)])


def rotate(value):
    return lax.ppermute(value, "tensor", [(k, (k + 1) % 4) for k in range(4)])


def late(values, *gates):
    return list(lax.optimization_barrier((*values, *gates))[: len(values)])


def with_core(near):
    return near + [(flip(a, 1), (r + 1, s)) for a, (r, s) in near]


ALL = (0, 1, 2, 3)


def over_tensor(shard):
    return [shard] + [cross(shard, hop) for hop in (1, 2, 3)]


def gather_staged(own, gates=()):
    over_x = flip(own, 2)
    over_y = flip(own, 4)
    half_x, half_y = late([over_x[:2], over_y[2:]], *gates)
    far_a = flip(half_x, 4)
    far_b = flip(half_y, 2)
    near = [(own, (0, ALL)), (over_x, (2, ALL)), (over_y, (4, ALL))]
    return with_core(near + [(far_a, (6, (0, 1))), (far_b, (6, (2, 3)))])


def add(*values):
    total = values[0].astype(fl)
    for value in values[1:]:
        total = total + value.astype(fl)
    return total


def reduce_core(near, far, gates=(), parts=1):
    got = late([flip(part, 1) for part in far], *gates) if gates else [flip(part, 1) for part in far]
    size, each = 4 // len(far), len(far) * parts
    return [
        add(near[a : a + 4 // each], got[a // size][a % size : a % size + 4 // each]).astype(bf)
        for a in range(0, 4, 4 // each)
    ]


def halves(parts):
    return [jnp.concatenate(parts[:2]), jnp.concatenate(parts[2:])]


def reduce_pair(half, axis, gates=()):
    got = flip(half[1], 2 * axis)
    if gates:
        (got,) = late([got], *gates)
    return [add(half[0][k], got[k]).astype(bf) for k in (0, 1)]


def reduce_chip(pair, axis, gates=()):
    got = flip(pair[1], 2 * axis)
    if gates:
        (got,) = late([got], *gates)
    return [add(pair[0][k : k + 2], got[k : k + 2]).astype(bf) for k in (0, 2)]


def reduce_tensor(plane, gates=()):
    got = cross(plane[1], 1)
    if gates:
        (got,) = late([got], *gates)
    near, far = add(plane[0][0], got[0]), add(plane[0][1], got[1]).astype(bf)
    return add(near, cross(far, 2))


def gather_plain(shard, extra=None):
    whole = lax.all_gather(lax.all_gather(shard, "dp", axis=0, tiled=True), "tensor", axis=0)
    whole = whole.reshape(4, SLABS, -1, 768)
    if extra is not None:
        extra = lax.all_gather(lax.psum(extra, "dp"), "tensor", axis=0)[:, None].astype(bf)
        extra = jnp.concatenate([extra] + [jnp.zeros_like(extra)] * (SLABS - 1), axis=1)
        whole = jnp.concatenate([whole, extra], axis=2)
    return [(whole[:, r], (r, ALL)) for r in range(SLABS)]


def reduce_plain(near, far, x_last=False):
    order = jnp.array([0, 2, 1, 3])
    grad = jnp.stack([near, jnp.concatenate(far)], axis=1)[:, :, order]
    grad = (grad[order] if x_last else grad).reshape(SLABS, 4, -1, 768).astype(fl)
    whole = grad[:, :, :DEPTH].transpose(1, 0, 2, 3).reshape(4, SLABS * DEPTH, 768)
    part = lax.psum_scatter(whole, "tensor", scatter_dimension=0, tiled=True)
    part = lax.psum_scatter(part[0], "dp", scatter_dimension=0, tiled=True)
    if near.shape[2] == DEPTH:
        return part
    extra = lax.psum_scatter(lax.psum(grad[0, :, DEPTH:], "dp"), "tensor", scatter_dimension=0, tiled=True)[0]
    return jnp.concatenate([part, extra])


def next_row(row, gate):
    (row,) = late([rotate(row)], gate)
    return row


def place_rows(rows, where, after=()):
    return call(place_kernel, "place_rows", [((4,) + rows[0].shape, rows[0].dtype)], where, *rows, after=after)[0]


def moment_update(state, grad):
    moment_one = beta_first * state[1] + (1.0 - beta_first) * grad
    moment_two = beta_second * state[2] + (1.0 - beta_second) * grad * grad
    return jnp.stack([moment_one, moment_two])


def body(
    hidden_in,
    out_grad,
    segment_ids,
    step_count,
    qkv_state,
    qv_bias_state,
    out_state,
    up_state,
    up_bias_state,
    down_state,
    vector_state,
):
    n_dp = lax.axis_size("dp")
    place = lax.axis_index("tensor")
    fast = n_dp == SLABS
    spot = lax.axis_index("dp") if fast else 0
    where = jnp.stack([jnp.int32(spot), (place if fast else 0) * jnp.int32(1)])
    spin = jnp.stack([jnp.int32(0), place * jnp.int32(1)])
    rows, width = qkv_state.shape[1], hidden_in.shape[2]
    cut = 2 * HD

    def spread(value, axis, whole):
        full = jnp.zeros(value.shape[:-1] + (whole,), bf)
        return lax.dynamic_update_slice_in_dim(full, value.astype(bf), axis * value.shape[-1], value.ndim - 1)

    dp = lax.axis_index("dp")
    q, k, v = (qkv_state[0, :, c].astype(bf) for c in range(3))
    o = out_state[0].T.astype(bf)
    attn_shard = jnp.concatenate(
        [q[:, :cut], k[:, :cut], v[:, :cut], q[:, cut:], v[:, cut:], o[:, :cut], k[:, cut:], o[:, cut:]], axis=1
    )
    bq, bv = spread(qv_bias_state[0], dp, HD).reshape(2, 3 * HD)
    gap = jnp.zeros((cut,), bf)
    bias = jnp.concatenate([bq[:cut], gap, bv[:cut], bq[cut:], bv[cut:], gap, gap])
    b_up = spread(up_bias_state[0], dp, LANES).reshape(1, 768)
    extra = jnp.concatenate(
        [spread(vector_state[0], dp, width), bias[None], b_up, jnp.zeros((EXTRA - 8, width), bf)]
    )
    up_shard = up_state[0].astype(bf)
    down_shard = down_state[0].T.astype(bf)

    x = lax.dynamic_index_in_dim(hidden_in, place, 0, keepdims=False)
    dy = lax.dynamic_index_in_dim(out_grad, place, 0, keepdims=False)
    seg = lax.dynamic_index_in_dim(segment_ids, place, 0, keepdims=True)
    seg_col = seg.reshape(-1, 1)
    length = x.shape[0]
    wide = (4, length, 768)
    row_f, row_b = ((length, width), fl), ((length, width), bf)
    whole = ((4, SLABS, DEPTH, 768), bf)
    attn_whole = ((4, SLABS, DEPTH + EXTRA, 768), bf)
    down_outs = [(((n, 4, DEPTH, 768), bf), slab_block) for n in (4, 1, 1, 1, 1)]
    up_outs = [(((n, 4, DEPTH, 768), bf), slab_block) for n in (4, 4)]
    attn_outs = [(((n, 4, DEPTH + EXTRA, 768), bf), slab_block) for n in (4, 1, 1, 1, 1)]
    thin = ((4, 1, 768), fl)

    if fast:
        own = jnp.stack(over_tensor(jnp.concatenate([attn_shard, extra])))
        ffn_slabs = over_tensor(late([jnp.concatenate([up_shard, down_shard])], own)[0])
        attn_pieces = gather_staged(own, ffn_slabs[1:3])
        ffn_own = jnp.stack(late(ffn_slabs, attn_pieces[3][0], attn_pieces[4][0]))
        wait = [ffn_own]
    else:
        attn_pieces = gather_plain(attn_shard, extra)
        ups, downs = gather_plain(up_shard), gather_plain(down_shard)
        ffn_pieces = [(jnp.concatenate([u, d], axis=1), w) for (u, w), (d, _) in zip(ups, downs)]
        wait = []

    def split(pieces):
        return [p for p, _ in pieces], tuple(w for _, w in pieces)

    pieces, plan = split(attn_pieces)
    proj, ctx, lse, attn_w, xhat, rstd, first, vec, b_up = call(
        functools.partial(attn_fwd_kernel, plan), "attn_fwd",
        [(wide, bf), ((4, length, 256), bf), ((4, 3, 1, length), fl), attn_whole, row_f, ((length, LANES), fl), row_b,
         ((8, width), fl), thin],
        where, x, seg, seg_col, *pieces, after=wait,
    )
    if fast:
        ffn_pieces = gather_staged(ffn_own, [vec])
    pieces, plan = split(ffn_pieces)
    out, dr2, act, slope, small_two, up_w, down_w = call(
        functools.partial(ffn_fwd_kernel, plan), "ffn_fwd",
        [row_b, row_f, (wide, bf), (wide, fl), ((3, width), fl), whole, whole],
        where, xhat, first, dy, vec, b_up, *pieces,
    )
    turned = pltpu.VMEM((width, length), bf)
    down_near, *down_far = call_groups(
        down_weights_kernel, "down_weights", down_outs, where, (dr2, whole_block), (act, group_block),
        scratch=[turned],
    )
    dup, b_up_grad = call_groups(
        down_bwd_kernel, "down_bwd", [((wide, bf), group_block), (thin, group_block)],
        where, (dr2, whole_block), (slope, group_block), (down_w, group_block),
    )
    out_one = next_row(out, b_up_grad)
    wait = [out_one]
    if fast:
        down_half = halves(reduce_core(down_near, down_far, [b_up_grad, out_one]))
        wait += down_half
    dr1, dctx, small_one = call(
        up_bwd_kernel, "up_bwd", [row_f, ((4, length, 256), bf), ((3, width), fl)],
        where, dr2, dup, xhat, rstd, vec, up_w, attn_w, after=wait,
    )
    out_two = next_row(out_one, small_one)
    grad_row, dproj, bias_grad = call(
        attn_bwd_kernel, "attn_bwd", [row_b, (wide, bf), thin],
        where, seg, seg_col, proj, lse, dr1, dctx, attn_w, after=[out_two],
        scratch=[pltpu.VMEM((length, width), fl)],
    )
    out_three = next_row(out_two, bias_grad)
    wait = [out_three]
    if fast:
        down_pair = reduce_pair(down_half, 1, [bias_grad])
        wait += down_pair
    attn_near, *attn_far = call_groups(
        attn_weights_kernel, "attn_weights", attn_outs,
        where, (x, whole_block), (dproj, group_block), (ctx, group_block), (dr1, whole_block),
        (bias_grad, group_block), (b_up_grad, group_block), (small_one, whole_block), (small_two, whole_block),
        scratch=[pltpu.VMEM((EXTRA, width), fl), turned, turned], after=wait,
    )
    up_near, *up_far = call_groups(
        up_weights_kernel, "up_weights", up_outs, where, (first, whole_block), (dup, group_block),
        scratch=[turned], after=[bias_grad, attn_near],
    )
    in_one = rotate(grad_row)
    in_two = rotate(in_one)
    in_three = rotate(in_two)
    hidden_out = place_rows([out, out_one, out_two, out_three], spin)
    wait = []
    if fast:
        down_plane = reduce_chip(down_pair, 2)
        attn_far = late(attn_far, *down_plane)
        attn_half = halves(reduce_core(attn_near, attn_far, [up_near, in_one]))
        up_far = late(up_far, in_one, *attn_half)
        up_pair = reduce_pair(reduce_core(up_near, up_far, parts=2), 1, [in_two])
        up_plane = reduce_chip(up_pair, 2)
        attn_pair = reduce_pair(attn_half, 2)
        attn_plane = reduce_chip(attn_pair, 1, [in_three, *up_pair])
        down_sum = reduce_tensor(down_plane, [*up_pair, *attn_pair])
        attn_sum = reduce_tensor([attn_plane[0]] + late(attn_plane[1:], *up_plane))
        up_sum = reduce_tensor(up_plane)
        wait = up_plane + attn_plane
    else:
        down_sum = reduce_plain(down_near, down_far, x_last=True)
        up_sum = reduce_plain(up_near, up_far, x_last=True)
        attn_sum = reduce_plain(attn_near, attn_far)

    grad_in = place_rows([grad_row, in_one, in_two, in_three], spin, wait)

    def own_part(value):
        size = value.shape[-1] // n_dp
        return lax.dynamic_slice_in_dim(value, dp * size, size, value.ndim - 1)

    small = attn_sum[rows:]
    gq = jnp.concatenate([small[6, :cut], small[6, 384 : 384 + HD]])
    gv = jnp.concatenate([small[6, 256 : 256 + cut], small[6, 384 + HD : 512]])
    grad_qv = own_part(jnp.stack([gq, gv]).reshape(2, 3, HD))
    grad_b_up = own_part(small[7].reshape(6, LANES))
    grad_vectors = own_part(small[:6])

    gk = [attn_sum[:rows, 128 * n : 128 * (n + 1)] for n in range(6)]
    grad_qkv = jnp.stack(
        [
            jnp.concatenate([gk[0], gk[3][:, :HD]], axis=1),
            jnp.concatenate([gk[1], gk[5][:, :HD]], axis=1),
            jnp.concatenate([gk[2], gk[3][:, HD:]], axis=1),
        ],
        axis=1,
    )
    grad_out = jnp.concatenate([gk[4], gk[5][:, HD:]], axis=1).T
    summed = (grad_qkv, grad_qv, grad_out, up_sum, grad_b_up, down_sum.T, grad_vectors)
    steps_f = step_count[0].astype(fl)
    factor = jnp.minimum(steps_f / warm_steps, (total_steps - steps_f) / (total_steps - warm_steps))
    fix_first = 1.0 - jnp.exp(steps_f * math.log(beta_first))
    fix_second = 1.0 - jnp.exp(steps_f * math.log(beta_second))
    states = (qkv_state, qv_bias_state, out_state, up_state, up_bias_state, down_state, vector_state)
    news = tuple((moment_update(s, g) for s, g in zip(states, summed)))
    plan_out = jnp.stack([factor, fix_first, fix_second])
    return (hidden_out, grad_in, *summed, *news, plan_out)


def solution(mesh):
    return jax.shard_map(
        body,
        mesh=mesh,
        in_specs=(
            P("dp", None, None),
            P("dp", None, None),
            P("dp", None),
            P(),
            P(None, "dp", None, "tensor"),
            P(None, None, "tensor", "dp"),
            P(None, "tensor", "dp"),
            P(None, "dp", "tensor"),
            P(None, "tensor", "dp"),
            P(None, "tensor", "dp"),
            P(None, None, "dp"),
        ),
        out_specs=(
            P("dp", None, None),
            P("dp", None, None),
            P("dp", None, "tensor"),
            P(None, "tensor", "dp"),
            P("tensor", "dp"),
            P("dp", "tensor"),
            P("tensor", "dp"),
            P("tensor", "dp"),
            P(None, "dp"),
            P(None, "dp", None, "tensor"),
            P(None, None, "tensor", "dp"),
            P(None, "tensor", "dp"),
            P(None, "dp", "tensor"),
            P(None, "tensor", "dp"),
            P(None, "tensor", "dp"),
            P(None, None, "dp"),
            P(),
        ),
        check_vma=False,
    )
```

```python
import functools
import math

import jax
import jax.numpy as jnp
from jax import lax
from jax.experimental import pallas as pl
from jax.experimental.pallas import tpu as pltpu
from jax.sharding import PartitionSpec as P

HD = 64
LANES = 128
VMEM_LIMIT = 60 * 1024 * 1024

norm_eps = 1e-05
beta_first = 0.9
beta_second = 0.999
warm_steps = 10000.0
total_steps = 200000.0

bf = jnp.bfloat16
fl = jnp.float32

SLABS = 8
DEPTH = 96
EXTRA = 16


def nt(left, right):
    return lax.dot_general(left, right, (((1,), (1,)), ((), ())), preferred_element_type=fl)


def nn(left, right):
    return lax.dot_general(left, right, (((1,), (0,)), ((), ())), preferred_element_type=fl)


def tn(left, right):
    return lax.dot_general(left, right, (((0,), (0,)), ((), ())), preferred_element_type=fl)


def low_lanes(shape):
    return lax.broadcasted_iota(jnp.int32, shape, 1) < HD


def assemble(where_ref, pieces, plan, *targets):
    for ref, (r, hops) in zip(pieces, plan):
        slab = jnp.bitwise_xor(where_ref[0], r)
        for k, hop in enumerate(hops):
            group = jnp.bitwise_xor(where_ref[1], hop)
            first = 0
            for target in targets:
                last = first + target.shape[2]
                target[group, slab] = ref[k, first:last]
                first = last


def scatter_slabs(where_ref, value, near_ref, far_refs, extra=None, x_last=False):
    chip = jnp.right_shift(where_ref[0], 1)
    core = jnp.bitwise_and(where_ref[0], 1)

    def put(near, far):
        for j in range(SLABS // 2):
            place = jnp.bitwise_xor(chip, j)
            if x_last:
                place = 2 * jnp.bitwise_and(place, 1) + jnp.right_shift(place, 1)

            def store(ref, index, slab):
                ref[index, 0, :DEPTH] = value[DEPTH * slab : DEPTH * (slab + 1)]
                if extra is not None:
                    ref[index, 0, DEPTH:] = extra

            store(near_ref, place, 2 * j + near)
            size = 4 // len(far_refs)
            for k, ref in enumerate(far_refs):
                inside = jnp.logical_and(place >= size * k, place < size * (k + 1))
                index = jnp.clip(place - size * k, 0, size - 1)
                pl.when(inside)(functools.partial(store, ref, index, 2 * j + far))

    pl.when(core == 0)(functools.partial(put, 0, 1))
    pl.when(core == 1)(functools.partial(put, 1, 0))


def matrix(ref, group):
    return ref[group][:, :DEPTH].reshape(SLABS * DEPTH, ref.shape[-1])


def out_matrix(ref, group):
    return ref[group][:, :DEPTH, 512:768].reshape(SLABS * DEPTH, 256)


def attn_fwd_kernel(plan, where_ref, x_ref, seg_row_ref, seg_col_ref, *refs):
    pieces = refs[: len(plan)]
    proj_ref, ctx_ref, lse_ref, weight_ref, xhat_ref, rstd_ref, first_ref, vec_ref, b_up_ref = refs[-9:]
    assemble(where_ref, pieces, plan, weight_ref)
    scale = HD ** (-0.5)
    length = x_ref.shape[0]

    def group_step(g, carry):
        small = jnp.sum(weight_ref[g, :, DEPTH:].astype(fl), axis=0)
        vec_ref[...] = small[:8]
        b_up_ref[g] = small[7:8]
        x = x_ref[...]
        proj = (nn(x, matrix(weight_ref, g)) + small[6:7]).astype(bf)
        proj_ref[g] = proj
        same = seg_col_ref[...] == seg_row_ref[...]
        low = low_lanes((length, LANES))
        none = jnp.zeros((length, LANES), bf)
        parts = [proj[:, LANES * k : LANES * (k + 1)] for k in range(6)]
        turned = [parts[2].T, parts[3].T]
        outs = []
        for head in range(3):
            query = parts[0] if head < 2 else parts[3]
            keys = parts[1] if head < 2 else parts[5]
            value = turned[0][:HD] if head == 0 else turned[head // 2][HD:]
            query = jnp.where(low, none, query) if head == 1 else jnp.where(low, query, none)
            scores = jnp.where(same, nt(keys, query) * scale, -1e30)
            top = jnp.max(scores, axis=0, keepdims=True)
            expd = jnp.exp(scores - top)
            denom = jnp.sum(expd, axis=0, keepdims=True)
            lse_ref[g, head] = top + jnp.log(denom)
            probs = (expd / denom).astype(bf)
            outs.append(nn(value, probs))
        outs.insert(2, jnp.zeros_like(outs[2]))
        ctx_ref[g, :, :LANES] = jnp.concatenate(outs[:2]).T.astype(bf)
        ctx_ref[g, :, LANES:] = jnp.concatenate(outs[2:]).T.astype(bf)
        return carry

    lax.fori_loop(0, 4, group_step, 0)
    total = x_ref[...].astype(fl) + vec_ref[4:5]
    attn = None
    for g in range(4):
        part = nt(ctx_ref[g], out_matrix(weight_ref, g))
        attn = part if attn is None else attn + part
    total = total + attn
    center = total - jnp.mean(total, axis=-1, keepdims=True)
    rstd = lax.rsqrt(jnp.mean(center * center, axis=-1, keepdims=True) + norm_eps)
    xhat = center * rstd
    xhat_ref[...] = xhat
    rstd_ref[...] = jnp.broadcast_to(rstd, rstd_ref.shape)
    first_ref[...] = (xhat * vec_ref[0:1] + vec_ref[1:2]).astype(bf)


def ffn_fwd_kernel(plan, where_ref, xhat_ref, first_ref, dy_ref, vec_ref, b_up_ref, *refs):
    pieces, refs = refs[: len(plan)], refs[len(plan) :]
    out_ref, dr2_ref, act_ref, slope_ref, small_ref, up_w_ref, down_w_ref = refs
    assemble(where_ref, pieces, plan, up_w_ref, down_w_ref)

    def step(g, carry):
        up = nn(first_ref[...], matrix(up_w_ref, g)) + b_up_ref[g]
        half = 0.5 * (1.0 + lax.erf(up * 0.7071067811865476))
        act_ref[g] = (up * half).astype(bf)
        slope_ref[g] = half + up * (jnp.exp(-0.5 * up * up) * 0.3989422804014327)
        return carry

    lax.fori_loop(0, 4, step, 0)
    ffn = None
    for g in range(4):
        part = nt(act_ref[g], matrix(down_w_ref, g))
        ffn = part if ffn is None else ffn + part
    first = xhat_ref[...] * vec_ref[0:1] + vec_ref[1:2]
    total = first + ffn + vec_ref[5:6]
    center = total - jnp.mean(total, axis=-1, keepdims=True)
    rstd = lax.rsqrt(jnp.mean(center * center, axis=-1, keepdims=True) + norm_eps)
    xhat = center * rstd
    out_ref[...] = (xhat * vec_ref[2:3] + vec_ref[3:4]).astype(bf)
    dy = dy_ref[...].astype(fl)
    small_ref[0:1] = jnp.sum(dy * xhat, axis=0, keepdims=True)
    small_ref[1:2] = jnp.sum(dy, axis=0, keepdims=True)
    dxhat = dy * vec_ref[2:3]
    dr2 = rstd * (
        dxhat
        - jnp.mean(dxhat, axis=-1, keepdims=True)
        - xhat * jnp.mean(dxhat * xhat, axis=-1, keepdims=True)
    )
    dr2_ref[...] = dr2
    small_ref[2:3] = jnp.sum(dr2, axis=0, keepdims=True)


def down_weights_kernel(where_ref, dr2_ref, act_ref, near_ref, *refs):
    *far_refs, turned_ref = refs

    @pl.when(pl.program_id(0) == 0)
    def _():
        turned_ref[...] = dr2_ref[...].astype(bf).T

    scatter_slabs(where_ref, nn(turned_ref[...], act_ref[0]).astype(bf), near_ref, far_refs, x_last=True)


def down_bwd_kernel(where_ref, dr2_ref, slope_ref, weight_ref, dup_ref, b_up_ref):
    dup = (nn(dr2_ref[...].astype(bf), matrix(weight_ref, 0)) * slope_ref[0]).astype(bf)
    dup_ref[0] = dup
    b_up_ref[0] = jnp.sum(dup.astype(fl), axis=0, keepdims=True)


def up_weights_kernel(where_ref, first_ref, dup_ref, near_ref, *refs):
    *far_refs, turned_ref = refs

    @pl.when(pl.program_id(0) == 0)
    def _():
        turned_ref[...] = first_ref[...].T

    scatter_slabs(where_ref, nn(turned_ref[...], dup_ref[0]).astype(bf), near_ref, far_refs, x_last=True)


def up_bwd_kernel(where_ref, dr2_ref, dup_ref, xhat_ref, rstd_ref, vec_ref, weight_ref, attn_weight_ref, *refs):
    dr1_ref, dctx_ref, small_ref = refs[-3:]
    feed = None
    for g in range(4):
        part = nt(dup_ref[g], matrix(weight_ref, g))
        feed = part if feed is None else feed + part
    dfirst = dr2_ref[...] + feed.astype(bf).astype(fl)
    xhat = xhat_ref[...]
    small_ref[0:1] = jnp.sum(dfirst * xhat, axis=0, keepdims=True)
    small_ref[1:2] = jnp.sum(dfirst, axis=0, keepdims=True)
    dxhat = dfirst * vec_ref[0:1]
    dr1 = rstd_ref[:, 0:1] * (
        dxhat
        - jnp.mean(dxhat, axis=-1, keepdims=True)
        - xhat * jnp.mean(dxhat * xhat, axis=-1, keepdims=True)
    )
    dr1_ref[...] = dr1
    small_ref[2:3] = jnp.sum(dr1, axis=0, keepdims=True)
    dattn = dr1.astype(bf)
    for g in range(4):
        dctx_ref[g] = nn(dattn, out_matrix(attn_weight_ref, g)).astype(bf)


def attn_bwd_kernel(where_ref, seg_row_ref, seg_col_ref, proj_ref, lse_ref, dr1_ref, dctx_ref, weight_ref, *refs):
    grad_in_ref, dproj_ref, bias_ref, back_ref = refs[-4:]
    scale = HD ** (-0.5)
    length = dr1_ref.shape[0]
    back_ref[...] = jnp.zeros_like(back_ref)

    def step(g, carry):
        same = seg_col_ref[...] == seg_row_ref[...]
        low = low_lanes((length, LANES))
        none = jnp.zeros((length, LANES), bf)
        parts = [proj_ref[g, :, LANES * k : LANES * (k + 1)] for k in range(6)]
        dctx = [dctx_ref[g, :, :LANES], dctx_ref[g, :, LANES:]]
        turned = [parts[1].T, parts[5].T]
        dq, dk, dv = [], [], []
        for head in range(3):
            query = parts[0] if head < 2 else parts[3]
            keys = parts[1] if head < 2 else parts[5]
            value = parts[2] if head < 2 else parts[3]
            dout = dctx[0] if head < 2 else dctx[1]
            query_in = jnp.where(low, none, query) if head == 1 else jnp.where(low, query, none)
            dout_in = jnp.where(low, dout, none) if head == 0 else jnp.where(low, none, dout)
            scores = jnp.where(same, nt(keys, query_in) * scale, -1e30)
            probs = jnp.exp(scores - lse_ref[g, head])
            dprobs = nt(value, dout_in)
            dv.append(nn(probs.astype(bf), dout))
            row_dot = jnp.sum(probs * dprobs, axis=0, keepdims=True)
            dscores = (probs * (dprobs - row_dot)).astype(bf)
            keys_turned = turned[0][HD:] if head == 1 else turned[head // 2][:HD]
            dq.append(nn(keys_turned, dscores) * scale)
            dk.append(nn(dscores, query) * scale)
        dq.append(jnp.zeros_like(dq[2]))
        dq_near, dq_far = jnp.concatenate(dq[:2]).T, jnp.concatenate(dq[2:]).T
        dproj = jnp.concatenate(
            [
                dq_near.astype(bf),
                jnp.where(low, dk[0], dk[1]).astype(bf),
                jnp.where(low, dv[0], dv[1]).astype(bf),
                jnp.where(low, dq_far, dv[2]).astype(bf),
                none,
                jnp.where(low, dk[2].astype(bf), none),
            ],
            axis=1,
        )
        dproj_ref[g] = dproj
        bias_ref[g] = jnp.sum(dproj.astype(fl), axis=0, keepdims=True)
        back_ref[...] += nt(dproj, matrix(weight_ref, g))
        return carry

    lax.fori_loop(0, 4, step, 0)
    dr1 = dr1_ref[...]
    grad_in_ref[...] = (dr1 + back_ref[...].astype(bf).astype(fl)).astype(bf)


def attn_weights_kernel(where_ref, x_ref, dproj_ref, ctx_ref, dr1_ref, bias_ref, b_up_ref, one_ref, two_ref,
                        near_ref, *refs):
    *far_refs, small_ref, x_turned_ref, dr1_turned_ref = refs

    @pl.when(pl.program_id(0) == 0)
    def _():
        small_ref[...] = jnp.zeros_like(small_ref)
        small_ref[0:2] = one_ref[0:2]
        small_ref[2:4] = two_ref[0:2]
        small_ref[4:5] = one_ref[2:3]
        small_ref[5:6] = two_ref[2:3]
        x_turned_ref[...] = x_ref[...].T
        dr1_turned_ref[...] = dr1_ref[...].astype(bf).T

    small_ref[6:7] = bias_ref[0]
    small_ref[7:8] = b_up_ref[0]
    main = nn(x_turned_ref[...], dproj_ref[0])
    side = nn(dr1_turned_ref[...], ctx_ref[0])
    whole = jnp.concatenate([main[:, :512], main[:, 512:] + side], axis=1).astype(bf)
    scatter_slabs(where_ref, whole, near_ref, far_refs, small_ref[...].astype(bf))


def place_kernel(where_ref, *refs):
    out_ref = refs[-1]
    for d, ref in enumerate(refs[:-1]):
        out_ref[jnp.bitwise_and(where_ref[1] + 4 - d, 3)] = ref[...]


smem = pl.BlockSpec(memory_space=pltpu.SMEM)
vmem = pl.BlockSpec(memory_space=pltpu.VMEM)


def call(kernel, name, outs, where, *args, scratch=(), after=()):
    if after:
        (where,) = late([where], *after)
    return pl.pallas_call(
        kernel,
        name=name,
        out_shape=[jax.ShapeDtypeStruct(s, d) for s, d in outs],
        in_specs=[smem] + [vmem] * len(args),
        out_specs=[vmem] * len(outs),
        scratch_shapes=list(scratch),
        compiler_params=pltpu.CompilerParams(vmem_limit_bytes=VMEM_LIMIT),
        cost_estimate=pl.CostEstimate(flops=COST, bytes_accessed=COST, transcendentals=0),
    )(where, *args)


COST = 1000


def whole_block(shape):
    return pl.BlockSpec(shape, lambda g, where: (0,) * len(shape))


def group_block(shape):
    return pl.BlockSpec((1, *shape[1:]), lambda g, where: (g,) + (0,) * (len(shape) - 1))


def slab_block(shape):
    def index(g, where):
        hop = jnp.bitwise_xor(g, where[1])
        return (0, 2 * jnp.bitwise_and(hop, 1) + jnp.right_shift(hop, 1), 0, 0)

    return pl.BlockSpec((shape[0], 1, *shape[2:]), index)


def call_groups(kernel, name, outs, where, *args, scratch=(), after=()):
    if after:
        (where,) = late([where], *after)
    return pl.pallas_call(
        kernel,
        name=name,
        out_shape=[jax.ShapeDtypeStruct(s, d) for (s, d), _ in outs],
        grid_spec=pltpu.PrefetchScalarGridSpec(
            num_scalar_prefetch=1,
            grid=(4,),
            in_specs=[block(a.shape) for a, block in args],
            out_specs=[block(s) for (s, _), block in outs],
            scratch_shapes=list(scratch),
        ),
        compiler_params=pltpu.CompilerParams(
            vmem_limit_bytes=VMEM_LIMIT, dimension_semantics=("arbitrary",)
        ),
        cost_estimate=pl.CostEstimate(flops=COST, bytes_accessed=COST, transcendentals=0),
    )(where, *[a for a, _ in args])


def flip(value, bits):
    n = lax.axis_size("dp")
    return lax.ppermute(value, "dp", [(k, k ^ bits) for k in range(n)])


def cross(value, bits):
    return lax.ppermute(value, "tensor", [(k, k ^ bits) for k in range(4)])


def rotate(value):
    return lax.ppermute(value, "tensor", [(k, (k + 1) % 4) for k in range(4)])


def late(values, *gates):
    return list(lax.optimization_barrier((*values, *gates))[: len(values)])


def with_core(near):
    return near + [(flip(a, 1), (r + 1, s)) for a, (r, s) in near]


ALL = (0, 1, 2, 3)


def over_tensor(shard):
    return [shard] + [cross(shard, hop) for hop in (1, 2, 3)]


def gather_staged(own, gates=()):
    over_x = flip(own, 2)
    over_y = flip(own, 4)
    half_x, half_y = late([over_x[:2], over_y[2:]], *gates)
    far_a = flip(half_x, 4)
    far_b = flip(half_y, 2)
    near = [(own, (0, ALL)), (over_x, (2, ALL)), (over_y, (4, ALL))]
    return with_core(near + [(far_a, (6, (0, 1))), (far_b, (6, (2, 3)))])


def add(*values):
    total = values[0].astype(fl)
    for value in values[1:]:
        total = total + value.astype(fl)
    return total


def reduce_core(near, far, gates=(), parts=1):
    got = late([flip(part, 1) for part in far], *gates) if gates else [flip(part, 1) for part in far]
    size, each = 4 // len(far), len(far) * parts
    return [
        add(near[a : a + 4 // each], got[a // size][a % size : a % size + 4 // each]).astype(bf)
        for a in range(0, 4, 4 // each)
    ]


def halves(parts):
    return [jnp.concatenate(parts[:2]), jnp.concatenate(parts[2:])]


def reduce_pair(half, axis, gates=()):
    got = flip(half[1], 2 * axis)
    if gates:
        (got,) = late([got], *gates)
    return [add(half[0][k], got[k]).astype(bf) for k in (0, 1)]


def reduce_chip(pair, axis, gates=()):
    got = flip(pair[1], 2 * axis)
    if gates:
        (got,) = late([got], *gates)
    return [add(pair[0][k : k + 2], got[k : k + 2]).astype(bf) for k in (0, 2)]


def reduce_tensor(plane, gates=()):
    got = cross(plane[1], 1)
    if gates:
        (got,) = late([got], *gates)
    return add(plane[0][0], got[0]), add(plane[0][1], got[1]).astype(bf)


def reduce_last(pair, gates=()):
    got = cross(pair[1], 2)
    if gates:
        (got,) = late([got], *gates)
    return add(pair[0], got)


def gather_plain(shard, extra=None):
    whole = lax.all_gather(lax.all_gather(shard, "dp", axis=0, tiled=True), "tensor", axis=0)
    whole = whole.reshape(4, SLABS, -1, 768)
    if extra is not None:
        extra = lax.all_gather(lax.psum(extra, "dp"), "tensor", axis=0)[:, None].astype(bf)
        extra = jnp.concatenate([extra] + [jnp.zeros_like(extra)] * (SLABS - 1), axis=1)
        whole = jnp.concatenate([whole, extra], axis=2)
    return [(whole[:, r], (r, ALL)) for r in range(SLABS)]


def reduce_plain(near, far, x_last=False):
    order = jnp.array([0, 2, 1, 3])
    grad = jnp.stack([near, jnp.concatenate(far)], axis=1)[:, :, order]
    grad = (grad[order] if x_last else grad).reshape(SLABS, 4, -1, 768).astype(fl)
    whole = grad[:, :, :DEPTH].transpose(1, 0, 2, 3).reshape(4, SLABS * DEPTH, 768)
    part = lax.psum_scatter(whole, "tensor", scatter_dimension=0, tiled=True)
    part = lax.psum_scatter(part[0], "dp", scatter_dimension=0, tiled=True)
    if near.shape[2] == DEPTH:
        return part
    extra = lax.psum_scatter(lax.psum(grad[0, :, DEPTH:], "dp"), "tensor", scatter_dimension=0, tiled=True)[0]
    return jnp.concatenate([part, extra])


def next_row(row, gate):
    (row,) = late([rotate(row)], gate)
    return row


def place_rows(rows, where, after=()):
    return call(place_kernel, "place_rows", [((4,) + rows[0].shape, rows[0].dtype)], where, *rows, after=after)[0]


def moment_update(state, grad):
    moment_one = beta_first * state[1] + (1.0 - beta_first) * grad
    moment_two = beta_second * state[2] + (1.0 - beta_second) * grad * grad
    return jnp.stack([moment_one, moment_two])


def body(
    hidden_in,
    out_grad,
    segment_ids,
    step_count,
    qkv_state,
    qv_bias_state,
    out_state,
    up_state,
    up_bias_state,
    down_state,
    vector_state,
):
    n_dp = lax.axis_size("dp")
    place = lax.axis_index("tensor")
    fast = n_dp == SLABS
    spot = lax.axis_index("dp") if fast else 0
    where = jnp.stack([jnp.int32(spot), (place if fast else 0) * jnp.int32(1)])
    spin = jnp.stack([jnp.int32(0), place * jnp.int32(1)])
    rows, width = qkv_state.shape[1], hidden_in.shape[2]
    cut = 2 * HD

    def spread(value, axis, whole):
        full = jnp.zeros(value.shape[:-1] + (whole,), bf)
        return lax.dynamic_update_slice_in_dim(full, value.astype(bf), axis * value.shape[-1], value.ndim - 1)

    dp = lax.axis_index("dp")
    q, k, v = (qkv_state[0, :, c].astype(bf) for c in range(3))
    o = out_state[0].T.astype(bf)
    attn_shard = jnp.concatenate(
        [q[:, :cut], k[:, :cut], v[:, :cut], q[:, cut:], v[:, cut:], o[:, :cut], k[:, cut:], o[:, cut:]], axis=1
    )
    bq, bv = spread(qv_bias_state[0], dp, HD).reshape(2, 3 * HD)
    gap = jnp.zeros((cut,), bf)
    bias = jnp.concatenate([bq[:cut], gap, bv[:cut], bq[cut:], bv[cut:], gap, gap])
    b_up = spread(up_bias_state[0], dp, LANES).reshape(1, 768)
    extra = jnp.concatenate(
        [spread(vector_state[0], dp, width), bias[None], b_up, jnp.zeros((EXTRA - 8, width), bf)]
    )
    up_shard = up_state[0].astype(bf)
    down_shard = down_state[0].T.astype(bf)

    x = lax.dynamic_index_in_dim(hidden_in, place, 0, keepdims=False)
    dy = lax.dynamic_index_in_dim(out_grad, place, 0, keepdims=False)
    seg = lax.dynamic_index_in_dim(segment_ids, place, 0, keepdims=True)
    seg_col = seg.reshape(-1, 1)
    length = x.shape[0]
    wide = (4, length, 768)
    row_f, row_b = ((length, width), fl), ((length, width), bf)
    whole = ((4, SLABS, DEPTH, 768), bf)
    attn_whole = ((4, SLABS, DEPTH + EXTRA, 768), bf)
    down_outs = [(((n, 4, DEPTH, 768), bf), slab_block) for n in (4, 1, 1, 1, 1)]
    up_outs = [(((n, 4, DEPTH, 768), bf), slab_block) for n in (4, 4)]
    attn_outs = [(((n, 4, DEPTH + EXTRA, 768), bf), slab_block) for n in (4, 1, 1, 1, 1)]
    thin = ((4, 1, 768), fl)

    if fast:
        own = jnp.stack(over_tensor(jnp.concatenate([attn_shard, extra])))
        ffn_slabs = over_tensor(late([jnp.concatenate([up_shard, down_shard])], own)[0])
        attn_pieces = gather_staged(own, ffn_slabs[1:3])
        ffn_own = jnp.stack(late(ffn_slabs, attn_pieces[3][0], attn_pieces[4][0]))
        wait = [ffn_own]
    else:
        attn_pieces = gather_plain(attn_shard, extra)
        ups, downs = gather_plain(up_shard), gather_plain(down_shard)
        ffn_pieces = [(jnp.concatenate([u, d], axis=1), w) for (u, w), (d, _) in zip(ups, downs)]
        wait = []

    def split(pieces):
        return [p for p, _ in pieces], tuple(w for _, w in pieces)

    pieces, plan = split(attn_pieces)
    proj, ctx, lse, attn_w, xhat, rstd, first, vec, b_up = call(
        functools.partial(attn_fwd_kernel, plan), "attn_fwd",
        [(wide, bf), ((4, length, 256), bf), ((4, 3, 1, length), fl), attn_whole, row_f, ((length, LANES), fl), row_b,
         ((8, width), fl), thin],
        where, x, seg, seg_col, *pieces, after=wait,
    )
    if fast:
        ffn_pieces = gather_staged(ffn_own, [vec])
    pieces, plan = split(ffn_pieces)
    out, dr2, act, slope, small_two, up_w, down_w = call(
        functools.partial(ffn_fwd_kernel, plan), "ffn_fwd",
        [row_b, row_f, (wide, bf), (wide, fl), ((3, width), fl), whole, whole],
        where, xhat, first, dy, vec, b_up, *pieces,
    )
    turned = pltpu.VMEM((width, length), bf)
    down_near, *down_far = call_groups(
        down_weights_kernel, "down_weights", down_outs, where, (dr2, whole_block), (act, group_block),
        scratch=[turned],
    )
    dup, b_up_grad = call_groups(
        down_bwd_kernel, "down_bwd", [((wide, bf), group_block), (thin, group_block)],
        where, (dr2, whole_block), (slope, group_block), (down_w, group_block),
    )
    out_one = next_row(out, b_up_grad)
    wait = [out_one]
    if fast:
        down_half = halves(reduce_core(down_near, down_far, [b_up_grad, out_one]))
        wait += down_half
    dr1, dctx, small_one = call(
        up_bwd_kernel, "up_bwd", [row_f, ((4, length, 256), bf), ((3, width), fl)],
        where, dr2, dup, xhat, rstd, vec, up_w, attn_w, after=wait,
    )
    out_two = next_row(out_one, small_one)
    grad_row, dproj, bias_grad = call(
        attn_bwd_kernel, "attn_bwd", [row_b, (wide, bf), thin],
        where, seg, seg_col, proj, lse, dr1, dctx, attn_w, after=[out_two],
        scratch=[pltpu.VMEM((length, width), fl)],
    )
    out_three = next_row(out_two, bias_grad)
    wait = [out_three]
    if fast:
        down_pair = reduce_pair(down_half, 1, [bias_grad])
        wait += down_pair
    attn_near, *attn_far = call_groups(
        attn_weights_kernel, "attn_weights", attn_outs,
        where, (x, whole_block), (dproj, group_block), (ctx, group_block), (dr1, whole_block),
        (bias_grad, group_block), (b_up_grad, group_block), (small_one, whole_block), (small_two, whole_block),
        scratch=[pltpu.VMEM((EXTRA, width), fl), turned, turned], after=wait,
    )
    up_near, *up_far = call_groups(
        up_weights_kernel, "up_weights", up_outs, where, (first, whole_block), (dup, group_block),
        scratch=[turned], after=[bias_grad, attn_near],
    )
    in_one = rotate(grad_row)
    in_two = rotate(in_one)
    in_three = rotate(in_two)
    hidden_out = place_rows([out, out_one, out_two, out_three], spin)
    wait = []
    if fast:
        down_plane = reduce_chip(down_pair, 2)
        attn_far = late(attn_far, *down_plane)
        attn_half = halves(reduce_core(attn_near, attn_far, [up_near, in_one]))
        up_far = late(up_far, in_one, *attn_half)
        up_pair = reduce_pair(reduce_core(up_near, up_far, parts=2), 1, [in_two])
        up_plane = reduce_chip(up_pair, 2)
        attn_pair = reduce_pair(attn_half, 2)
        attn_plane = reduce_chip(attn_pair, 1, [in_three, *up_pair])
        down_last = reduce_tensor(down_plane, [*up_pair, *attn_pair])
        attn_last = reduce_tensor([attn_plane[0]] + late(attn_plane[1:], *up_plane))
        up_last = reduce_tensor(up_plane)
        down_sum = reduce_last(down_last, [attn_last[1], up_last[1]])
        attn_sum = reduce_last(attn_last)
        up_sum = reduce_last(up_last)
        wait = up_plane + attn_plane
    else:
        down_sum = reduce_plain(down_near, down_far, x_last=True)
        up_sum = reduce_plain(up_near, up_far, x_last=True)
        attn_sum = reduce_plain(attn_near, attn_far)

    grad_in = place_rows([grad_row, in_one, in_two, in_three], spin, wait)

    def own_part(value):
        size = value.shape[-1] // n_dp
        return lax.dynamic_slice_in_dim(value, dp * size, size, value.ndim - 1)

    small = attn_sum[rows:]
    gq = jnp.concatenate([small[6, :cut], small[6, 384 : 384 + HD]])
    gv = jnp.concatenate([small[6, 256 : 256 + cut], small[6, 384 + HD : 512]])
    grad_qv = own_part(jnp.stack([gq, gv]).reshape(2, 3, HD))
    grad_b_up = own_part(small[7].reshape(6, LANES))
    grad_vectors = own_part(small[:6])

    gk = [attn_sum[:rows, 128 * n : 128 * (n + 1)] for n in range(6)]
    grad_qkv = jnp.stack(
        [
            jnp.concatenate([gk[0], gk[3][:, :HD]], axis=1),
            jnp.concatenate([gk[1], gk[5][:, :HD]], axis=1),
            jnp.concatenate([gk[2], gk[3][:, HD:]], axis=1),
        ],
        axis=1,
    )
    grad_out = jnp.concatenate([gk[4], gk[5][:, HD:]], axis=1).T
    summed = (grad_qkv, grad_qv, grad_out, up_sum, grad_b_up, down_sum.T, grad_vectors)
    steps_f = step_count[0].astype(fl)
    factor = jnp.minimum(steps_f / warm_steps, (total_steps - steps_f) / (total_steps - warm_steps))
    fix_first = 1.0 - jnp.exp(steps_f * math.log(beta_first))
    fix_second = 1.0 - jnp.exp(steps_f * math.log(beta_second))
    states = (qkv_state, qv_bias_state, out_state, up_state, up_bias_state, down_state, vector_state)
    news = tuple((moment_update(s, g) for s, g in zip(states, summed)))
    plan_out = jnp.stack([factor, fix_first, fix_second])
    return (hidden_out, grad_in, *summed, *news, plan_out)


def solution(mesh):
    return jax.shard_map(
        body,
        mesh=mesh,
        in_specs=(
            P("dp", None, None),
            P("dp", None, None),
            P("dp", None),
            P(),
            P(None, "dp", None, "tensor"),
            P(None, None, "tensor", "dp"),
            P(None, "tensor", "dp"),
            P(None, "dp", "tensor"),
            P(None, "tensor", "dp"),
            P(None, "tensor", "dp"),
            P(None, None, "dp"),
        ),
        out_specs=(
            P("dp", None, None),
            P("dp", None, None),
            P("dp", None, "tensor"),
            P(None, "tensor", "dp"),
            P("tensor", "dp"),
            P("dp", "tensor"),
            P("tensor", "dp"),
            P("tensor", "dp"),
            P(None, "dp"),
            P(None, "dp", None, "tensor"),
            P(None, None, "tensor", "dp"),
            P(None, "tensor", "dp"),
            P(None, "dp", "tensor"),
            P(None, "tensor", "dp"),
            P(None, "tensor", "dp"),
            P(None, None, "dp"),
            P(),
        ),
        check_vma=False,
    )
```

```python
import functools
import math

import jax
import jax.numpy as jnp
from jax import lax
from jax.experimental import pallas as pl
from jax.experimental.pallas import tpu as pltpu
from jax.sharding import PartitionSpec as P

HD = 64
LANES = 128
VMEM_LIMIT = 60 * 1024 * 1024

norm_eps = 1e-05
beta_first = 0.9
beta_second = 0.999
warm_steps = 10000.0
total_steps = 200000.0

bf = jnp.bfloat16
fl = jnp.float32

SLABS = 8
DEPTH = 96
EXTRA = 16


def nt(left, right):
    return lax.dot_general(left, right, (((1,), (1,)), ((), ())), preferred_element_type=fl)


def nn(left, right):
    return lax.dot_general(left, right, (((1,), (0,)), ((), ())), preferred_element_type=fl)


def tn(left, right):
    return lax.dot_general(left, right, (((0,), (0,)), ((), ())), preferred_element_type=fl)


def low_lanes(shape):
    return lax.broadcasted_iota(jnp.int32, shape, 1) < HD


def assemble(where_ref, pieces, plan, *targets):
    for ref, (r, hops) in zip(pieces, plan):
        slab = jnp.bitwise_xor(where_ref[0], r)
        for k, hop in enumerate(hops):
            group = jnp.bitwise_xor(where_ref[1], hop)
            first = 0
            for target in targets:
                last = first + target.shape[2]
                target[group, slab] = ref[k, first:last]
                first = last


def scatter_slabs(where_ref, value, near_ref, far_refs, extra=None, x_last=False):
    chip = jnp.right_shift(where_ref[0], 1)
    core = jnp.bitwise_and(where_ref[0], 1)

    def put(near, far):
        for j in range(SLABS // 2):
            place = jnp.bitwise_xor(chip, j)
            if x_last:
                place = 2 * jnp.bitwise_and(place, 1) + jnp.right_shift(place, 1)

            def store(ref, index, slab):
                ref[index, 0, :DEPTH] = value[DEPTH * slab : DEPTH * (slab + 1)]
                if extra is not None:
                    ref[index, 0, DEPTH:] = extra

            store(near_ref, place, 2 * j + near)
            size = 4 // len(far_refs)
            for k, ref in enumerate(far_refs):
                inside = jnp.logical_and(place >= size * k, place < size * (k + 1))
                index = jnp.clip(place - size * k, 0, size - 1)
                pl.when(inside)(functools.partial(store, ref, index, 2 * j + far))

    pl.when(core == 0)(functools.partial(put, 0, 1))
    pl.when(core == 1)(functools.partial(put, 1, 0))


def matrix(ref, group):
    return ref[group][:, :DEPTH].reshape(SLABS * DEPTH, ref.shape[-1])


def out_matrix(ref, group):
    return ref[group][:, :DEPTH, 512:768].reshape(SLABS * DEPTH, 256)


def attn_fwd_kernel(plan, where_ref, x_ref, seg_row_ref, seg_col_ref, *refs):
    pieces = refs[: len(plan)]
    proj_ref, ctx_ref, lse_ref, weight_ref, xhat_ref, rstd_ref, first_ref, vec_ref, b_up_ref = refs[-9:]
    assemble(where_ref, pieces, plan, weight_ref)
    scale = HD ** (-0.5)
    length = x_ref.shape[0]

    def group_step(g, carry):
        small = jnp.sum(weight_ref[g, :, DEPTH:].astype(fl), axis=0)
        vec_ref[...] = small[:8]
        b_up_ref[g] = small[7:8]
        x = x_ref[...]
        proj = (nn(x, matrix(weight_ref, g)) + small[6:7]).astype(bf)
        proj_ref[g] = proj
        same = seg_col_ref[...] == seg_row_ref[...]
        low = low_lanes((length, LANES))
        none = jnp.zeros((length, LANES), bf)
        parts = [proj[:, LANES * k : LANES * (k + 1)] for k in range(6)]
        turned = [parts[2].T, parts[3].T]
        outs = []
        for head in range(3):
            query = parts[0] if head < 2 else parts[3]
            keys = parts[1] if head < 2 else parts[5]
            value = turned[0][:HD] if head == 0 else turned[head // 2][HD:]
            query = jnp.where(low, none, query) if head == 1 else jnp.where(low, query, none)
            scores = jnp.where(same, nt(keys, query) * scale, -1e30)
            top = jnp.max(scores, axis=0, keepdims=True)
            expd = jnp.exp(scores - top)
            denom = jnp.sum(expd, axis=0, keepdims=True)
            lse_ref[g, head] = top + jnp.log(denom)
            probs = (expd / denom).astype(bf)
            outs.append(nn(value, probs))
        outs.insert(2, jnp.zeros_like(outs[2]))
        ctx_ref[g, :, :LANES] = jnp.concatenate(outs[:2]).T.astype(bf)
        ctx_ref[g, :, LANES:] = jnp.concatenate(outs[2:]).T.astype(bf)
        return carry

    lax.fori_loop(0, 4, group_step, 0)
    total = x_ref[...].astype(fl) + vec_ref[4:5]
    attn = None
    for g in range(4):
        part = nt(ctx_ref[g], out_matrix(weight_ref, g))
        attn = part if attn is None else attn + part
    total = total + attn
    center = total - jnp.mean(total, axis=-1, keepdims=True)
    rstd = lax.rsqrt(jnp.mean(center * center, axis=-1, keepdims=True) + norm_eps)
    xhat = center * rstd
    xhat_ref[...] = xhat
    rstd_ref[...] = jnp.broadcast_to(rstd, rstd_ref.shape)
    first_ref[...] = (xhat * vec_ref[0:1] + vec_ref[1:2]).astype(bf)


def ffn_fwd_kernel(plan, where_ref, xhat_ref, first_ref, dy_ref, vec_ref, b_up_ref, *refs):
    pieces, refs = refs[: len(plan)], refs[len(plan) :]
    out_ref, dr2_ref, act_ref, slope_ref, small_ref, up_w_ref, down_w_ref = refs
    assemble(where_ref, pieces, plan, up_w_ref, down_w_ref)

    def step(g, carry):
        up = nn(first_ref[...], matrix(up_w_ref, g)) + b_up_ref[g]
        half = 0.5 * (1.0 + lax.erf(up * 0.7071067811865476))
        act_ref[g] = (up * half).astype(bf)
        slope_ref[g] = half + up * (jnp.exp(-0.5 * up * up) * 0.3989422804014327)
        return carry

    lax.fori_loop(0, 4, step, 0)
    ffn = None
    for g in range(4):
        part = nt(act_ref[g], matrix(down_w_ref, g))
        ffn = part if ffn is None else ffn + part
    first = xhat_ref[...] * vec_ref[0:1] + vec_ref[1:2]
    total = first + ffn + vec_ref[5:6]
    center = total - jnp.mean(total, axis=-1, keepdims=True)
    rstd = lax.rsqrt(jnp.mean(center * center, axis=-1, keepdims=True) + norm_eps)
    xhat = center * rstd
    out_ref[...] = (xhat * vec_ref[2:3] + vec_ref[3:4]).astype(bf)
    dy = dy_ref[...].astype(fl)
    small_ref[0:1] = jnp.sum(dy * xhat, axis=0, keepdims=True)
    small_ref[1:2] = jnp.sum(dy, axis=0, keepdims=True)
    dxhat = dy * vec_ref[2:3]
    dr2 = rstd * (
        dxhat
        - jnp.mean(dxhat, axis=-1, keepdims=True)
        - xhat * jnp.mean(dxhat * xhat, axis=-1, keepdims=True)
    )
    dr2_ref[...] = dr2
    small_ref[2:3] = jnp.sum(dr2, axis=0, keepdims=True)


def down_weights_kernel(where_ref, dr2_ref, act_ref, near_ref, *refs):
    *far_refs, turned_ref = refs

    @pl.when(pl.program_id(0) == 0)
    def _():
        turned_ref[...] = dr2_ref[...].astype(bf).T

    scatter_slabs(where_ref, nn(turned_ref[...], act_ref[0]).astype(bf), near_ref, far_refs, x_last=True)


def down_bwd_kernel(where_ref, dr2_ref, slope_ref, weight_ref, dup_ref, b_up_ref):
    dup = (nn(dr2_ref[...].astype(bf), matrix(weight_ref, 0)) * slope_ref[0]).astype(bf)
    dup_ref[0] = dup
    b_up_ref[0] = jnp.sum(dup.astype(fl), axis=0, keepdims=True)


def up_weights_kernel(where_ref, first_ref, dup_ref, near_ref, *refs):
    *far_refs, turned_ref = refs

    @pl.when(pl.program_id(0) == 0)
    def _():
        turned_ref[...] = first_ref[...].T

    scatter_slabs(where_ref, nn(turned_ref[...], dup_ref[0]).astype(bf), near_ref, far_refs, x_last=True)


def up_bwd_kernel(where_ref, dr2_ref, dup_ref, xhat_ref, rstd_ref, vec_ref, weight_ref, attn_weight_ref, *refs):
    dr1_ref, dctx_ref, small_ref = refs[-3:]
    feed = None
    for g in range(4):
        part = nt(dup_ref[g], matrix(weight_ref, g))
        feed = part if feed is None else feed + part
    dfirst = dr2_ref[...] + feed.astype(bf).astype(fl)
    xhat = xhat_ref[...]
    small_ref[0:1] = jnp.sum(dfirst * xhat, axis=0, keepdims=True)
    small_ref[1:2] = jnp.sum(dfirst, axis=0, keepdims=True)
    dxhat = dfirst * vec_ref[0:1]
    dr1 = rstd_ref[:, 0:1] * (
        dxhat
        - jnp.mean(dxhat, axis=-1, keepdims=True)
        - xhat * jnp.mean(dxhat * xhat, axis=-1, keepdims=True)
    )
    dr1_ref[...] = dr1
    small_ref[2:3] = jnp.sum(dr1, axis=0, keepdims=True)
    dattn = dr1.astype(bf)
    for g in range(4):
        dctx_ref[g] = nn(dattn, out_matrix(attn_weight_ref, g)).astype(bf)


def attn_bwd_kernel(where_ref, seg_row_ref, seg_col_ref, proj_ref, lse_ref, dr1_ref, dctx_ref, weight_ref, *refs):
    grad_in_ref, dproj_ref, bias_ref, back_ref = refs[-4:]
    scale = HD ** (-0.5)
    length = dr1_ref.shape[0]
    back_ref[...] = jnp.zeros_like(back_ref)

    def step(g, carry):
        same = seg_col_ref[...] == seg_row_ref[...]
        low = low_lanes((length, LANES))
        none = jnp.zeros((length, LANES), bf)
        parts = [proj_ref[g, :, LANES * k : LANES * (k + 1)] for k in range(6)]
        dctx = [dctx_ref[g, :, :LANES], dctx_ref[g, :, LANES:]]
        turned = [parts[1].T, parts[5].T]
        dq, dk, dv = [], [], []
        for head in range(3):
            query = parts[0] if head < 2 else parts[3]
            keys = parts[1] if head < 2 else parts[5]
            value = parts[2] if head < 2 else parts[3]
            dout = dctx[0] if head < 2 else dctx[1]
            query_in = jnp.where(low, none, query) if head == 1 else jnp.where(low, query, none)
            dout_in = jnp.where(low, dout, none) if head == 0 else jnp.where(low, none, dout)
            scores = jnp.where(same, nt(keys, query_in) * scale, -1e30)
            probs = jnp.exp(scores - lse_ref[g, head])
            dprobs = nt(value, dout_in)
            dv.append(nn(probs.astype(bf), dout))
            row_dot = jnp.sum(probs * dprobs, axis=0, keepdims=True)
            dscores = (probs * (dprobs - row_dot)).astype(bf)
            keys_turned = turned[0][HD:] if head == 1 else turned[head // 2][:HD]
            dq.append(nn(keys_turned, dscores) * scale)
            dk.append(nn(dscores, query) * scale)
        dq.append(jnp.zeros_like(dq[2]))
        dq_near, dq_far = jnp.concatenate(dq[:2]).T, jnp.concatenate(dq[2:]).T
        dproj = jnp.concatenate(
            [
                dq_near.astype(bf),
                jnp.where(low, dk[0], dk[1]).astype(bf),
                jnp.where(low, dv[0], dv[1]).astype(bf),
                jnp.where(low, dq_far, dv[2]).astype(bf),
                none,
                jnp.where(low, dk[2].astype(bf), none),
            ],
            axis=1,
        )
        dproj_ref[g] = dproj
        bias_ref[g] = jnp.sum(dproj.astype(fl), axis=0, keepdims=True)
        back_ref[...] += nt(dproj, matrix(weight_ref, g))
        return carry

    lax.fori_loop(0, 4, step, 0)
    dr1 = dr1_ref[...]
    grad_in_ref[...] = (dr1 + back_ref[...].astype(bf).astype(fl)).astype(bf)


def attn_weights_kernel(where_ref, x_ref, dproj_ref, ctx_ref, dr1_ref, bias_ref, b_up_ref, one_ref, two_ref,
                        near_ref, *refs):
    *far_refs, small_ref, x_turned_ref, dr1_turned_ref = refs

    @pl.when(pl.program_id(0) == 0)
    def _():
        small_ref[...] = jnp.zeros_like(small_ref)
        small_ref[0:2] = one_ref[0:2]
        small_ref[2:4] = two_ref[0:2]
        small_ref[4:5] = one_ref[2:3]
        small_ref[5:6] = two_ref[2:3]
        x_turned_ref[...] = x_ref[...].T
        dr1_turned_ref[...] = dr1_ref[...].astype(bf).T

    small_ref[6:7] = bias_ref[0]
    small_ref[7:8] = b_up_ref[0]
    main = nn(x_turned_ref[...], dproj_ref[0])
    side = nn(dr1_turned_ref[...], ctx_ref[0])
    whole = jnp.concatenate([main[:, :512], main[:, 512:] + side], axis=1).astype(bf)
    scatter_slabs(where_ref, whole, near_ref, far_refs, small_ref[...].astype(bf))


def place_kernel(where_ref, *refs):
    out_ref = refs[-1]
    for d, ref in enumerate(refs[:-1]):
        out_ref[jnp.bitwise_and(where_ref[1] + 4 - d, 3)] = ref[...]


smem = pl.BlockSpec(memory_space=pltpu.SMEM)
vmem = pl.BlockSpec(memory_space=pltpu.VMEM)


def call(kernel, name, outs, where, *args, scratch=(), after=()):
    if after:
        (where,) = late([where], *after)
    return pl.pallas_call(
        kernel,
        name=name,
        out_shape=[jax.ShapeDtypeStruct(s, d) for s, d in outs],
        in_specs=[smem] + [vmem] * len(args),
        out_specs=[vmem] * len(outs),
        scratch_shapes=list(scratch),
        compiler_params=pltpu.CompilerParams(vmem_limit_bytes=VMEM_LIMIT),
        cost_estimate=pl.CostEstimate(flops=COST, bytes_accessed=COST, transcendentals=0),
    )(where, *args)


COST = 1000


def whole_block(shape):
    return pl.BlockSpec(shape, lambda g, where: (0,) * len(shape))


def group_block(shape):
    return pl.BlockSpec((1, *shape[1:]), lambda g, where: (g,) + (0,) * (len(shape) - 1))


def slab_block(shape):
    def index(g, where):
        hop = jnp.bitwise_xor(g, where[1])
        return (0, 2 * jnp.bitwise_and(hop, 1) + jnp.right_shift(hop, 1), 0, 0)

    return pl.BlockSpec((shape[0], 1, *shape[2:]), index)


def call_groups(kernel, name, outs, where, *args, scratch=(), after=()):
    if after:
        (where,) = late([where], *after)
    return pl.pallas_call(
        kernel,
        name=name,
        out_shape=[jax.ShapeDtypeStruct(s, d) for (s, d), _ in outs],
        grid_spec=pltpu.PrefetchScalarGridSpec(
            num_scalar_prefetch=1,
            grid=(4,),
            in_specs=[block(a.shape) for a, block in args],
            out_specs=[block(s) for (s, _), block in outs],
            scratch_shapes=list(scratch),
        ),
        compiler_params=pltpu.CompilerParams(
            vmem_limit_bytes=VMEM_LIMIT, dimension_semantics=("arbitrary",)
        ),
        cost_estimate=pl.CostEstimate(flops=COST, bytes_accessed=COST, transcendentals=0),
    )(where, *[a for a, _ in args])


def flip(value, bits):
    n = lax.axis_size("dp")
    return lax.ppermute(value, "dp", [(k, k ^ bits) for k in range(n)])


def cross(value, bits):
    return lax.ppermute(value, "tensor", [(k, k ^ bits) for k in range(4)])


def rotate(value):
    return lax.ppermute(value, "tensor", [(k, (k + 1) % 4) for k in range(4)])


def late(values, *gates):
    return list(lax.optimization_barrier((*values, *gates))[: len(values)])


def with_core(near):
    return near + [(flip(a, 1), (r + 1, s)) for a, (r, s) in near]


ALL = (0, 1, 2, 3)


def over_tensor(shard):
    return [shard] + [cross(shard, hop) for hop in (1, 2, 3)]


def gather_staged(own, gates=()):
    over_x = flip(own, 2)
    over_y = flip(own, 4)
    half_x, half_y = late([over_x[:2], over_y[2:]], *gates)
    far_a = flip(half_x, 4)
    far_b = flip(half_y, 2)
    near = [(own, (0, ALL)), (over_x, (2, ALL)), (over_y, (4, ALL))]
    return with_core(near + [(far_a, (6, (0, 1))), (far_b, (6, (2, 3)))])


def add(*values):
    total = values[0].astype(fl)
    for value in values[1:]:
        total = total + value.astype(fl)
    return total


def reduce_core(near, far, gates=(), parts=1):
    got = late([flip(part, 1) for part in far], *gates) if gates else [flip(part, 1) for part in far]
    size, each = 4 // len(far), len(far) * parts
    return [
        add(near[a : a + 4 // each], got[a // size][a % size : a % size + 4 // each]).astype(bf)
        for a in range(0, 4, 4 // each)
    ]


def halves(parts):
    return [jnp.concatenate(parts[:2]), jnp.concatenate(parts[2:])]


def reduce_pair(half, axis, gates=()):
    got = flip(half[1], 2 * axis)
    if gates:
        (got,) = late([got], *gates)
    return [add(half[0][k], got[k]).astype(bf) for k in (0, 1)]


def reduce_chip(pair, axis, gates=()):
    got = flip(pair[1], 2 * axis)
    if gates:
        (got,) = late([got], *gates)
    return [add(pair[0][k : k + 2], got[k : k + 2]).astype(bf) for k in (0, 2)]


def reduce_some(sums, gates):
    one, two, three, four = [part[0] for part in sums]
    over_x = flip(jnp.stack([two[:2], four[:2]]), 2)
    over_y = flip(jnp.stack([three[2:], four[2:]]), 4)
    over_x, over_y = late([over_x, over_y], *gates)
    pairs = ((one[:2], over_x[0]), (three[:2], over_x[1]), (one[2:], over_y[0]), (two[2:], over_y[1]))
    return [add(*pair).astype(bf) for pair in pairs]


def reduce_rest(some, gates):
    over_y, over_x = late([flip(some[1], 4), flip(some[3], 2)], *gates)
    return [add(some[0], over_y).astype(bf), add(some[2], over_x).astype(bf)]


def reduce_tensor(plane, gates=()):
    got = cross(plane[1], 1)
    if gates:
        (got,) = late([got], *gates)
    return add(plane[0][0], got[0]), add(plane[0][1], got[1]).astype(bf)


def reduce_last(pair, gates=()):
    got = cross(pair[1], 2)
    if gates:
        (got,) = late([got], *gates)
    return add(pair[0], got)


def gather_plain(shard, extra=None):
    whole = lax.all_gather(lax.all_gather(shard, "dp", axis=0, tiled=True), "tensor", axis=0)
    whole = whole.reshape(4, SLABS, -1, 768)
    if extra is not None:
        extra = lax.all_gather(lax.psum(extra, "dp"), "tensor", axis=0)[:, None].astype(bf)
        extra = jnp.concatenate([extra] + [jnp.zeros_like(extra)] * (SLABS - 1), axis=1)
        whole = jnp.concatenate([whole, extra], axis=2)
    return [(whole[:, r], (r, ALL)) for r in range(SLABS)]


def reduce_plain(near, far, x_last=False):
    order = jnp.array([0, 2, 1, 3])
    grad = jnp.stack([near, jnp.concatenate(far)], axis=1)[:, :, order]
    grad = (grad[order] if x_last else grad).reshape(SLABS, 4, -1, 768).astype(fl)
    whole = grad[:, :, :DEPTH].transpose(1, 0, 2, 3).reshape(4, SLABS * DEPTH, 768)
    part = lax.psum_scatter(whole, "tensor", scatter_dimension=0, tiled=True)
    part = lax.psum_scatter(part[0], "dp", scatter_dimension=0, tiled=True)
    if near.shape[2] == DEPTH:
        return part
    extra = lax.psum_scatter(lax.psum(grad[0, :, DEPTH:], "dp"), "tensor", scatter_dimension=0, tiled=True)[0]
    return jnp.concatenate([part, extra])


def next_row(row, gate):
    (row,) = late([rotate(row)], gate)
    return row


def place_rows(rows, where, after=()):
    return call(place_kernel, "place_rows", [((4,) + rows[0].shape, rows[0].dtype)], where, *rows, after=after)[0]


def moment_update(state, grad):
    moment_one = beta_first * state[1] + (1.0 - beta_first) * grad
    moment_two = beta_second * state[2] + (1.0 - beta_second) * grad * grad
    return jnp.stack([moment_one, moment_two])


def body(
    hidden_in,
    out_grad,
    segment_ids,
    step_count,
    qkv_state,
    qv_bias_state,
    out_state,
    up_state,
    up_bias_state,
    down_state,
    vector_state,
):
    n_dp = lax.axis_size("dp")
    place = lax.axis_index("tensor")
    fast = n_dp == SLABS
    spot = lax.axis_index("dp") if fast else 0
    where = jnp.stack([jnp.int32(spot), (place if fast else 0) * jnp.int32(1)])
    spin = jnp.stack([jnp.int32(0), place * jnp.int32(1)])
    rows, width = qkv_state.shape[1], hidden_in.shape[2]
    cut = 2 * HD

    def spread(value, axis, whole):
        full = jnp.zeros(value.shape[:-1] + (whole,), bf)
        return lax.dynamic_update_slice_in_dim(full, value.astype(bf), axis * value.shape[-1], value.ndim - 1)

    dp = lax.axis_index("dp")
    q, k, v = (qkv_state[0, :, c].astype(bf) for c in range(3))
    o = out_state[0].T.astype(bf)
    attn_shard = jnp.concatenate(
        [q[:, :cut], k[:, :cut], v[:, :cut], q[:, cut:], v[:, cut:], o[:, :cut], k[:, cut:], o[:, cut:]], axis=1
    )
    bq, bv = spread(qv_bias_state[0], dp, HD).reshape(2, 3 * HD)
    gap = jnp.zeros((cut,), bf)
    bias = jnp.concatenate([bq[:cut], gap, bv[:cut], bq[cut:], bv[cut:], gap, gap])
    b_up = spread(up_bias_state[0], dp, LANES).reshape(1, 768)
    extra = jnp.concatenate(
        [spread(vector_state[0], dp, width), bias[None], b_up, jnp.zeros((EXTRA - 8, width), bf)]
    )
    up_shard = up_state[0].astype(bf)
    down_shard = down_state[0].T.astype(bf)

    x = lax.dynamic_index_in_dim(hidden_in, place, 0, keepdims=False)
    dy = lax.dynamic_index_in_dim(out_grad, place, 0, keepdims=False)
    seg = lax.dynamic_index_in_dim(segment_ids, place, 0, keepdims=True)
    seg_col = seg.reshape(-1, 1)
    length = x.shape[0]
    wide = (4, length, 768)
    row_f, row_b = ((length, width), fl), ((length, width), bf)
    whole = ((4, SLABS, DEPTH, 768), bf)
    attn_whole = ((4, SLABS, DEPTH + EXTRA, 768), bf)
    down_outs = [(((n, 4, DEPTH, 768), bf), slab_block) for n in (4, 1, 1, 1, 1)]
    up_outs = [(((n, 4, DEPTH, 768), bf), slab_block) for n in (4, 4)]
    attn_outs = [(((n, 4, DEPTH + EXTRA, 768), bf), slab_block) for n in (4, 4)]
    thin = ((4, 1, 768), fl)

    if fast:
        own = jnp.stack(over_tensor(jnp.concatenate([attn_shard, extra])))
        ffn_slabs = over_tensor(late([jnp.concatenate([up_shard, down_shard])], own)[0])
        attn_pieces = gather_staged(own, ffn_slabs[1:3])
        ffn_own = jnp.stack(late(ffn_slabs, attn_pieces[3][0], attn_pieces[4][0]))
        wait = [ffn_own]
    else:
        attn_pieces = gather_plain(attn_shard, extra)
        ups, downs = gather_plain(up_shard), gather_plain(down_shard)
        ffn_pieces = [(jnp.concatenate([u, d], axis=1), w) for (u, w), (d, _) in zip(ups, downs)]
        wait = []

    def split(pieces):
        return [p for p, _ in pieces], tuple(w for _, w in pieces)

    pieces, plan = split(attn_pieces)
    proj, ctx, lse, attn_w, xhat, rstd, first, vec, b_up = call(
        functools.partial(attn_fwd_kernel, plan), "attn_fwd",
        [(wide, bf), ((4, length, 256), bf), ((4, 3, 1, length), fl), attn_whole, row_f, ((length, LANES), fl), row_b,
         ((8, width), fl), thin],
        where, x, seg, seg_col, *pieces, after=wait,
    )
    if fast:
        ffn_pieces = gather_staged(ffn_own, [vec])
    pieces, plan = split(ffn_pieces)
    out, dr2, act, slope, small_two, up_w, down_w = call(
        functools.partial(ffn_fwd_kernel, plan), "ffn_fwd",
        [row_b, row_f, (wide, bf), (wide, fl), ((3, width), fl), whole, whole],
        where, xhat, first, dy, vec, b_up, *pieces,
    )
    turned = pltpu.VMEM((width, length), bf)
    down_near, *down_far = call_groups(
        down_weights_kernel, "down_weights", down_outs, where, (dr2, whole_block), (act, group_block),
        scratch=[turned],
    )
    dup, b_up_grad = call_groups(
        down_bwd_kernel, "down_bwd", [((wide, bf), group_block), (thin, group_block)],
        where, (dr2, whole_block), (slope, group_block), (down_w, group_block),
    )
    out_one = next_row(out, b_up_grad)
    wait = [out_one]
    if fast:
        down_half = halves(reduce_core(down_near, down_far, [b_up_grad, out_one]))
        wait += down_half
    dr1, dctx, small_one = call(
        up_bwd_kernel, "up_bwd", [row_f, ((4, length, 256), bf), ((3, width), fl)],
        where, dr2, dup, xhat, rstd, vec, up_w, attn_w, after=wait,
    )
    up_near, *up_far = call_groups(
        up_weights_kernel, "up_weights", up_outs, where, (first, whole_block), (dup, group_block),
        scratch=[turned], after=[small_one],
    )
    out_two = next_row(out_one, up_near)
    grad_row, dproj, bias_grad = call(
        attn_bwd_kernel, "attn_bwd", [row_b, (wide, bf), thin],
        where, seg, seg_col, proj, lse, dr1, dctx, attn_w, after=[out_two, up_near],
        scratch=[pltpu.VMEM((length, width), fl)],
    )
    out_three = next_row(out_two, bias_grad)
    wait = [out_three]
    if fast:
        down_pair = reduce_pair(down_half, 1, [bias_grad])
        wait += down_pair
    attn_near, *attn_far = call_groups(
        attn_weights_kernel, "attn_weights", attn_outs,
        where, (x, whole_block), (dproj, group_block), (ctx, group_block), (dr1, whole_block),
        (bias_grad, group_block), (b_up_grad, group_block), (small_one, whole_block), (small_two, whole_block),
        scratch=[pltpu.VMEM((EXTRA, width), fl), turned, turned], after=wait,
    )
    in_one = rotate(grad_row)
    in_two = rotate(in_one)
    in_three = rotate(in_two)
    hidden_out = place_rows([out, out_one, out_two, out_three], spin)
    wait = []
    if fast:
        down_plane = reduce_chip(down_pair, 2, [attn_near])
        attn_far = late(attn_far, in_one, *down_plane)
        up_half = reduce_core(up_near, late(up_far, in_one), parts=2)
        attn_sums = reduce_core(attn_near, attn_far, parts=4)
        up_pair = reduce_pair(up_half, 1, attn_sums)
        attn_some = reduce_some(attn_sums, [in_two])
        up_plane = reduce_chip(up_pair, 2, attn_some)
        attn_plane = reduce_rest(attn_some, [in_three])
        down_last = reduce_tensor(down_plane, [*up_pair, *attn_some])
        attn_last = reduce_tensor([attn_plane[0]] + late(attn_plane[1:], *up_plane))
        up_last = reduce_tensor(up_plane)
        down_sum = reduce_last(down_last, [attn_last[1], up_last[1]])
        attn_sum = reduce_last(attn_last)
        up_sum = reduce_last(up_last)
        wait = up_plane + attn_plane
    else:
        down_sum = reduce_plain(down_near, down_far, x_last=True)
        up_sum = reduce_plain(up_near, up_far, x_last=True)
        attn_sum = reduce_plain(attn_near, attn_far)

    grad_in = place_rows([grad_row, in_one, in_two, in_three], spin, wait)

    def own_part(value):
        size = value.shape[-1] // n_dp
        return lax.dynamic_slice_in_dim(value, dp * size, size, value.ndim - 1)

    small = attn_sum[rows:]
    gq = jnp.concatenate([small[6, :cut], small[6, 384 : 384 + HD]])
    gv = jnp.concatenate([small[6, 256 : 256 + cut], small[6, 384 + HD : 512]])
    grad_qv = own_part(jnp.stack([gq, gv]).reshape(2, 3, HD))
    grad_b_up = own_part(small[7].reshape(6, LANES))
    grad_vectors = own_part(small[:6])

    gk = [attn_sum[:rows, 128 * n : 128 * (n + 1)] for n in range(6)]
    grad_qkv = jnp.stack(
        [
            jnp.concatenate([gk[0], gk[3][:, :HD]], axis=1),
            jnp.concatenate([gk[1], gk[5][:, :HD]], axis=1),
            jnp.concatenate([gk[2], gk[3][:, HD:]], axis=1),
        ],
        axis=1,
    )
    grad_out = jnp.concatenate([gk[4], gk[5][:, HD:]], axis=1).T
    summed = (grad_qkv, grad_qv, grad_out, up_sum, grad_b_up, down_sum.T, grad_vectors)
    steps_f = step_count[0].astype(fl)
    factor = jnp.minimum(steps_f / warm_steps, (total_steps - steps_f) / (total_steps - warm_steps))
    fix_first = 1.0 - jnp.exp(steps_f * math.log(beta_first))
    fix_second = 1.0 - jnp.exp(steps_f * math.log(beta_second))
    states = (qkv_state, qv_bias_state, out_state, up_state, up_bias_state, down_state, vector_state)
    news = tuple((moment_update(s, g) for s, g in zip(states, summed)))
    plan_out = jnp.stack([factor, fix_first, fix_second])
    return (hidden_out, grad_in, *summed, *news, plan_out)


def solution(mesh):
    return jax.shard_map(
        body,
        mesh=mesh,
        in_specs=(
            P("dp", None, None),
            P("dp", None, None),
            P("dp", None),
            P(),
            P(None, "dp", None, "tensor"),
            P(None, None, "tensor", "dp"),
            P(None, "tensor", "dp"),
            P(None, "dp", "tensor"),
            P(None, "tensor", "dp"),
            P(None, "tensor", "dp"),
            P(None, None, "dp"),
        ),
        out_specs=(
            P("dp", None, None),
            P("dp", None, None),
            P("dp", None, "tensor"),
            P(None, "tensor", "dp"),
            P("tensor", "dp"),
            P("dp", "tensor"),
            P("tensor", "dp"),
            P("tensor", "dp"),
            P(None, "dp"),
            P(None, "dp", None, "tensor"),
            P(None, None, "tensor", "dp"),
            P(None, "tensor", "dp"),
            P(None, "dp", "tensor"),
            P(None, "tensor", "dp"),
            P(None, "tensor", "dp"),
            P(None, None, "dp"),
            P(),
        ),
        check_vma=False,
    )
```

```python
import functools
import math

import jax
import jax.numpy as jnp
from jax import lax
from jax.experimental import pallas as pl
from jax.experimental.pallas import tpu as pltpu
from jax.sharding import PartitionSpec as P

HD = 64
LANES = 128
VMEM_LIMIT = 60 * 1024 * 1024

norm_eps = 1e-05
beta_first = 0.9
beta_second = 0.999
warm_steps = 10000.0
total_steps = 200000.0

bf = jnp.bfloat16
fl = jnp.float32

SLABS = 8
DEPTH = 96
EXTRA = 16


def nt(left, right):
    return lax.dot_general(left, right, (((1,), (1,)), ((), ())), preferred_element_type=fl)


def nn(left, right):
    return lax.dot_general(left, right, (((1,), (0,)), ((), ())), preferred_element_type=fl)


def tn(left, right):
    return lax.dot_general(left, right, (((0,), (0,)), ((), ())), preferred_element_type=fl)


def low_lanes(shape):
    return lax.broadcasted_iota(jnp.int32, shape, 1) < HD


def assemble(where_ref, pieces, plan, *targets):
    for ref, (r, hops) in zip(pieces, plan):
        slab = jnp.bitwise_xor(where_ref[0], r)
        for k, hop in enumerate(hops):
            group = jnp.bitwise_xor(where_ref[1], hop)
            first = 0
            for target in targets:
                last = first + target.shape[2]
                target[group, slab] = ref[k, first:last]
                first = last


def scatter_slabs(where_ref, value, near_ref, far_refs, extra=None, x_last=False):
    chip = jnp.right_shift(where_ref[0], 1)
    core = jnp.bitwise_and(where_ref[0], 1)

    def put(near, far):
        for j in range(SLABS // 2):
            place = jnp.bitwise_xor(chip, j)
            if x_last:
                place = 2 * jnp.bitwise_and(place, 1) + jnp.right_shift(place, 1)

            def store(ref, index, slab):
                ref[index, 0, :DEPTH] = value[DEPTH * slab : DEPTH * (slab + 1)]
                if extra is not None:
                    ref[index, 0, DEPTH:] = extra

            store(near_ref, place, 2 * j + near)
            size = 4 // len(far_refs)
            for k, ref in enumerate(far_refs):
                inside = jnp.logical_and(place >= size * k, place < size * (k + 1))
                index = jnp.clip(place - size * k, 0, size - 1)
                pl.when(inside)(functools.partial(store, ref, index, 2 * j + far))

    pl.when(core == 0)(functools.partial(put, 0, 1))
    pl.when(core == 1)(functools.partial(put, 1, 0))


def matrix(ref, group):
    return ref[group][:, :DEPTH].reshape(SLABS * DEPTH, ref.shape[-1])


def out_matrix(ref, group):
    return ref[group][:, :DEPTH, 512:768].reshape(SLABS * DEPTH, 256)


def attn_fwd_kernel(plan, where_ref, x_ref, seg_row_ref, seg_col_ref, *refs):
    pieces = refs[: len(plan)]
    proj_ref, ctx_ref, lse_ref, weight_ref, xhat_ref, rstd_ref, first_ref, vec_ref, b_up_ref = refs[-9:]
    assemble(where_ref, pieces, plan, weight_ref)
    scale = HD ** (-0.5)
    length = x_ref.shape[0]

    def group_step(g, carry):
        small = jnp.sum(weight_ref[g, :, DEPTH:].astype(fl), axis=0)
        vec_ref[...] = small[:8]
        b_up_ref[g] = small[7:8]
        x = x_ref[...]
        proj = (nn(x, matrix(weight_ref, g)) + small[6:7]).astype(bf)
        proj_ref[g] = proj
        same = seg_col_ref[...] == seg_row_ref[...]
        low = low_lanes((length, LANES))
        none = jnp.zeros((length, LANES), bf)
        parts = [proj[:, LANES * k : LANES * (k + 1)] for k in range(6)]
        turned = [parts[2].T, parts[3].T]
        outs = []
        for head in range(3):
            query = parts[0] if head < 2 else parts[3]
            keys = parts[1] if head < 2 else parts[5]
            value = turned[0][:HD] if head == 0 else turned[head // 2][HD:]
            query = jnp.where(low, none, query) if head == 1 else jnp.where(low, query, none)
            scores = jnp.where(same, nt(keys, query) * scale, -1e30)
            top = jnp.max(scores, axis=0, keepdims=True)
            expd = jnp.exp(scores - top)
            denom = jnp.sum(expd, axis=0, keepdims=True)
            lse_ref[g, head] = top + jnp.log(denom)
            probs = (expd / denom).astype(bf)
            outs.append(nn(value, probs))
        outs.insert(2, jnp.zeros_like(outs[2]))
        ctx_ref[g, :, :LANES] = jnp.concatenate(outs[:2]).T.astype(bf)
        ctx_ref[g, :, LANES:] = jnp.concatenate(outs[2:]).T.astype(bf)
        return carry

    lax.fori_loop(0, 4, group_step, 0)
    total = x_ref[...].astype(fl) + vec_ref[4:5]
    attn = None
    for g in range(4):
        part = nt(ctx_ref[g], out_matrix(weight_ref, g))
        attn = part if attn is None else attn + part
    total = total + attn
    center = total - jnp.mean(total, axis=-1, keepdims=True)
    rstd = lax.rsqrt(jnp.mean(center * center, axis=-1, keepdims=True) + norm_eps)
    xhat = center * rstd
    xhat_ref[...] = xhat
    rstd_ref[...] = jnp.broadcast_to(rstd, rstd_ref.shape)
    first_ref[...] = (xhat * vec_ref[0:1] + vec_ref[1:2]).astype(bf)


def ffn_fwd_kernel(plan, where_ref, xhat_ref, first_ref, dy_ref, vec_ref, b_up_ref, *refs):
    pieces, refs = refs[: len(plan)], refs[len(plan) :]
    out_ref, dr2_ref, act_ref, slope_ref, small_ref, up_w_ref, down_w_ref = refs
    assemble(where_ref, pieces, plan, up_w_ref, down_w_ref)

    def step(g, carry):
        up = nn(first_ref[...], matrix(up_w_ref, g)) + b_up_ref[g]
        half = 0.5 * (1.0 + lax.erf(up * 0.7071067811865476))
        act_ref[g] = (up * half).astype(bf)
        slope_ref[g] = half + up * (jnp.exp(-0.5 * up * up) * 0.3989422804014327)
        return carry

    lax.fori_loop(0, 4, step, 0)
    ffn = None
    for g in range(4):
        part = nt(act_ref[g], matrix(down_w_ref, g))
        ffn = part if ffn is None else ffn + part
    first = xhat_ref[...] * vec_ref[0:1] + vec_ref[1:2]
    total = first + ffn + vec_ref[5:6]
    center = total - jnp.mean(total, axis=-1, keepdims=True)
    rstd = lax.rsqrt(jnp.mean(center * center, axis=-1, keepdims=True) + norm_eps)
    xhat = center * rstd
    out_ref[...] = (xhat * vec_ref[2:3] + vec_ref[3:4]).astype(bf)
    dy = dy_ref[...].astype(fl)
    small_ref[0:1] = jnp.sum(dy * xhat, axis=0, keepdims=True)
    small_ref[1:2] = jnp.sum(dy, axis=0, keepdims=True)
    dxhat = dy * vec_ref[2:3]
    dr2 = rstd * (
        dxhat
        - jnp.mean(dxhat, axis=-1, keepdims=True)
        - xhat * jnp.mean(dxhat * xhat, axis=-1, keepdims=True)
    )
    dr2_ref[...] = dr2
    small_ref[2:3] = jnp.sum(dr2, axis=0, keepdims=True)


def down_weights_kernel(where_ref, dr2_ref, act_ref, near_ref, *refs):
    *far_refs, turned_ref = refs

    @pl.when(pl.program_id(0) == 0)
    def _():
        turned_ref[...] = dr2_ref[...].astype(bf).T

    scatter_slabs(where_ref, nn(turned_ref[...], act_ref[0]).astype(bf), near_ref, far_refs, x_last=True)


def down_bwd_kernel(where_ref, dr2_ref, slope_ref, weight_ref, dup_ref, b_up_ref):
    dup = (nn(dr2_ref[...].astype(bf), matrix(weight_ref, 0)) * slope_ref[0]).astype(bf)
    dup_ref[0] = dup
    b_up_ref[0] = jnp.sum(dup.astype(fl), axis=0, keepdims=True)


def up_weights_kernel(where_ref, first_ref, dup_ref, near_ref, *refs):
    *far_refs, turned_ref = refs

    @pl.when(pl.program_id(0) == 0)
    def _():
        turned_ref[...] = first_ref[...].T

    scatter_slabs(where_ref, nn(turned_ref[...], dup_ref[0]).astype(bf), near_ref, far_refs, x_last=True)


def up_bwd_kernel(where_ref, dr2_ref, dup_ref, xhat_ref, rstd_ref, vec_ref, weight_ref, attn_weight_ref, *refs):
    dr1_ref, dctx_ref, small_ref = refs[-3:]
    feed = None
    for g in range(4):
        part = nt(dup_ref[g], matrix(weight_ref, g))
        feed = part if feed is None else feed + part
    dfirst = dr2_ref[...] + feed.astype(bf).astype(fl)
    xhat = xhat_ref[...]
    small_ref[0:1] = jnp.sum(dfirst * xhat, axis=0, keepdims=True)
    small_ref[1:2] = jnp.sum(dfirst, axis=0, keepdims=True)
    dxhat = dfirst * vec_ref[0:1]
    dr1 = rstd_ref[:, 0:1] * (
        dxhat
        - jnp.mean(dxhat, axis=-1, keepdims=True)
        - xhat * jnp.mean(dxhat * xhat, axis=-1, keepdims=True)
    )
    dr1_ref[...] = dr1
    small_ref[2:3] = jnp.sum(dr1, axis=0, keepdims=True)
    dattn = dr1.astype(bf)
    for g in range(4):
        dctx_ref[g] = nn(dattn, out_matrix(attn_weight_ref, g)).astype(bf)


def attn_bwd_kernel(where_ref, seg_row_ref, seg_col_ref, proj_ref, lse_ref, dr1_ref, dctx_ref, weight_ref, *refs):
    grad_in_ref, dproj_ref, bias_ref, back_ref = refs[-4:]
    scale = HD ** (-0.5)
    length = dr1_ref.shape[0]
    back_ref[...] = jnp.zeros_like(back_ref)

    def step(g, carry):
        same = seg_col_ref[...] == seg_row_ref[...]
        low = low_lanes((length, LANES))
        none = jnp.zeros((length, LANES), bf)
        parts = [proj_ref[g, :, LANES * k : LANES * (k + 1)] for k in range(6)]
        dctx = [dctx_ref[g, :, :LANES], dctx_ref[g, :, LANES:]]
        turned = [parts[1].T, parts[5].T]
        dq, dk, dv = [], [], []
        for head in range(3):
            query = parts[0] if head < 2 else parts[3]
            keys = parts[1] if head < 2 else parts[5]
            value = parts[2] if head < 2 else parts[3]
            dout = dctx[0] if head < 2 else dctx[1]
            query_in = jnp.where(low, none, query) if head == 1 else jnp.where(low, query, none)
            dout_in = jnp.where(low, dout, none) if head == 0 else jnp.where(low, none, dout)
            scores = jnp.where(same, nt(keys, query_in) * scale, -1e30)
            probs = jnp.exp(scores - lse_ref[g, head])
            dprobs = nt(value, dout_in)
            dv.append(nn(probs.astype(bf), dout))
            row_dot = jnp.sum(probs * dprobs, axis=0, keepdims=True)
            dscores = (probs * (dprobs - row_dot)).astype(bf)
            keys_turned = turned[0][HD:] if head == 1 else turned[head // 2][:HD]
            dq.append(nn(keys_turned, dscores) * scale)
            dk.append(nn(dscores, query) * scale)
        dq.append(jnp.zeros_like(dq[2]))
        dq_near, dq_far = jnp.concatenate(dq[:2]).T, jnp.concatenate(dq[2:]).T
        dproj = jnp.concatenate(
            [
                dq_near.astype(bf),
                jnp.where(low, dk[0], dk[1]).astype(bf),
                jnp.where(low, dv[0], dv[1]).astype(bf),
                jnp.where(low, dq_far, dv[2]).astype(bf),
                none,
                jnp.where(low, dk[2].astype(bf), none),
            ],
            axis=1,
        )
        dproj_ref[g] = dproj
        bias_ref[g] = jnp.sum(dproj.astype(fl), axis=0, keepdims=True)
        back_ref[...] += nt(dproj, matrix(weight_ref, g))
        return carry

    lax.fori_loop(0, 4, step, 0)
    dr1 = dr1_ref[...]
    grad_in_ref[...] = (dr1 + back_ref[...].astype(bf).astype(fl)).astype(bf)


def attn_weights_kernel(where_ref, x_ref, dproj_ref, ctx_ref, dr1_ref, bias_ref, b_up_ref, one_ref, two_ref,
                        near_ref, *refs):
    *far_refs, small_ref, x_turned_ref, dr1_turned_ref = refs

    @pl.when(pl.program_id(0) == 0)
    def _():
        small_ref[...] = jnp.zeros_like(small_ref)
        small_ref[0:2] = one_ref[0:2]
        small_ref[2:4] = two_ref[0:2]
        small_ref[4:5] = one_ref[2:3]
        small_ref[5:6] = two_ref[2:3]
        x_turned_ref[...] = x_ref[...].T
        dr1_turned_ref[...] = dr1_ref[...].astype(bf).T

    small_ref[6:7] = bias_ref[0]
    small_ref[7:8] = b_up_ref[0]
    main = nn(x_turned_ref[...], dproj_ref[0])
    side = nn(dr1_turned_ref[...], ctx_ref[0])
    whole = jnp.concatenate([main[:, :512], main[:, 512:] + side], axis=1).astype(bf)
    scatter_slabs(where_ref, whole, near_ref, far_refs, small_ref[...].astype(bf))


def place_kernel(where_ref, *refs):
    out_ref = refs[-1]
    for d, ref in enumerate(refs[:-1]):
        out_ref[jnp.bitwise_and(where_ref[1] + 4 - d, 3)] = ref[...]


smem = pl.BlockSpec(memory_space=pltpu.SMEM)
vmem = pl.BlockSpec(memory_space=pltpu.VMEM)


def call(kernel, name, outs, where, *args, scratch=(), after=()):
    if after:
        (where,) = late([where], *after)
    return pl.pallas_call(
        kernel,
        name=name,
        out_shape=[jax.ShapeDtypeStruct(s, d) for s, d in outs],
        in_specs=[smem] + [vmem] * len(args),
        out_specs=[vmem] * len(outs),
        scratch_shapes=list(scratch),
        compiler_params=pltpu.CompilerParams(vmem_limit_bytes=VMEM_LIMIT),
        cost_estimate=pl.CostEstimate(flops=COST, bytes_accessed=COST, transcendentals=0),
    )(where, *args)


COST = 1000


def whole_block(shape):
    return pl.BlockSpec(shape, lambda g, where: (0,) * len(shape))


def group_block(shape):
    return pl.BlockSpec((1, *shape[1:]), lambda g, where: (g,) + (0,) * (len(shape) - 1))


def slab_block(shape):
    def index(g, where):
        hop = jnp.bitwise_xor(g, where[1])
        return (0, 2 * jnp.bitwise_and(hop, 1) + jnp.right_shift(hop, 1), 0, 0)

    return pl.BlockSpec((shape[0], 1, *shape[2:]), index)


def call_groups(kernel, name, outs, where, *args, scratch=(), after=()):
    if after:
        (where,) = late([where], *after)
    return pl.pallas_call(
        kernel,
        name=name,
        out_shape=[jax.ShapeDtypeStruct(s, d) for (s, d), _ in outs],
        grid_spec=pltpu.PrefetchScalarGridSpec(
            num_scalar_prefetch=1,
            grid=(4,),
            in_specs=[block(a.shape) for a, block in args],
            out_specs=[block(s) for (s, _), block in outs],
            scratch_shapes=list(scratch),
        ),
        compiler_params=pltpu.CompilerParams(
            vmem_limit_bytes=VMEM_LIMIT, dimension_semantics=("arbitrary",)
        ),
        cost_estimate=pl.CostEstimate(flops=COST, bytes_accessed=COST, transcendentals=0),
    )(where, *[a for a, _ in args])


def flip(value, bits):
    n = lax.axis_size("dp")
    return lax.ppermute(value, "dp", [(k, k ^ bits) for k in range(n)])


def cross(value, bits):
    return lax.ppermute(value, "tensor", [(k, k ^ bits) for k in range(4)])


def rotate(value):
    return lax.ppermute(value, "tensor", [(k, (k + 1) % 4) for k in range(4)])


def late(values, *gates):
    return list(lax.optimization_barrier((*values, *gates))[: len(values)])


def with_core(near):
    return near + [(flip(a, 1), (r + 1, s)) for a, (r, s) in near]


ALL = (0, 1, 2, 3)


def over_tensor(shard):
    return [shard] + [cross(shard, hop) for hop in (1, 2, 3)]


def gather_staged(own, gates=()):
    over_x = flip(own, 2)
    over_y = flip(own, 4)
    half_x, half_y = late([over_x[:2], over_y[2:]], *gates)
    far_a = flip(half_x, 4)
    far_b = flip(half_y, 2)
    near = [(own, (0, ALL)), (over_x, (2, ALL)), (over_y, (4, ALL))]
    return with_core(near + [(far_a, (6, (0, 1))), (far_b, (6, (2, 3)))])


def add(*values):
    total = values[0].astype(fl)
    for value in values[1:]:
        total = total + value.astype(fl)
    return total


def reduce_core(near, far, gates=(), parts=1):
    got = late([flip(part, 1) for part in far], *gates) if gates else [flip(part, 1) for part in far]
    size, each = 4 // len(far), len(far) * parts
    return [
        add(near[a : a + 4 // each], got[a // size][a % size : a % size + 4 // each]).astype(bf)
        for a in range(0, 4, 4 // each)
    ]


def halves(parts):
    return [jnp.concatenate(parts[:2]), jnp.concatenate(parts[2:])]


def reduce_pair(half, axis, gates=()):
    got = flip(half[1], 2 * axis)
    if gates:
        (got,) = late([got], *gates)
    return [add(half[0][k], got[k]).astype(bf) for k in (0, 1)]


def reduce_chip(pair, axis, gates=()):
    got = flip(pair[1], 2 * axis)
    if gates:
        (got,) = late([got], *gates)
    return [add(pair[0][k : k + 2], got[k : k + 2]).astype(bf) for k in (0, 2)]


def reduce_some(sums, gates):
    one, two, three, four = [part[0] for part in sums]
    over_x = flip(jnp.stack([two[:2], four[:2]]), 2)
    over_y = flip(jnp.stack([three[2:], four[2:]]), 4)
    over_x, over_y = late([over_x, over_y], *gates)
    pairs = ((one[:2], over_x[0]), (three[:2], over_x[1]), (one[2:], over_y[0]), (two[2:], over_y[1]))
    return [add(*pair).astype(bf) for pair in pairs]


def reduce_rest(some, gates):
    over_y, over_x = late([flip(some[1], 4), flip(some[3], 2)], *gates)
    return [add(some[0], over_y).astype(bf), add(some[2], over_x).astype(bf)]


def reduce_tensor(plane, gates=()):
    got = cross(plane[1], 1)
    if gates:
        (got,) = late([got], *gates)
    return add(plane[0][0], got[0]), add(plane[0][1], got[1]).astype(bf)


def reduce_last(pair, gates=()):
    got = cross(pair[1], 2)
    if gates:
        (got,) = late([got], *gates)
    return add(pair[0], got)


def gather_plain(shard, extra=None):
    whole = lax.all_gather(lax.all_gather(shard, "dp", axis=0, tiled=True), "tensor", axis=0)
    whole = whole.reshape(4, SLABS, -1, 768)
    if extra is not None:
        extra = lax.all_gather(lax.psum(extra, "dp"), "tensor", axis=0)[:, None].astype(bf)
        extra = jnp.concatenate([extra] + [jnp.zeros_like(extra)] * (SLABS - 1), axis=1)
        whole = jnp.concatenate([whole, extra], axis=2)
    return [(whole[:, r], (r, ALL)) for r in range(SLABS)]


def reduce_plain(near, far, x_last=False):
    order = jnp.array([0, 2, 1, 3])
    grad = jnp.stack([near, jnp.concatenate(far)], axis=1)[:, :, order]
    grad = (grad[order] if x_last else grad).reshape(SLABS, 4, -1, 768).astype(fl)
    whole = grad[:, :, :DEPTH].transpose(1, 0, 2, 3).reshape(4, SLABS * DEPTH, 768)
    part = lax.psum_scatter(whole, "tensor", scatter_dimension=0, tiled=True)
    part = lax.psum_scatter(part[0], "dp", scatter_dimension=0, tiled=True)
    if near.shape[2] == DEPTH:
        return part
    extra = lax.psum_scatter(lax.psum(grad[0, :, DEPTH:], "dp"), "tensor", scatter_dimension=0, tiled=True)[0]
    return jnp.concatenate([part, extra])


def next_row(row, gate):
    (row,) = late([rotate(row)], gate)
    return row


def place_rows(rows, where, after=()):
    return call(place_kernel, "place_rows", [((4,) + rows[0].shape, rows[0].dtype)], where, *rows, after=after)[0]


def moment_update(state, grad):
    moment_one = beta_first * state[1] + (1.0 - beta_first) * grad
    moment_two = beta_second * state[2] + (1.0 - beta_second) * grad * grad
    return jnp.stack([moment_one, moment_two])


def body(
    hidden_in,
    out_grad,
    segment_ids,
    step_count,
    qkv_state,
    qv_bias_state,
    out_state,
    up_state,
    up_bias_state,
    down_state,
    vector_state,
):
    n_dp = lax.axis_size("dp")
    place = lax.axis_index("tensor")
    fast = n_dp == SLABS
    spot = lax.axis_index("dp") if fast else 0
    where = jnp.stack([jnp.int32(spot), (place if fast else 0) * jnp.int32(1)])
    spin = jnp.stack([jnp.int32(0), place * jnp.int32(1)])
    rows, width = qkv_state.shape[1], hidden_in.shape[2]
    cut = 2 * HD

    def spread(value, axis, whole):
        full = jnp.zeros(value.shape[:-1] + (whole,), bf)
        return lax.dynamic_update_slice_in_dim(full, value.astype(bf), axis * value.shape[-1], value.ndim - 1)

    dp = lax.axis_index("dp")
    q, k, v = (qkv_state[0, :, c].astype(bf) for c in range(3))
    o = out_state[0].T.astype(bf)
    attn_shard = jnp.concatenate(
        [q[:, :cut], k[:, :cut], v[:, :cut], q[:, cut:], v[:, cut:], o[:, :cut], k[:, cut:], o[:, cut:]], axis=1
    )
    bq, bv = spread(qv_bias_state[0], dp, HD).reshape(2, 3 * HD)
    gap = jnp.zeros((cut,), bf)
    bias = jnp.concatenate([bq[:cut], gap, bv[:cut], bq[cut:], bv[cut:], gap, gap])
    b_up = spread(up_bias_state[0], dp, LANES).reshape(1, 768)
    extra = jnp.concatenate(
        [spread(vector_state[0], dp, width), bias[None], b_up, jnp.zeros((EXTRA - 8, width), bf)]
    )
    up_shard = up_state[0].astype(bf)
    down_shard = down_state[0].T.astype(bf)

    x = lax.dynamic_index_in_dim(hidden_in, place, 0, keepdims=False)
    dy = lax.dynamic_index_in_dim(out_grad, place, 0, keepdims=False)
    seg = lax.dynamic_index_in_dim(segment_ids, place, 0, keepdims=True)
    seg_col = seg.reshape(-1, 1)
    length = x.shape[0]
    wide = (4, length, 768)
    row_f, row_b = ((length, width), fl), ((length, width), bf)
    whole = ((4, SLABS, DEPTH, 768), bf)
    attn_whole = ((4, SLABS, DEPTH + EXTRA, 768), bf)
    down_outs = [(((n, 4, DEPTH, 768), bf), slab_block) for n in (4, 1, 1, 1, 1)]
    up_outs = [(((n, 4, DEPTH, 768), bf), slab_block) for n in (4, 4)]
    attn_outs = [(((n, 4, DEPTH + EXTRA, 768), bf), slab_block) for n in (4, 1, 1, 1, 1)]
    thin = ((4, 1, 768), fl)

    if fast:
        own = jnp.stack(over_tensor(jnp.concatenate([attn_shard, extra])))
        ffn_slabs = over_tensor(late([jnp.concatenate([up_shard, down_shard])], own)[0])
        attn_pieces = gather_staged(own, ffn_slabs[1:3])
        ffn_own = jnp.stack(late(ffn_slabs, attn_pieces[3][0], attn_pieces[4][0]))
        wait = [ffn_own]
    else:
        attn_pieces = gather_plain(attn_shard, extra)
        ups, downs = gather_plain(up_shard), gather_plain(down_shard)
        ffn_pieces = [(jnp.concatenate([u, d], axis=1), w) for (u, w), (d, _) in zip(ups, downs)]
        wait = []

    def split(pieces):
        return [p for p, _ in pieces], tuple(w for _, w in pieces)

    pieces, plan = split(attn_pieces)
    proj, ctx, lse, attn_w, xhat, rstd, first, vec, b_up = call(
        functools.partial(attn_fwd_kernel, plan), "attn_fwd",
        [(wide, bf), ((4, length, 256), bf), ((4, 3, 1, length), fl), attn_whole, row_f, ((length, LANES), fl), row_b,
         ((8, width), fl), thin],
        where, x, seg, seg_col, *pieces, after=wait,
    )
    if fast:
        ffn_pieces = gather_staged(ffn_own, [vec])
    pieces, plan = split(ffn_pieces)
    out, dr2, act, slope, small_two, up_w, down_w = call(
        functools.partial(ffn_fwd_kernel, plan), "ffn_fwd",
        [row_b, row_f, (wide, bf), (wide, fl), ((3, width), fl), whole, whole],
        where, xhat, first, dy, vec, b_up, *pieces,
    )
    turned = pltpu.VMEM((width, length), bf)
    down_near, *down_far = call_groups(
        down_weights_kernel, "down_weights", down_outs, where, (dr2, whole_block), (act, group_block),
        scratch=[turned],
    )
    dup, b_up_grad = call_groups(
        down_bwd_kernel, "down_bwd", [((wide, bf), group_block), (thin, group_block)],
        where, (dr2, whole_block), (slope, group_block), (down_w, group_block),
    )
    out_one = next_row(out, b_up_grad)
    wait = [out_one]
    if fast:
        down_half = halves(reduce_core(down_near, down_far, [b_up_grad, out_one]))
        wait += down_half
    dr1, dctx, small_one = call(
        up_bwd_kernel, "up_bwd", [row_f, ((4, length, 256), bf), ((3, width), fl)],
        where, dr2, dup, xhat, rstd, vec, up_w, attn_w, after=wait,
    )
    up_near, *up_far = call_groups(
        up_weights_kernel, "up_weights", up_outs, where, (first, whole_block), (dup, group_block),
        scratch=[turned], after=[small_one],
    )
    out_two = next_row(out_one, up_near)
    grad_row, dproj, bias_grad = call(
        attn_bwd_kernel, "attn_bwd", [row_b, (wide, bf), thin],
        where, seg, seg_col, proj, lse, dr1, dctx, attn_w, after=[out_two, up_near],
        scratch=[pltpu.VMEM((length, width), fl)],
    )
    out_three = next_row(out_two, bias_grad)
    wait = [out_three]
    if fast:
        down_pair = reduce_pair(down_half, 1, [bias_grad])
        wait += down_pair
    attn_near, *attn_far = call_groups(
        attn_weights_kernel, "attn_weights", attn_outs,
        where, (x, whole_block), (dproj, group_block), (ctx, group_block), (dr1, whole_block),
        (bias_grad, group_block), (b_up_grad, group_block), (small_one, whole_block), (small_two, whole_block),
        scratch=[pltpu.VMEM((EXTRA, width), fl), turned, turned], after=wait,
    )
    in_one = rotate(grad_row)
    in_two = rotate(in_one)
    in_three = rotate(in_two)
    hidden_out = place_rows([out, out_one, out_two, out_three], spin)
    wait = []
    if fast:
        down_plane = reduce_chip(down_pair, 2, [attn_near])
        attn_far = late(attn_far, *down_plane)
        attn_sums = reduce_core(attn_near, attn_far, [in_one, hidden_out])
        up_half = reduce_core(up_near, late(up_far, in_one, *attn_sums), parts=2)
        attn_some = reduce_some(attn_sums, [in_two, *up_half])
        up_pair = reduce_pair(up_half, 1, attn_some)
        attn_plane = reduce_rest(attn_some, [in_three])
        up_plane = reduce_chip(up_pair, 2, attn_plane)
        down_last = reduce_tensor(down_plane, attn_some)
        attn_last = reduce_tensor(attn_plane, up_pair)
        up_last = reduce_tensor(up_plane)
        down_sum = reduce_last(down_last, [attn_last[1]])
        attn_sum = reduce_last(attn_last, up_last[1:])
        up_sum = reduce_last(up_last)
        wait = attn_plane
    else:
        down_sum = reduce_plain(down_near, down_far, x_last=True)
        up_sum = reduce_plain(up_near, up_far, x_last=True)
        attn_sum = reduce_plain(attn_near, attn_far)

    grad_in = place_rows([grad_row, in_one, in_two, in_three], spin, wait)

    def own_part(value):
        size = value.shape[-1] // n_dp
        return lax.dynamic_slice_in_dim(value, dp * size, size, value.ndim - 1)

    small = attn_sum[rows:]
    gq = jnp.concatenate([small[6, :cut], small[6, 384 : 384 + HD]])
    gv = jnp.concatenate([small[6, 256 : 256 + cut], small[6, 384 + HD : 512]])
    grad_qv = own_part(jnp.stack([gq, gv]).reshape(2, 3, HD))
    grad_b_up = own_part(small[7].reshape(6, LANES))
    grad_vectors = own_part(small[:6])

    gk = [attn_sum[:rows, 128 * n : 128 * (n + 1)] for n in range(6)]
    grad_qkv = jnp.stack(
        [
            jnp.concatenate([gk[0], gk[3][:, :HD]], axis=1),
            jnp.concatenate([gk[1], gk[5][:, :HD]], axis=1),
            jnp.concatenate([gk[2], gk[3][:, HD:]], axis=1),
        ],
        axis=1,
    )
    grad_out = jnp.concatenate([gk[4], gk[5][:, HD:]], axis=1).T
    summed = (grad_qkv, grad_qv, grad_out, up_sum, grad_b_up, down_sum.T, grad_vectors)
    steps_f = step_count[0].astype(fl)
    factor = jnp.minimum(steps_f / warm_steps, (total_steps - steps_f) / (total_steps - warm_steps))
    fix_first = 1.0 - jnp.exp(steps_f * math.log(beta_first))
    fix_second = 1.0 - jnp.exp(steps_f * math.log(beta_second))
    states = (qkv_state, qv_bias_state, out_state, up_state, up_bias_state, down_state, vector_state)
    news = tuple((moment_update(s, g) for s, g in zip(states, summed)))
    plan_out = jnp.stack([factor, fix_first, fix_second])
    return (hidden_out, grad_in, *summed, *news, plan_out)


def solution(mesh):
    return jax.shard_map(
        body,
        mesh=mesh,
        in_specs=(
            P("dp", None, None),
            P("dp", None, None),
            P("dp", None),
            P(),
            P(None, "dp", None, "tensor"),
            P(None, None, "tensor", "dp"),
            P(None, "tensor", "dp"),
            P(None, "dp", "tensor"),
            P(None, "tensor", "dp"),
            P(None, "tensor", "dp"),
            P(None, None, "dp"),
        ),
        out_specs=(
            P("dp", None, None),
            P("dp", None, None),
            P("dp", None, "tensor"),
            P(None, "tensor", "dp"),
            P("tensor", "dp"),
            P("dp", "tensor"),
            P("tensor", "dp"),
            P("tensor", "dp"),
            P(None, "dp"),
            P(None, "dp", None, "tensor"),
            P(None, None, "tensor", "dp"),
            P(None, "tensor", "dp"),
            P(None, "dp", "tensor"),
            P(None, "tensor", "dp"),
            P(None, "tensor", "dp"),
            P(None, None, "dp"),
            P(),
        ),
        check_vma=False,
    )
```

```python
import functools
import math

import jax
import jax.numpy as jnp
from jax import lax
from jax.experimental import pallas as pl
from jax.experimental.pallas import tpu as pltpu
from jax.sharding import PartitionSpec as P

HD = 64
LANES = 128
VMEM_LIMIT = 60 * 1024 * 1024

norm_eps = 1e-05
beta_first = 0.9
beta_second = 0.999
warm_steps = 10000.0
total_steps = 200000.0

bf = jnp.bfloat16
fl = jnp.float32

SLABS = 8
DEPTH = 96
EXTRA = 16


def nt(left, right):
    return lax.dot_general(left, right, (((1,), (1,)), ((), ())), preferred_element_type=fl)


def nn(left, right):
    return lax.dot_general(left, right, (((1,), (0,)), ((), ())), preferred_element_type=fl)


def tn(left, right):
    return lax.dot_general(left, right, (((0,), (0,)), ((), ())), preferred_element_type=fl)


def low_lanes(shape):
    return lax.broadcasted_iota(jnp.int32, shape, 1) < HD


def assemble(where_ref, pieces, plan, *targets):
    for ref, (r, hops) in zip(pieces, plan):
        slab = jnp.bitwise_xor(where_ref[0], r)
        for k, hop in enumerate(hops):
            group = jnp.bitwise_xor(where_ref[1], hop)
            first = 0
            for target in targets:
                last = first + target.shape[2]
                target[group, slab] = ref[k, first:last]
                first = last


def scatter_slabs(where_ref, value, near_ref, far_refs, extra=None, x_last=False):
    chip = jnp.right_shift(where_ref[0], 1)
    core = jnp.bitwise_and(where_ref[0], 1)

    def put(near, far):
        for j in range(SLABS // 2):
            place = jnp.bitwise_xor(chip, j)
            if x_last:
                place = 2 * jnp.bitwise_and(place, 1) + jnp.right_shift(place, 1)

            def store(ref, index, slab):
                ref[index, 0, :DEPTH] = value[DEPTH * slab : DEPTH * (slab + 1)]
                if extra is not None:
                    ref[index, 0, DEPTH:] = extra

            store(near_ref, place, 2 * j + near)
            size = 4 // len(far_refs)
            for k, ref in enumerate(far_refs):
                inside = jnp.logical_and(place >= size * k, place < size * (k + 1))
                index = jnp.clip(place - size * k, 0, size - 1)
                pl.when(inside)(functools.partial(store, ref, index, 2 * j + far))

    pl.when(core == 0)(functools.partial(put, 0, 1))
    pl.when(core == 1)(functools.partial(put, 1, 0))


def matrix(ref, group):
    return ref[group][:, :DEPTH].reshape(SLABS * DEPTH, ref.shape[-1])


def out_matrix(ref, group):
    return ref[group][:, :DEPTH, 512:768].reshape(SLABS * DEPTH, 256)


def attn_fwd_kernel(plan, where_ref, x_ref, seg_row_ref, seg_col_ref, *refs):
    pieces = refs[: len(plan)]
    proj_ref, ctx_ref, lse_ref, weight_ref, xhat_ref, rstd_ref, first_ref, vec_ref, b_up_ref = refs[-9:]
    assemble(where_ref, pieces, plan, weight_ref)
    scale = HD ** (-0.5)
    length = x_ref.shape[0]

    def group_step(g, carry):
        small = jnp.sum(weight_ref[g, :, DEPTH:].astype(fl), axis=0)
        vec_ref[...] = small[:8]
        b_up_ref[g] = small[7:8]
        x = x_ref[...]
        proj = (nn(x, matrix(weight_ref, g)) + small[6:7]).astype(bf)
        proj_ref[g] = proj
        same = seg_col_ref[...] == seg_row_ref[...]
        low = low_lanes((length, LANES))
        none = jnp.zeros((length, LANES), bf)
        parts = [proj[:, LANES * k : LANES * (k + 1)] for k in range(6)]
        turned = [parts[2].T, parts[3].T]
        outs = []
        for head in range(3):
            query = parts[0] if head < 2 else parts[3]
            keys = parts[1] if head < 2 else parts[5]
            value = turned[0][:HD] if head == 0 else turned[head // 2][HD:]
            query = jnp.where(low, none, query) if head == 1 else jnp.where(low, query, none)
            scores = jnp.where(same, nt(keys, query) * scale, -1e30)
            top = jnp.max(scores, axis=0, keepdims=True)
            expd = jnp.exp(scores - top)
            denom = jnp.sum(expd, axis=0, keepdims=True)
            lse_ref[g, head] = top + jnp.log(denom)
            probs = (expd / denom).astype(bf)
            outs.append(nn(value, probs))
        outs.insert(2, jnp.zeros_like(outs[2]))
        ctx_ref[g, :, :LANES] = jnp.concatenate(outs[:2]).T.astype(bf)
        ctx_ref[g, :, LANES:] = jnp.concatenate(outs[2:]).T.astype(bf)
        return carry

    lax.fori_loop(0, 4, group_step, 0)
    total = x_ref[...].astype(fl) + vec_ref[4:5]
    attn = None
    for g in range(4):
        part = nt(ctx_ref[g], out_matrix(weight_ref, g))
        attn = part if attn is None else attn + part
    total = total + attn
    center = total - jnp.mean(total, axis=-1, keepdims=True)
    rstd = lax.rsqrt(jnp.mean(center * center, axis=-1, keepdims=True) + norm_eps)
    xhat = center * rstd
    xhat_ref[...] = xhat
    rstd_ref[...] = jnp.broadcast_to(rstd, rstd_ref.shape)
    first_ref[...] = (xhat * vec_ref[0:1] + vec_ref[1:2]).astype(bf)


def ffn_fwd_kernel(plan, where_ref, xhat_ref, first_ref, dy_ref, vec_ref, b_up_ref, *refs):
    pieces, refs = refs[: len(plan)], refs[len(plan) :]
    out_ref, dr2_ref, act_ref, slope_ref, small_ref, up_w_ref, down_w_ref = refs
    assemble(where_ref, pieces, plan, up_w_ref, down_w_ref)

    def step(g, carry):
        up = nn(first_ref[...], matrix(up_w_ref, g)) + b_up_ref[g]
        half = 0.5 * (1.0 + lax.erf(up * 0.7071067811865476))
        act_ref[g] = (up * half).astype(bf)
        slope_ref[g] = half + up * (jnp.exp(-0.5 * up * up) * 0.3989422804014327)
        return carry

    lax.fori_loop(0, 4, step, 0)
    ffn = None
    for g in range(4):
        part = nt(act_ref[g], matrix(down_w_ref, g))
        ffn = part if ffn is None else ffn + part
    first = xhat_ref[...] * vec_ref[0:1] + vec_ref[1:2]
    total = first + ffn + vec_ref[5:6]
    center = total - jnp.mean(total, axis=-1, keepdims=True)
    rstd = lax.rsqrt(jnp.mean(center * center, axis=-1, keepdims=True) + norm_eps)
    xhat = center * rstd
    out_ref[...] = (xhat * vec_ref[2:3] + vec_ref[3:4]).astype(bf)
    dy = dy_ref[...].astype(fl)
    small_ref[0:1] = jnp.sum(dy * xhat, axis=0, keepdims=True)
    small_ref[1:2] = jnp.sum(dy, axis=0, keepdims=True)
    dxhat = dy * vec_ref[2:3]
    dr2 = rstd * (
        dxhat
        - jnp.mean(dxhat, axis=-1, keepdims=True)
        - xhat * jnp.mean(dxhat * xhat, axis=-1, keepdims=True)
    )
    dr2_ref[...] = dr2
    small_ref[2:3] = jnp.sum(dr2, axis=0, keepdims=True)


def down_weights_kernel(where_ref, dr2_ref, act_ref, near_ref, *refs):
    *far_refs, turned_ref = refs

    @pl.when(pl.program_id(0) == 0)
    def _():
        turned_ref[...] = dr2_ref[...].astype(bf).T

    scatter_slabs(where_ref, nn(turned_ref[...], act_ref[0]).astype(bf), near_ref, far_refs, x_last=True)


def down_bwd_kernel(where_ref, dr2_ref, slope_ref, weight_ref, dup_ref, b_up_ref):
    dup = (nn(dr2_ref[...].astype(bf), matrix(weight_ref, 0)) * slope_ref[0]).astype(bf)
    dup_ref[0] = dup
    b_up_ref[0] = jnp.sum(dup.astype(fl), axis=0, keepdims=True)


def up_weights_kernel(where_ref, first_ref, dup_ref, near_ref, *refs):
    *far_refs, turned_ref = refs

    @pl.when(pl.program_id(0) == 0)
    def _():
        turned_ref[...] = first_ref[...].T

    scatter_slabs(where_ref, nn(turned_ref[...], dup_ref[0]).astype(bf), near_ref, far_refs, x_last=True)


def up_bwd_kernel(where_ref, dr2_ref, dup_ref, xhat_ref, rstd_ref, vec_ref, weight_ref, attn_weight_ref, *refs):
    dr1_ref, dctx_ref, small_ref = refs[-3:]
    feed = None
    for g in range(4):
        part = nt(dup_ref[g], matrix(weight_ref, g))
        feed = part if feed is None else feed + part
    dfirst = dr2_ref[...] + feed.astype(bf).astype(fl)
    xhat = xhat_ref[...]
    small_ref[0:1] = jnp.sum(dfirst * xhat, axis=0, keepdims=True)
    small_ref[1:2] = jnp.sum(dfirst, axis=0, keepdims=True)
    dxhat = dfirst * vec_ref[0:1]
    dr1 = rstd_ref[:, 0:1] * (
        dxhat
        - jnp.mean(dxhat, axis=-1, keepdims=True)
        - xhat * jnp.mean(dxhat * xhat, axis=-1, keepdims=True)
    )
    dr1_ref[...] = dr1
    small_ref[2:3] = jnp.sum(dr1, axis=0, keepdims=True)
    dattn = dr1.astype(bf)
    for g in range(4):
        dctx_ref[g] = nn(dattn, out_matrix(attn_weight_ref, g)).astype(bf)


def attn_bwd_kernel(where_ref, seg_row_ref, seg_col_ref, proj_ref, lse_ref, dr1_ref, dctx_ref, weight_ref, *refs):
    grad_in_ref, dproj_ref, bias_ref, back_ref = refs[-4:]
    scale = HD ** (-0.5)
    length = dr1_ref.shape[0]
    back_ref[...] = jnp.zeros_like(back_ref)

    def step(g, carry):
        same = seg_col_ref[...] == seg_row_ref[...]
        low = low_lanes((length, LANES))
        none = jnp.zeros((length, LANES), bf)
        parts = [proj_ref[g, :, LANES * k : LANES * (k + 1)] for k in range(6)]
        dctx = [dctx_ref[g, :, :LANES], dctx_ref[g, :, LANES:]]
        turned = [parts[1].T, parts[5].T]
        dq, dk, dv = [], [], []
        for head in range(3):
            query = parts[0] if head < 2 else parts[3]
            keys = parts[1] if head < 2 else parts[5]
            value = parts[2] if head < 2 else parts[3]
            dout = dctx[0] if head < 2 else dctx[1]
            query_in = jnp.where(low, none, query) if head == 1 else jnp.where(low, query, none)
            dout_in = jnp.where(low, dout, none) if head == 0 else jnp.where(low, none, dout)
            scores = jnp.where(same, nt(keys, query_in) * scale, -1e30)
            probs = jnp.exp(scores - lse_ref[g, head])
            dprobs = nt(value, dout_in)
            dv.append(nn(probs.astype(bf), dout))
            row_dot = jnp.sum(probs * dprobs, axis=0, keepdims=True)
            dscores = (probs * (dprobs - row_dot)).astype(bf)
            keys_turned = turned[0][HD:] if head == 1 else turned[head // 2][:HD]
            dq.append(nn(keys_turned, dscores) * scale)
            dk.append(nn(dscores, query) * scale)
        dq.append(jnp.zeros_like(dq[2]))
        dq_near, dq_far = jnp.concatenate(dq[:2]).T, jnp.concatenate(dq[2:]).T
        dproj = jnp.concatenate(
            [
                dq_near.astype(bf),
                jnp.where(low, dk[0], dk[1]).astype(bf),
                jnp.where(low, dv[0], dv[1]).astype(bf),
                jnp.where(low, dq_far, dv[2]).astype(bf),
                none,
                jnp.where(low, dk[2].astype(bf), none),
            ],
            axis=1,
        )
        dproj_ref[g] = dproj
        bias_ref[g] = jnp.sum(dproj.astype(fl), axis=0, keepdims=True)
        back_ref[...] += nt(dproj, matrix(weight_ref, g))
        return carry

    lax.fori_loop(0, 4, step, 0)
    dr1 = dr1_ref[...]
    grad_in_ref[...] = (dr1 + back_ref[...].astype(bf).astype(fl)).astype(bf)


def attn_weights_kernel(where_ref, x_ref, dproj_ref, ctx_ref, dr1_ref, bias_ref, b_up_ref, one_ref, two_ref,
                        near_ref, *refs):
    *far_refs, small_ref, x_turned_ref, dr1_turned_ref = refs

    @pl.when(pl.program_id(0) == 0)
    def _():
        small_ref[...] = jnp.zeros_like(small_ref)
        small_ref[0:2] = one_ref[0:2]
        small_ref[2:4] = two_ref[0:2]
        small_ref[4:5] = one_ref[2:3]
        small_ref[5:6] = two_ref[2:3]
        x_turned_ref[...] = x_ref[...].T
        dr1_turned_ref[...] = dr1_ref[...].astype(bf).T

    small_ref[6:7] = bias_ref[0]
    small_ref[7:8] = b_up_ref[0]
    main = nn(x_turned_ref[...], dproj_ref[0])
    side = nn(dr1_turned_ref[...], ctx_ref[0])
    whole = jnp.concatenate([main[:, :512], main[:, 512:] + side], axis=1).astype(bf)
    scatter_slabs(where_ref, whole, near_ref, far_refs, small_ref[...].astype(bf))


def place_kernel(where_ref, *refs):
    out_ref = refs[-1]
    for d, ref in enumerate(refs[:-1]):
        out_ref[jnp.bitwise_and(where_ref[1] + 4 - d, 3)] = ref[...]


smem = pl.BlockSpec(memory_space=pltpu.SMEM)
vmem = pl.BlockSpec(memory_space=pltpu.VMEM)


def call(kernel, name, outs, where, *args, scratch=(), after=()):
    if after:
        (where,) = late([where], *after)
    return pl.pallas_call(
        kernel,
        name=name,
        out_shape=[jax.ShapeDtypeStruct(s, d) for s, d in outs],
        in_specs=[smem] + [vmem] * len(args),
        out_specs=[vmem] * len(outs),
        scratch_shapes=list(scratch),
        compiler_params=pltpu.CompilerParams(vmem_limit_bytes=VMEM_LIMIT),
        cost_estimate=pl.CostEstimate(flops=COST, bytes_accessed=COST, transcendentals=0),
    )(where, *args)


COST = 1000


def whole_block(shape):
    return pl.BlockSpec(shape, lambda g, where: (0,) * len(shape))


def group_block(shape):
    return pl.BlockSpec((1, *shape[1:]), lambda g, where: (g,) + (0,) * (len(shape) - 1))


def slab_block(shape):
    def index(g, where):
        hop = jnp.bitwise_xor(g, where[1])
        return (0, 2 * jnp.bitwise_and(hop, 1) + jnp.right_shift(hop, 1), 0, 0)

    return pl.BlockSpec((shape[0], 1, *shape[2:]), index)


def call_groups(kernel, name, outs, where, *args, scratch=(), after=()):
    if after:
        (where,) = late([where], *after)
    return pl.pallas_call(
        kernel,
        name=name,
        out_shape=[jax.ShapeDtypeStruct(s, d) for (s, d), _ in outs],
        grid_spec=pltpu.PrefetchScalarGridSpec(
            num_scalar_prefetch=1,
            grid=(4,),
            in_specs=[block(a.shape) for a, block in args],
            out_specs=[block(s) for (s, _), block in outs],
            scratch_shapes=list(scratch),
        ),
        compiler_params=pltpu.CompilerParams(
            vmem_limit_bytes=VMEM_LIMIT, dimension_semantics=("arbitrary",)
        ),
        cost_estimate=pl.CostEstimate(flops=COST, bytes_accessed=COST, transcendentals=0),
    )(where, *[a for a, _ in args])


def flip(value, bits):
    n = lax.axis_size("dp")
    return lax.ppermute(value, "dp", [(k, k ^ bits) for k in range(n)])


def cross(value, bits):
    return lax.ppermute(value, "tensor", [(k, k ^ bits) for k in range(4)])


def rotate(value):
    return lax.ppermute(value, "tensor", [(k, (k + 1) % 4) for k in range(4)])


def late(values, *gates):
    return list(lax.optimization_barrier((*values, *gates))[: len(values)])


def with_core(near):
    return near + [(flip(a, 1), (r + 1, s)) for a, (r, s) in near]


ALL = (0, 1, 2, 3)


def over_tensor(shard):
    return [shard] + [cross(shard, hop) for hop in (1, 2, 3)]


def gather_staged(own, gates=()):
    over_x = flip(own, 2)
    over_y = flip(own, 4)
    half_x, half_y = late([over_x[:2], over_y[2:]], *gates)
    far_a = flip(half_x, 4)
    far_b = flip(half_y, 2)
    near = [(own, (0, ALL)), (over_x, (2, ALL)), (over_y, (4, ALL))]
    return with_core(near + [(far_a, (6, (0, 1))), (far_b, (6, (2, 3)))])


def add(*values):
    total = values[0].astype(fl)
    for value in values[1:]:
        total = total + value.astype(fl)
    return total


def reduce_core(near, far, gates=(), parts=1):
    got = late([flip(part, 1) for part in far], *gates) if gates else [flip(part, 1) for part in far]
    size, each = 4 // len(far), len(far) * parts
    return [
        add(near[a : a + 4 // each], got[a // size][a % size : a % size + 4 // each]).astype(bf)
        for a in range(0, 4, 4 // each)
    ]


def halves(parts):
    return [jnp.concatenate(parts[:2]), jnp.concatenate(parts[2:])]


def reduce_pair(half, axis, gates=()):
    got = flip(half[1], 2 * axis)
    if gates:
        (got,) = late([got], *gates)
    return [add(half[0][k], got[k]).astype(bf) for k in (0, 1)]


def reduce_chip(pair, axis, gates=()):
    got = flip(pair[1], 2 * axis)
    if gates:
        (got,) = late([got], *gates)
    return [add(pair[0][k : k + 2], got[k : k + 2]).astype(bf) for k in (0, 2)]


def reduce_some(sums, gates):
    one, two, three, four = [part[0] for part in sums]
    over_x = flip(jnp.stack([two[:2], four[:2]]), 2)
    over_y = flip(jnp.stack([three[2:], four[2:]]), 4)
    over_x, over_y = late([over_x, over_y], *gates)
    pairs = ((one[:2], over_x[0]), (three[:2], over_x[1]), (one[2:], over_y[0]), (two[2:], over_y[1]))
    return [add(*pair).astype(bf) for pair in pairs]


def reduce_rest(some, gates):
    over_y, over_x = late([flip(some[1], 4), flip(some[3], 2)], *gates)
    return [add(some[0], over_y).astype(bf), add(some[2], over_x).astype(bf)]


def reduce_tensor(plane, gates=()):
    got = cross(plane[1], 1)
    if gates:
        (got,) = late([got], *gates)
    return add(plane[0][0], got[0]), add(plane[0][1], got[1]).astype(bf)


def reduce_last(pair, gates=()):
    got = cross(pair[1], 2)
    if gates:
        (got,) = late([got], *gates)
    return add(pair[0], got)


def gather_plain(shard, extra=None):
    whole = lax.all_gather(lax.all_gather(shard, "dp", axis=0, tiled=True), "tensor", axis=0)
    whole = whole.reshape(4, SLABS, -1, 768)
    if extra is not None:
        extra = lax.all_gather(lax.psum(extra, "dp"), "tensor", axis=0)[:, None].astype(bf)
        extra = jnp.concatenate([extra] + [jnp.zeros_like(extra)] * (SLABS - 1), axis=1)
        whole = jnp.concatenate([whole, extra], axis=2)
    return [(whole[:, r], (r, ALL)) for r in range(SLABS)]


def reduce_plain(near, far, x_last=False):
    order = jnp.array([0, 2, 1, 3])
    grad = jnp.stack([near, jnp.concatenate(far)], axis=1)[:, :, order]
    grad = (grad[order] if x_last else grad).reshape(SLABS, 4, -1, 768).astype(fl)
    whole = grad[:, :, :DEPTH].transpose(1, 0, 2, 3).reshape(4, SLABS * DEPTH, 768)
    part = lax.psum_scatter(whole, "tensor", scatter_dimension=0, tiled=True)
    part = lax.psum_scatter(part[0], "dp", scatter_dimension=0, tiled=True)
    if near.shape[2] == DEPTH:
        return part
    extra = lax.psum_scatter(lax.psum(grad[0, :, DEPTH:], "dp"), "tensor", scatter_dimension=0, tiled=True)[0]
    return jnp.concatenate([part, extra])


def next_row(row, gate):
    (row,) = late([rotate(row)], gate)
    return row


def place_rows(rows, where, after=()):
    return call(place_kernel, "place_rows", [((4,) + rows[0].shape, rows[0].dtype)], where, *rows, after=after)[0]


def moment_update(state, grad):
    moment_one = beta_first * state[1] + (1.0 - beta_first) * grad
    moment_two = beta_second * state[2] + (1.0 - beta_second) * grad * grad
    return jnp.stack([moment_one, moment_two])


def body(
    hidden_in,
    out_grad,
    segment_ids,
    step_count,
    qkv_state,
    qv_bias_state,
    out_state,
    up_state,
    up_bias_state,
    down_state,
    vector_state,
):
    n_dp = lax.axis_size("dp")
    place = lax.axis_index("tensor")
    fast = n_dp == SLABS
    spot = lax.axis_index("dp") if fast else 0
    where = jnp.stack([jnp.int32(spot), (place if fast else 0) * jnp.int32(1)])
    spin = jnp.stack([jnp.int32(0), place * jnp.int32(1)])
    rows, width = qkv_state.shape[1], hidden_in.shape[2]
    cut = 2 * HD

    def spread(value, axis, whole):
        full = jnp.zeros(value.shape[:-1] + (whole,), bf)
        return lax.dynamic_update_slice_in_dim(full, value.astype(bf), axis * value.shape[-1], value.ndim - 1)

    dp = lax.axis_index("dp")
    q, k, v = (qkv_state[0, :, c].astype(bf) for c in range(3))
    o = out_state[0].T.astype(bf)
    attn_shard = jnp.concatenate(
        [q[:, :cut], k[:, :cut], v[:, :cut], q[:, cut:], v[:, cut:], o[:, :cut], k[:, cut:], o[:, cut:]], axis=1
    )
    bq, bv = spread(qv_bias_state[0], dp, HD).reshape(2, 3 * HD)
    gap = jnp.zeros((cut,), bf)
    bias = jnp.concatenate([bq[:cut], gap, bv[:cut], bq[cut:], bv[cut:], gap, gap])
    b_up = spread(up_bias_state[0], dp, LANES).reshape(1, 768)
    extra = jnp.concatenate(
        [spread(vector_state[0], dp, width), bias[None], b_up, jnp.zeros((EXTRA - 8, width), bf)]
    )
    up_shard = up_state[0].astype(bf)
    down_shard = down_state[0].T.astype(bf)

    x = lax.dynamic_index_in_dim(hidden_in, place, 0, keepdims=False)
    dy = lax.dynamic_index_in_dim(out_grad, place, 0, keepdims=False)
    seg = lax.dynamic_index_in_dim(segment_ids, place, 0, keepdims=True)
    seg_col = seg.reshape(-1, 1)
    length = x.shape[0]
    wide = (4, length, 768)
    row_f, row_b = ((length, width), fl), ((length, width), bf)
    whole = ((4, SLABS, DEPTH, 768), bf)
    attn_whole = ((4, SLABS, DEPTH + EXTRA, 768), bf)
    down_outs = [(((n, 4, DEPTH, 768), bf), slab_block) for n in (4, 1, 1, 1, 1)]
    up_outs = [(((n, 4, DEPTH, 768), bf), slab_block) for n in (4, 4)]
    attn_outs = [(((n, 4, DEPTH + EXTRA, 768), bf), slab_block) for n in (4, 1, 1, 1, 1)]
    thin = ((4, 1, 768), fl)

    if fast:
        own = jnp.stack(over_tensor(jnp.concatenate([attn_shard, extra])))
        ffn_slabs = over_tensor(late([jnp.concatenate([up_shard, down_shard])], own)[0])
        attn_pieces = gather_staged(own, ffn_slabs[1:3])
        ffn_own = jnp.stack(late(ffn_slabs, attn_pieces[3][0], attn_pieces[4][0]))
        wait = [ffn_own]
    else:
        attn_pieces = gather_plain(attn_shard, extra)
        ups, downs = gather_plain(up_shard), gather_plain(down_shard)
        ffn_pieces = [(jnp.concatenate([u, d], axis=1), w) for (u, w), (d, _) in zip(ups, downs)]
        wait = []

    def split(pieces):
        return [p for p, _ in pieces], tuple(w for _, w in pieces)

    pieces, plan = split(attn_pieces)
    proj, ctx, lse, attn_w, xhat, rstd, first, vec, b_up = call(
        functools.partial(attn_fwd_kernel, plan), "attn_fwd",
        [(wide, bf), ((4, length, 256), bf), ((4, 3, 1, length), fl), attn_whole, row_f, ((length, LANES), fl), row_b,
         ((8, width), fl), thin],
        where, x, seg, seg_col, *pieces, after=wait,
    )
    if fast:
        ffn_pieces = gather_staged(ffn_own, [vec])
    pieces, plan = split(ffn_pieces)
    out, dr2, act, slope, small_two, up_w, down_w = call(
        functools.partial(ffn_fwd_kernel, plan), "ffn_fwd",
        [row_b, row_f, (wide, bf), (wide, fl), ((3, width), fl), whole, whole],
        where, xhat, first, dy, vec, b_up, *pieces,
    )
    turned = pltpu.VMEM((width, length), bf)
    down_near, *down_far = call_groups(
        down_weights_kernel, "down_weights", down_outs, where, (dr2, whole_block), (act, group_block),
        scratch=[turned],
    )
    dup, b_up_grad = call_groups(
        down_bwd_kernel, "down_bwd", [((wide, bf), group_block), (thin, group_block)],
        where, (dr2, whole_block), (slope, group_block), (down_w, group_block),
    )
    out_one = next_row(out, b_up_grad)
    wait = [out_one]
    if fast:
        down_half = halves(reduce_core(down_near, down_far, [b_up_grad, out_one]))
        wait += down_half
    dr1, dctx, small_one = call(
        up_bwd_kernel, "up_bwd", [row_f, ((4, length, 256), bf), ((3, width), fl)],
        where, dr2, dup, xhat, rstd, vec, up_w, attn_w, after=wait,
    )
    out_two = next_row(out_one, small_one)
    grad_row, dproj, bias_grad = call(
        attn_bwd_kernel, "attn_bwd", [row_b, (wide, bf), thin],
        where, seg, seg_col, proj, lse, dr1, dctx, attn_w, after=[out_two],
        scratch=[pltpu.VMEM((length, width), fl)],
    )
    out_three = next_row(out_two, bias_grad)
    wait = [out_three]
    if fast:
        down_pair = reduce_pair(down_half, 1, [bias_grad])
        wait += down_pair
    attn_near, *attn_far = call_groups(
        attn_weights_kernel, "attn_weights", attn_outs,
        where, (x, whole_block), (dproj, group_block), (ctx, group_block), (dr1, whole_block),
        (bias_grad, group_block), (b_up_grad, group_block), (small_one, whole_block), (small_two, whole_block),
        scratch=[pltpu.VMEM((EXTRA, width), fl), turned, turned], after=wait,
    )
    up_near, *up_far = call_groups(
        up_weights_kernel, "up_weights", up_outs, where, (first, whole_block), (dup, group_block),
        scratch=[turned], after=[bias_grad, attn_near],
    )
    in_one = rotate(grad_row)
    in_two = rotate(in_one)
    in_three = rotate(in_two)
    hidden_out = place_rows([out, out_one, out_two, out_three], spin)
    wait = []
    if fast:
        down_plane = reduce_chip(down_pair, 2)
        attn_far = late(attn_far, *down_plane)
        attn_sums = reduce_core(attn_near, attn_far, [up_near, in_one])
        up_far = late(up_far, in_one, *attn_sums)
        up_pair = reduce_pair(reduce_core(up_near, up_far, parts=2), 1, [in_two])
        up_plane = reduce_chip(up_pair, 2)
        attn_some = reduce_some(attn_sums, [in_two])
        attn_plane = reduce_rest(attn_some, [in_three, *up_pair])
        down_last = reduce_tensor(down_plane, [*up_pair, *attn_some])
        attn_last = reduce_tensor([attn_plane[0]] + late(attn_plane[1:], *up_plane))
        up_last = reduce_tensor(up_plane)
        down_sum = reduce_last(down_last, [attn_last[1], up_last[1]])
        attn_sum = reduce_last(attn_last)
        up_sum = reduce_last(up_last)
        wait = up_plane + attn_plane
    else:
        down_sum = reduce_plain(down_near, down_far, x_last=True)
        up_sum = reduce_plain(up_near, up_far, x_last=True)
        attn_sum = reduce_plain(attn_near, attn_far)

    grad_in = place_rows([grad_row, in_one, in_two, in_three], spin, wait)

    def own_part(value):
        size = value.shape[-1] // n_dp
        return lax.dynamic_slice_in_dim(value, dp * size, size, value.ndim - 1)

    small = attn_sum[rows:]
    gq = jnp.concatenate([small[6, :cut], small[6, 384 : 384 + HD]])
    gv = jnp.concatenate([small[6, 256 : 256 + cut], small[6, 384 + HD : 512]])
    grad_qv = own_part(jnp.stack([gq, gv]).reshape(2, 3, HD))
    grad_b_up = own_part(small[7].reshape(6, LANES))
    grad_vectors = own_part(small[:6])

    gk = [attn_sum[:rows, 128 * n : 128 * (n + 1)] for n in range(6)]
    grad_qkv = jnp.stack(
        [
            jnp.concatenate([gk[0], gk[3][:, :HD]], axis=1),
            jnp.concatenate([gk[1], gk[5][:, :HD]], axis=1),
            jnp.concatenate([gk[2], gk[3][:, HD:]], axis=1),
        ],
        axis=1,
    )
    grad_out = jnp.concatenate([gk[4], gk[5][:, HD:]], axis=1).T
    summed = (grad_qkv, grad_qv, grad_out, up_sum, grad_b_up, down_sum.T, grad_vectors)
    steps_f = step_count[0].astype(fl)
    factor = jnp.minimum(steps_f / warm_steps, (total_steps - steps_f) / (total_steps - warm_steps))
    fix_first = 1.0 - jnp.exp(steps_f * math.log(beta_first))
    fix_second = 1.0 - jnp.exp(steps_f * math.log(beta_second))
    states = (qkv_state, qv_bias_state, out_state, up_state, up_bias_state, down_state, vector_state)
    news = tuple((moment_update(s, g) for s, g in zip(states, summed)))
    plan_out = jnp.stack([factor, fix_first, fix_second])
    return (hidden_out, grad_in, *summed, *news, plan_out)


def solution(mesh):
    return jax.shard_map(
        body,
        mesh=mesh,
        in_specs=(
            P("dp", None, None),
            P("dp", None, None),
            P("dp", None),
            P(),
            P(None, "dp", None, "tensor"),
            P(None, None, "tensor", "dp"),
            P(None, "tensor", "dp"),
            P(None, "dp", "tensor"),
            P(None, "tensor", "dp"),
            P(None, "tensor", "dp"),
            P(None, None, "dp"),
        ),
        out_specs=(
            P("dp", None, None),
            P("dp", None, None),
            P("dp", None, "tensor"),
            P(None, "tensor", "dp"),
            P("tensor", "dp"),
            P("dp", "tensor"),
            P("tensor", "dp"),
            P("tensor", "dp"),
            P(None, "dp"),
            P(None, "dp", None, "tensor"),
            P(None, None, "tensor", "dp"),
            P(None, "tensor", "dp"),
            P(None, "dp", "tensor"),
            P(None, "tensor", "dp"),
            P(None, "tensor", "dp"),
            P(None, None, "dp"),
            P(),
        ),
        check_vma=False,
    )
```
